128 devices in a mesh: lat: 4 (over x_hi, core), lon: 32 (over z, y, x_lo).
Axes of the slice: x: 4 (x_hi: 2, x_lo: 2; x = x_hi * 2 + x_lo), y: 4, z: 4, core: 2. Of those that a mesh axis runs over, the one named last changes fastest.
Arguments:
- background: bfloat16 [512, 4096, 128], P('lat', 'lon'), may hold values from -6 to 6
- obs_values: bfloat16 [128, 128, 96, 128], P(('lat', 'lon')), may hold values from -6 to 6
- obs_cells: int32 [128, 128, 96], P(('lat', 'lon')), may hold values from 0 to 16383
- obs_counts: int32 [128, 128], P(('lat', 'lon')), may hold values from 0 to 96, as said below
- conv1_weight: bfloat16 [3, 3, 128, 128], replicated, may hold values from -0.1875 to 0.1875
- conv1_bias: float32 [128], replicated, may hold values from -3 to 3
- conv2_weight: bfloat16 [3, 3, 128, 128], replicated, may hold values from -0.1875 to 0.1875
- conv2_bias: float32 [128], replicated, may hold values from -3 to 3
Outputs:
- coarse: bfloat16 [256, 2048, 128], P('lat', 'lon')
The draws below stay inside these ranges and needn't reach their ends.
Inputs may be any that keep to these rules, and one draw needn't show every extreme that they name: `obs_counts`: every draw has an owner that receives 96 live slots from every device.
All inputs are finite; a program needn't handle non-finite values.
Results may differ from the reference program's by a relative error of at most 0.0051.
Values may be sent and summed in bfloat16 or wider, within the bound.
No kernel may reach another device: no remote copies, remote signals or barrier semaphores. Data moves between devices by JAX's collectives and lax.ppermute only.
A program may use at most 128 MiB of HBM per device.

```python
import jax
import jax.numpy as jnp
from jax import lax

C = 128
HL = 128
WL = 128
CAP = 96
NLAT = 512
NLON = 4096
N_LON = 32
DEVICES = 128


def draw_obs_counts(key, part):
    key_heat, key_base, key_hot = jax.random.split(jax.random.fold_in(key, 17), 3)
    heat = jax.random.randint(key_heat, (DEVICES,), 1, 5)
    base = jax.random.randint(key_base, (DEVICES, DEVICES), 0, CAP // 2 + 1)
    counts = jnp.minimum(CAP, base * heat[None, :] // 2)
    hot = jax.random.randint(key_hot, (), 0, DEVICES)
    counts = jnp.where(jnp.arange(DEVICES)[None, :] == hot, CAP, counts)
    return counts.astype(jnp.int32)


def with_ends(result, own_key, low, top_value):
    longest = result.shape.index(max(result.shape))
    spots = []
    for shift in (0, 1):
        where = [jax.random.randint(jax.random.fold_in(own_key, axis), (), 0, length) for axis, length in enumerate(result.shape)]
        where[longest] = (where[longest] + shift) % result.shape[longest]
        spots.append(tuple(where))
    return result.at[spots[0]].set(low).at[spots[1]].set(top_value)


def block_levels(key, dims, pieces, smallest, top_value):
    level = 1.0
    for axis_at, shards_of in pieces:
        draws = jax.random.uniform(jax.random.fold_in(jax.random.fold_in(key, 6), axis_at), (shards_of,), jnp.float32, smallest / len(pieces), top_value / len(pieces))
        level = level * jnp.repeat(jnp.exp(draws), dims[axis_at] // shards_of).reshape((-1,) + (1,) * (len(dims) - 1 - axis_at))
    return level


def centred(rng, extent, spread, limit, cuts=(), held_as=jnp.bfloat16):
    factor_of = block_levels(rng, extent, cuts, -0.22, 0.18) if cuts else 1.0
    entries = jax.random.normal(rng, extent, jnp.float32) * spread * factor_of
    return jnp.minimum(jnp.maximum(entries, -limit), limit).astype(held_as)


def setup_inputs(seed: int = 0) -> dict:
    arg_keys = jax.random.split(jax.random.key(seed), 9)
    return {
        "background": centred(arg_keys[0], (NLAT, NLON, C), 1.0, 6.0, ((0, 4), (1, 32))),
        "obs_values": centred(arg_keys[1], (DEVICES, DEVICES, CAP, C), 1.0, 6.0, ((0, 128),)),
        "obs_cells": with_ends(jax.random.randint(arg_keys[2], (DEVICES, DEVICES, CAP), 0, HL * WL), jax.random.fold_in(arg_keys[2], 1), 0, (HL * WL) - 1).astype(jnp.int32),
        "obs_counts": draw_obs_counts(jax.random.fold_in(arg_keys[8], 71), 0),
        "conv1_weight": centred(arg_keys[4], (3, 3, C, C), (9 * C) ** -0.5, 0.1875),
        "conv1_bias": centred(arg_keys[5], (C,), 0.5, 3.0, (), jnp.float32),
        "conv2_weight": centred(arg_keys[6], (3, 3, C, C), (9 * C) ** -0.5, 0.1875),
        "conv2_bias": centred(arg_keys[7], (C,), 0.5, 3.0, (), jnp.float32),
    }


def extend(field):
    half = field.shape[1] // 2
    top = jnp.roll(field[0], half, axis=0)
    bottom = jnp.roll(field[-1], half, axis=0)
    tall = jnp.concatenate([top[None], field, bottom[None]], axis=0)
    return jnp.concatenate([tall[:, -1:], tall, tall[:, :1]], axis=1)


def convolve(padded, weight, stride):
    rows = (padded.shape[0] - 2) // stride
    cols = (padded.shape[1] - 2) // stride
    chans = padded.shape[2]
    total = jnp.zeros((rows * cols, weight.shape[3]), jnp.float32)
    for di in range(3):
        for dj in range(3):
            part = padded[di:di + rows * stride:stride, dj:dj + cols * stride:stride]
            total = total + jnp.dot(part.reshape(rows * cols, chans), weight[di, dj], preferred_element_type=jnp.float32)
    return total.reshape(rows, cols, weight.shape[3])


def reference(background, obs_values, obs_cells, obs_counts, conv1_weight, conv1_bias, conv2_weight, conv2_bias):
    chans = background.shape[2]
    owners = jnp.arange(DEVICES).astype(jnp.int32)
    band = owners // N_LON
    sector = owners % N_LON
    slots = jnp.arange(CAP).astype(jnp.int32)

    def add_source(total, item):
        values, cells, counts = item
        live = slots[None, :] < counts[:, None]
        row_index = band[:, None] * HL + cells // WL
        col_index = sector[:, None] * WL + cells % WL
        flat = (row_index * NLON + col_index).astype(jnp.int32)
        terms = jnp.where(live[:, :, None], values.astype(jnp.float32), jnp.float32(0.0))
        total = total.at[flat.reshape(-1)].add(terms.reshape(-1, chans))
        return total, None

    increment, _ = lax.scan(add_source, jnp.zeros((NLAT * NLON, chans), jnp.float32), (obs_values, obs_cells, obs_counts))
    analysis = (background.astype(jnp.float32) + increment.reshape(NLAT, NLON, chans)).astype(jnp.bfloat16)
    hidden = jax.nn.gelu(convolve(extend(analysis), conv1_weight, 1) + conv1_bias).astype(jnp.bfloat16)
    coarse = convolve(extend(hidden), conv2_weight, 2) + conv2_bias
    return coarse.astype(jnp.bfloat16)
```

```python
import functools

import jax
import jax.numpy as jnp
from jax import lax
from jax.experimental import pallas as pl
from jax.experimental.pallas import tpu as pltpu
from jax.sharding import PartitionSpec as P

PITCH, ODD, EVEN = 152, 8, 80
SLABS = 138
NACC = 4
META = 8
GELU_A, GELU_B = 0.7978845608028654, 0.044715
VMEM = pl.BlockSpec(memory_space=pltpu.VMEM)
SMEM = pl.BlockSpec(memory_space=pltpu.SMEM)
ANY = pl.BlockSpec(memory_space=pl.ANY)


def on_chip(x):
    return pltpu.with_memory_space_constraint(x, pltpu.VMEM)


def gelu(x):
    return 0.5 * x * (1.0 + jnp.tanh(GELU_A * (x + GELU_B * (x * x * x))))


def pack_kernel(values_ref, cells_ref, counts_ref, out_ref, meta_ref, sem):
    slots = values_ref.shape[1]
    body = pltpu.make_async_copy(values_ref, out_ref.at[:, pl.ds(0, slots), :], sem.at[0])
    body.start()
    cells = cells_ref[...]
    live = lax.broadcasted_iota(jnp.int32, cells.shape, 1) < counts_ref[...]
    row = cells >> 7
    col = cells & 127
    high = jnp.where(live, row + 2, 0).astype(jnp.float32)
    low = jnp.where(live, (col >> 1) + jnp.where((col & 1) == 1, ODD, EVEN), 0).astype(jnp.float32)
    both = jnp.concatenate(
        [high[:, None, :], low[:, None, :], jnp.zeros((cells.shape[0], META - 2, 128), jnp.float32)], axis=1
    )
    meta_ref[...] = both.astype(jnp.bfloat16)
    tail = pltpu.make_async_copy(meta_ref, out_ref.at[:, pl.ds(slots, META), :], sem.at[1])
    tail.start()
    body.wait()
    tail.wait()


def pack(values, cells, counts):
    owners, slots, chans = values.shape
    return pl.pallas_call(
        pack_kernel,
        out_shape=jax.ShapeDtypeStruct((owners, slots + META, chans), jnp.bfloat16),
        in_specs=[ANY, VMEM, VMEM],
        out_specs=ANY,
        scratch_shapes=[
            pltpu.VMEM((owners, META, chans), jnp.bfloat16),
            pltpu.SemaphoreType.DMA((2,)),
        ],
        compiler_params=pltpu.CompilerParams(vmem_limit_bytes=8 << 20),
        name="pack",
    )(values, jnp.pad(cells, ((0, 0), (0, 128 - slots))), counts)


def spread_kernel(field_ref, acc_ref, wide_ref):
    def step(r, carry):
        wide_ref[...] = field_ref[r].astype(jnp.float32)
        base = pl.multiple_of((r + 2) * PITCH, 8)
        acc_ref[pl.ds(base + ODD, 64), :] = wide_ref[pl.ds(1, 64, stride=2), :]
        acc_ref[pl.ds(base + EVEN, 64), :] = wide_ref[pl.ds(0, 64, stride=2), :]
        return carry

    lax.fori_loop(0, field_ref.shape[0], step, 0)


def spread(field):
    return pl.pallas_call(
        spread_kernel,
        out_shape=pltpu.VMEM((SLABS * PITCH, 128), jnp.float32),
        in_specs=[VMEM],
        out_specs=VMEM,
        scratch_shapes=[pltpu.VMEM((128, 128), jnp.float32)],
        compiler_params=pltpu.CompilerParams(vmem_limit_bytes=12 << 20),
        name="spread",
    )(field)


def scatter_kernel(got_ref, start_ref, acc_ref, right_ref, left_ref, rows_ref, *rest):
    more = rest[: NACC - 1]
    wide_ref, meta_ref, index_ref, place_ref, sem = rest[NACC - 1 :]
    del start_ref
    sources, slots = got_ref.shape[0], got_ref.shape[1] - META

    def unpack(s, carry):
        meta_ref[pl.ds(pl.multiple_of(s * META, META), META), :] = got_ref[s, pl.ds(slots, META), :].astype(jnp.float32)
        return carry

    lax.fori_loop(0, sources, unpack, 0, unroll=8)
    high = meta_ref[pl.ds(0, sources, stride=META), :]
    low = meta_ref[pl.ds(1, sources, stride=META), :]
    index_ref[...] = (high * PITCH + low).astype(jnp.int32)
    copy = pltpu.make_async_copy(index_ref, place_ref, sem)
    copy.start()

    def clear(r, carry):
        base = pl.multiple_of((r + 2) * PITCH, 8)
        for acc in more:
            acc[pl.ds(base, PITCH), :] = jnp.zeros((PITCH, 128), jnp.float32)
        return carry

    lax.fori_loop(0, 128, clear, 0)
    copy.wait()
    accs = (acc_ref, *more)

    def add(s, carry):
        wide_ref[...] = got_ref[s, pl.ds(0, slots), :].astype(jnp.float32)
        for k in range(slots):
            acc = accs[k % NACC]
            i = place_ref[s, k]
            acc[pl.ds(i, 1), :] = acc[pl.ds(i, 1), :] + wide_ref[pl.ds(k, 1), :]
        return carry

    lax.fori_loop(0, sources, add, 0)

    def merge(r, carry):
        here = pl.ds(pl.multiple_of((r + 2) * PITCH, 8), PITCH)
        total = acc_ref[here, :]
        for acc in more:
            total = total + acc[here, :]
        acc_ref[here, :] = total
        return carry

    lax.fori_loop(0, 128, merge, 0)
    right_ref[0] = acc_ref[pl.ds(2 * PITCH + EVEN + 63, 128, stride=PITCH), :].astype(jnp.bfloat16)
    right_ref[1] = acc_ref[pl.ds(2 * PITCH + ODD + 63, 128, stride=PITCH), :].astype(jnp.bfloat16)
    left_ref[...] = acc_ref[pl.ds(2 * PITCH + EVEN, 128, stride=PITCH), :].astype(jnp.bfloat16)
    for n, r in enumerate((0, 1, 126, 127)):
        base = (r + 2) * PITCH
        rows_ref[n, pl.ds(0, 64), :] = acc_ref[pl.ds(base + ODD, 64), :].astype(jnp.bfloat16)
        rows_ref[n, pl.ds(64, 64), :] = acc_ref[pl.ds(base + EVEN, 64), :].astype(jnp.bfloat16)


def scatter(got, start):
    return pl.pallas_call(
        scatter_kernel,
        out_shape=[
            pltpu.VMEM(start.shape, jnp.float32),
            jax.ShapeDtypeStruct((2, 128, 128), jnp.bfloat16),
            jax.ShapeDtypeStruct((128, 128), jnp.bfloat16),
            jax.ShapeDtypeStruct((4, 128, 128), jnp.bfloat16),
        ],
        in_specs=[VMEM, VMEM],
        out_specs=[VMEM] * 4,
        scratch_shapes=[pltpu.VMEM((130 * PITCH, 128), jnp.float32)] * (NACC - 1)
        + [
            pltpu.VMEM((96, 128), jnp.float32),
            pltpu.VMEM((128 * META, 128), jnp.float32),
            pltpu.VMEM((128, 128), jnp.int32),
            pltpu.SMEM((128, 128), jnp.int32),
            pltpu.SemaphoreType.DMA,
        ],
        input_output_aliases={1: 0},
        compiler_params=pltpu.CompilerParams(vmem_limit_bytes=40 << 20),
        name="scatter",
    )(on_chip(got), on_chip(start))


def conv_kernel(
    band_ref,
    start_ref,
    west_ref,
    east_ref,
    down_ref,
    up_ref,
    across_ref,
    w1_ref,
    w1s_ref,
    b1_ref,
    w2_ref,
    b2_ref,
    acc_ref,
    out_ref,
    lhs_ref,
    col_ref,
    shift_ref,
    even_ref,
    odd_ref,
):
    del start_ref
    f32, bf16 = jnp.float32, jnp.bfloat16
    band = band_ref[0]
    dot = functools.partial(jnp.dot, preferred_element_type=f32)

    acc_ref[pl.ds(2 * PITCH + EVEN - 1, 128, stride=PITCH), :] = west_ref[0].astype(f32)
    acc_ref[pl.ds(2 * PITCH + ODD - 1, 128, stride=PITCH), :] = west_ref[1].astype(f32)
    acc_ref[pl.ds(2 * PITCH + EVEN + 64, 128, stride=PITCH), :] = east_ref[...].astype(f32)

    def put(slab, row):
        base = slab * PITCH
        acc_ref[pl.ds(base + ODD, 64), :] = row[0:64]
        acc_ref[pl.ds(base + EVEN, 64), :] = row[64:128]
        acc_ref[pl.ds(base + EVEN - 1, 1), :] = row[128:129]
        acc_ref[pl.ds(base + ODD - 1, 1), :] = row[129:130]
        acc_ref[pl.ds(base + EVEN + 64, 1), :] = row[130:131]

    north = band == 0
    south = band == 3
    put(0, jnp.where(north, across_ref[1].astype(f32), down_ref[0].astype(f32)))
    put(1, jnp.where(north, across_ref[0].astype(f32), down_ref[1].astype(f32)))
    put(130, jnp.where(south, across_ref[1].astype(f32), up_ref[0].astype(f32)))
    first = jnp.where(north, 2, 0)
    last = 2 - first
    flipped = (first, 1, last)

    def fill(slab):
        base = pl.multiple_of(slab * PITCH, 8)
        parts = [acc_ref[pl.ds(base + at, 64), :].astype(bf16) for at in (ODD - 1, EVEN, ODD, EVEN + 1)]
        lhs_ref[slab] = jnp.concatenate(parts, axis=-1)

    bias = b1_ref[...]
    total = jnp.zeros((136, 128), f32) + bias
    top = jnp.zeros((8, 128), f32) + bias
    for di in range(3):
        parts = [
            acc_ref[pl.ds(di * PITCH + at, 136, stride=PITCH), :].astype(bf16) for at in (EVEN - 1, ODD - 1, EVEN)
        ]
        window = jnp.concatenate(parts, axis=-1)
        total = total + dot(window, w1s_ref[di])
        top = top + dot(window[0:8], w1s_ref[flipped[di]])
    col_ref[pl.ds(0, 136), :] = gelu(total)
    col_ref[pl.ds(0, 1), :] = gelu(top)[0:1]

    bias2 = jnp.concatenate([bias, bias], axis=-1)

    def fill_step(slab, carry):
        fill(slab)
        return carry

    lax.fori_loop(0, 131, fill_step, 0)
    pre = bias2
    for di in range(3):
        pre = pre + dot(lhs_ref[di], w1_ref[flipped[di]])
    hid = gelu(pre)
    shift_ref[0, pl.ds(8, 64), :] = hid[:, 128:]
    shift_ref[0, pl.ds(7, 1), :] = col_ref[pl.ds(0, 1), :]
    odd_ref[0] = jnp.concatenate([shift_ref[0, pl.ds(7, 64), :], hid[:, :128], hid[:, 128:]], axis=-1).astype(bf16)

    def step(b, carry):
        pre = jnp.broadcast_to(bias2, (512, 256))
        for di in range(3):
            window = lhs_ref[pl.ds(b * 8 + 1 + di, 8)].reshape(512, 512)
            pre = pre + dot(window, w1_ref[di])
        hid = gelu(pre).reshape(8, 64, 256)
        shift_ref[:, pl.ds(8, 64), :] = hid[:, :, 128:]
        for n in range(8):
            shift_ref[n, pl.ds(7, 1), :] = col_ref[pl.ds(b * 8 + 1 + n, 1), :]
        wide = jnp.concatenate([shift_ref[:, pl.ds(7, 64), :], hid[:, :, :128], hid[:, :, 128:]], axis=-1)
        wide = wide.astype(bf16).reshape(4, 2, 64, 384)
        even_ref[pl.ds(b * 4, 4)] = wide[:, 0]
        odd_ref[pl.ds(b * 4 + 1, 4)] = wide[:, 1]
        return carry

    lax.fori_loop(0, 16, step, 0)

    def finish(b, carry):
        total = jnp.broadcast_to(b2_ref[...], (256, 128))
        total = total + dot(odd_ref[pl.ds(b * 4, 4)].reshape(256, 384), w2_ref[0])
        total = total + dot(even_ref[pl.ds(b * 4, 4)].reshape(256, 384), w2_ref[1])
        total = total + dot(odd_ref[pl.ds(b * 4 + 1, 4)].reshape(256, 384), w2_ref[2])
        out_ref[pl.ds(b * 4, 4)] = total.reshape(4, 64, 128).astype(bf16)
        return carry

    lax.fori_loop(0, 16, finish, 0)


def convolve(band, field, west, east, down, up, across, w1, w1s, b1, w2, b2):
    return pl.pallas_call(
        conv_kernel,
        out_shape=[
            pltpu.VMEM(field.shape, jnp.float32),
            jax.ShapeDtypeStruct((64, 64, 128), jnp.bfloat16),
        ],
        in_specs=[SMEM] + [VMEM] * 11,
        out_specs=[VMEM, VMEM],
        scratch_shapes=[
            pltpu.VMEM((131, 64, 512), jnp.bfloat16),
            pltpu.VMEM((136, 128), jnp.float32),
            pltpu.VMEM((8, 72, 128), jnp.float32),
            pltpu.VMEM((64, 64, 384), jnp.bfloat16),
            pltpu.VMEM((65, 64, 384), jnp.bfloat16),
        ],
        input_output_aliases={1: 0},
        compiler_params=pltpu.CompilerParams(vmem_limit_bytes=32 << 20),
        name="convolve",
    )(band, on_chip(field), west, east, down, up, across, w1, w1s, b1, w2, b2)[1]


def shards(background, values, cells, counts, w1, b1, w2, b2):
    lat, lon = lax.axis_size("lat"), lax.axis_size("lon")
    band = lax.axis_index("lat")
    east_pairs = [(i, (i + 1) % lon) for i in range(lon)]
    west_pairs = [(j, i) for i, j in east_pairs]
    down_pairs = [(i, i + 1) for i in range(lat - 1)]
    up_pairs = [(j, i) for i, j in down_pairs]
    pole_pairs = [(b * lon + i, b * lon + (i + lon // 2) % lon) for b in (0, lat - 1) for i in range(lon)]

    sent = pack(values[0], cells[0], counts[0][:, None])
    got = lax.all_to_all(sent, ("lat", "lon"), split_axis=0, concat_axis=0, tiled=True)
    field, right, left, rows = scatter(got, spread(background))

    west = lax.ppermute(right, "lon", east_pairs)
    east = lax.ppermute(left, "lon", west_pairs)
    cols = jnp.concatenate([west, east[None]], axis=0)
    sides = jnp.concatenate([cols[:, 0:2], cols[:, 126:128]], axis=1).transpose(1, 0, 2)
    rows = jnp.concatenate([rows, sides, jnp.zeros((4, 5, 128), jnp.bfloat16)], axis=1)
    down = lax.ppermute(rows[2:], "lat", down_pairs)
    up = lax.ppermute(rows[:2], "lat", up_pairs)
    across = lax.ppermute(jnp.where(band == 0, rows[:2], rows[2:]), ("lat", "lon"), pole_pairs)

    flat = w1.reshape(3, 384, 128)
    blank = jnp.zeros((3, 128, 128), jnp.bfloat16)
    paired = jnp.concatenate(
        [jnp.concatenate([flat, blank], axis=1), jnp.concatenate([blank, flat], axis=1)], axis=2
    )
    return convolve(
        band[None],
        field,
        west,
        east,
        down,
        up,
        across,
        paired,
        flat,
        b1[None],
        w2.reshape(3, 384, 128),
        b2[None],
    )


def solution(mesh):
    placed = (
        P("lat", "lon", None),
        P(("lat", "lon"), None, None, None),
        P(("lat", "lon"), None, None),
        P(("lat", "lon"), None),
        P(),
        P(),
        P(),
        P(),
    )
    return jax.shard_map(
        shards, mesh=mesh, in_specs=placed, out_specs=P("lat", "lon", None), check_vma=False
    )
```

```python
import functools

import jax
import jax.numpy as jnp
from jax import lax
from jax.experimental import pallas as pl
from jax.experimental.pallas import tpu as pltpu
from jax.sharding import PartitionSpec as P

PITCH, ODD, EVEN = 152, 8, 80
SLABS = 131
NACC = 4
META = 8
GELU_A, GELU_B = 0.7978845608028654, 0.044715
VMEM = pl.BlockSpec(memory_space=pltpu.VMEM)
SMEM = pl.BlockSpec(memory_space=pltpu.SMEM)
ANY = pl.BlockSpec(memory_space=pl.ANY)


def on_chip(x):
    return pltpu.with_memory_space_constraint(x, pltpu.VMEM)


def gelu(x):
    return 0.5 * x * (1.0 + jnp.tanh(GELU_A * (x + GELU_B * (x * x * x))))


def pack_kernel(values_ref, cells_ref, counts_ref, out_ref, meta_ref, sem):
    slots = values_ref.shape[1]
    body = pltpu.make_async_copy(values_ref, out_ref.at[:, pl.ds(0, slots), :], sem.at[0])
    body.start()
    cells = cells_ref[...]
    live = lax.broadcasted_iota(jnp.int32, cells.shape, 1) < counts_ref[...]
    row = cells >> 7
    col = cells & 127
    high = jnp.where(live, row + 2, 0).astype(jnp.float32)
    low = jnp.where(live, (col >> 1) + jnp.where((col & 1) == 1, ODD, EVEN), 0).astype(jnp.float32)
    both = jnp.concatenate(
        [high[:, None, :], low[:, None, :], jnp.zeros((cells.shape[0], META - 2, 128), jnp.float32)], axis=1
    )
    meta_ref[...] = both.astype(jnp.bfloat16)
    tail = pltpu.make_async_copy(meta_ref, out_ref.at[:, pl.ds(slots, META), :], sem.at[1])
    tail.start()
    body.wait()
    tail.wait()


def pack(values, cells, counts):
    owners, slots, chans = values.shape
    return pl.pallas_call(
        pack_kernel,
        out_shape=jax.ShapeDtypeStruct((owners, slots + META, chans), jnp.bfloat16),
        in_specs=[ANY, VMEM, VMEM],
        out_specs=ANY,
        scratch_shapes=[
            pltpu.VMEM((owners, META, chans), jnp.bfloat16),
            pltpu.SemaphoreType.DMA((2,)),
        ],
        compiler_params=pltpu.CompilerParams(vmem_limit_bytes=8 << 20),
        name="pack",
    )(values, jnp.pad(cells, ((0, 0), (0, 128 - slots))), counts)


def spread_kernel(field_ref, acc_ref, wide_ref):
    def step(r, carry):
        wide_ref[...] = field_ref[r].astype(jnp.float32)
        base = pl.multiple_of((r + 2) * PITCH, 8)
        acc_ref[pl.ds(base + ODD, 64), :] = wide_ref[pl.ds(1, 64, stride=2), :]
        acc_ref[pl.ds(base + EVEN, 64), :] = wide_ref[pl.ds(0, 64, stride=2), :]
        for at in (0, EVEN - 8, EVEN + 64):
            acc_ref[pl.ds(base + at, 8), :] = jnp.zeros((8, 128), jnp.float32)
        return carry

    lax.fori_loop(0, field_ref.shape[0], step, 0)


def spread(field):
    return pl.pallas_call(
        spread_kernel,
        out_shape=jax.ShapeDtypeStruct((SLABS * PITCH, 128), jnp.float32),
        in_specs=[VMEM],
        out_specs=VMEM,
        scratch_shapes=[pltpu.VMEM((128, 128), jnp.float32)],
        compiler_params=pltpu.CompilerParams(vmem_limit_bytes=12 << 20),
        name="spread",
    )(field)


def scatter_kernel(band_ref, got_ref, start_ref, acc_ref, right_ref, left_ref, near_ref, rows_ref, *rest):
    more = rest[: NACC - 1]
    wide_ref, meta_ref, index_ref, place_ref, sem = rest[NACC - 1 :]
    del band_ref
    sources, slots = got_ref.shape[0], got_ref.shape[1] - META
    first = pltpu.make_async_copy(start_ref, acc_ref, sem.at[1])
    first.start()

    def unpack(s, carry):
        meta_ref[pl.ds(pl.multiple_of(s * META, META), META), :] = got_ref[s, pl.ds(slots, META), :].astype(jnp.float32)
        return carry

    lax.fori_loop(0, sources, unpack, 0, unroll=8)
    high = meta_ref[pl.ds(0, sources, stride=META), :]
    low = meta_ref[pl.ds(1, sources, stride=META), :]
    index_ref[...] = (high * PITCH + low).astype(jnp.int32)
    copy = pltpu.make_async_copy(index_ref, place_ref, sem.at[0])
    copy.start()

    def clear(r, carry):
        base = pl.multiple_of((r + 2) * PITCH, 8)
        for acc in more:
            acc[pl.ds(base, PITCH), :] = jnp.zeros((PITCH, 128), jnp.float32)
        return carry

    lax.fori_loop(0, 128, clear, 0)
    copy.wait()
    first.wait()
    accs = (acc_ref, *more)

    def add(s, carry):
        wide_ref[...] = got_ref[s, pl.ds(0, slots), :].astype(jnp.float32)
        for k in range(slots):
            acc = accs[k % NACC]
            i = place_ref[s, k]
            acc[pl.ds(i, 1), :] = acc[pl.ds(i, 1), :] + wide_ref[pl.ds(k, 1), :]
        return carry

    lax.fori_loop(0, sources, add, 0)

    def merge(r, carry):
        here = pl.ds(pl.multiple_of((r + 2) * PITCH, 8), PITCH)
        total = acc_ref[here, :]
        for acc in more:
            total = total + acc[here, :]
        acc_ref[here, :] = total
        return carry

    lax.fori_loop(0, 128, merge, 0)
    bf16 = jnp.bfloat16
    ends = (0, 1, 126, 127)
    for n, at in enumerate((EVEN + 63, ODD + 63)):
        right_ref[pl.ds(n * 128, 128), :] = acc_ref[pl.ds(2 * PITCH + at, 128, stride=PITCH), :].astype(bf16)
    left_ref[pl.ds(0, 128), :] = acc_ref[pl.ds(2 * PITCH + EVEN, 128, stride=PITCH), :].astype(bf16)
    near_ref[...] = acc_ref[pl.ds(2 * PITCH + ODD, 128, stride=PITCH), :].astype(bf16)
    east = [acc_ref[pl.ds((r + 2) * PITCH + at, 1), :] for r in ends for at in (EVEN + 63, ODD + 63)]
    west = [acc_ref[pl.ds((r + 2) * PITCH + EVEN, 1), :] for r in ends]
    right_ref[pl.ds(256, 8), :] = jnp.concatenate(east, axis=0).astype(bf16)
    left_ref[pl.ds(128, 8), :] = jnp.concatenate(west + west, axis=0).astype(bf16)
    for n, r in enumerate(ends):
        base = (r + 2) * PITCH
        rows_ref[n, pl.ds(0, 64), :] = acc_ref[pl.ds(base + ODD, 64), :].astype(bf16)
        rows_ref[n, pl.ds(64, 64), :] = acc_ref[pl.ds(base + EVEN, 64), :].astype(bf16)


def scatter(band, got, start):
    return pl.pallas_call(
        scatter_kernel,
        out_shape=[
            pltpu.VMEM(start.shape, jnp.float32),
            jax.ShapeDtypeStruct((264, 128), jnp.bfloat16),
            jax.ShapeDtypeStruct((136, 128), jnp.bfloat16),
            jax.ShapeDtypeStruct((128, 128), jnp.bfloat16),
            jax.ShapeDtypeStruct((4, 128, 128), jnp.bfloat16),
        ],
        in_specs=[SMEM, VMEM, ANY],
        out_specs=[VMEM] * 5,
        scratch_shapes=[pltpu.VMEM((130 * PITCH, 128), jnp.float32)] * (NACC - 1)
        + [
            pltpu.VMEM((96, 128), jnp.float32),
            pltpu.VMEM((128 * META, 128), jnp.float32),
            pltpu.VMEM((128, 128), jnp.int32),
            pltpu.SMEM((128, 128), jnp.int32),
            pltpu.SemaphoreType.DMA((2,)),
        ],
        compiler_params=pltpu.CompilerParams(vmem_limit_bytes=40 << 20),
        name="scatter",
    )(band, on_chip(got), start)


def frame_kernel(after_ref, rows_ref, west_ref, east_ref, down_ref, up_ref, all_ref):
    del after_ref
    f32, bf16 = jnp.float32, jnp.bfloat16
    west = west_ref[pl.ds(256, 8), :].astype(f32)
    east = east_ref[pl.ds(128, 8), :].astype(f32)
    for n in range(4):
        tail = jnp.concatenate([west[2 * n : 2 * n + 2], east[n : n + 1], jnp.zeros((5, 128), f32)], axis=0)
        for ref, at in ((all_ref, n), (up_ref, n) if n < 2 else (down_ref, n - 2)):
            ref[at, pl.ds(0, 128), :] = rows_ref[n]
            ref[at, pl.ds(128, 8), :] = tail.astype(bf16)


def frame(after, rows, west, east):
    return pl.pallas_call(
        frame_kernel,
        out_shape=[
            jax.ShapeDtypeStruct((2, 136, 128), jnp.bfloat16),
            jax.ShapeDtypeStruct((2, 136, 128), jnp.bfloat16),
            jax.ShapeDtypeStruct((4, 136, 128), jnp.bfloat16),
        ],
        in_specs=[ANY] + [VMEM] * 3,
        out_specs=[VMEM] * 3,
        compiler_params=pltpu.CompilerParams(vmem_limit_bytes=4 << 20),
        name="frame",
    )(after, rows, west, east)


def inner_kernel(low, field_ref, w1_ref, b1_ref, even_ref, odd_ref, mark_ref, lhs_ref, shift_ref):
    f32, bf16 = jnp.float32, jnp.bfloat16

    def fill(t, carry):
        base = pl.multiple_of((low + 1 + t) * PITCH, 8)
        parts = [field_ref[pl.ds(base + at, 64), :].astype(bf16) for at in (ODD - 1, EVEN, ODD, EVEN + 1)]
        lhs_ref[t] = jnp.concatenate(parts, axis=-1)
        return carry

    lax.fori_loop(0, 66, fill, 0)
    bias = jnp.concatenate([b1_ref[...], b1_ref[...]], axis=-1)

    def step(b, carry):
        pre = jnp.broadcast_to(bias, (512, 256))
        for di in range(3):
            window = lhs_ref[pl.ds(b * 8 + di, 8)].reshape(512, 512)
            pre = pre + jnp.dot(window, w1_ref[di], preferred_element_type=f32)
        hid = gelu(pre).reshape(8, 64, 256)
        shift_ref[:, pl.ds(8, 64), :] = hid[:, :, 128:]
        wide = jnp.concatenate([shift_ref[:, pl.ds(7, 64), :], hid[:, :, :128], hid[:, :, 128:]], axis=-1)
        wide = wide.astype(bf16).reshape(4, 2, 64, 384)
        even_ref[pl.ds(b * 4, 4)] = wide[:, 0]
        odd_ref[pl.ds(b * 4 + 1, 4)] = wide[:, 1]
        return carry

    lax.fori_loop(0, 8, step, 0)
    mark_ref[...] = jnp.zeros(mark_ref.shape, mark_ref.dtype)


def inner(low, field, w1, b1):
    return pl.pallas_call(
        functools.partial(inner_kernel, low),
        out_shape=[
            pltpu.VMEM((32, 64, 384), jnp.bfloat16),
            pltpu.VMEM((33, 64, 384), jnp.bfloat16),
            jax.ShapeDtypeStruct((8, 128), jnp.float32),
        ],
        in_specs=[VMEM] * 3,
        out_specs=[VMEM] * 3,
        scratch_shapes=[pltpu.VMEM((66, 64, 512), jnp.bfloat16), pltpu.VMEM((8, 72, 128), jnp.float32)],
        compiler_params=pltpu.CompilerParams(vmem_limit_bytes=24 << 20),
        name="inner",
    )(on_chip(field), w1, b1)


def rim_kernel(
    band_ref,
    even0_in,
    odd0_in,
    even1_in,
    odd1_in,
    right_ref,
    left_ref,
    near_ref,
    west_ref,
    east_ref,
    own_ref,
    down_ref,
    up_ref,
    across_ref,
    w1_ref,
    w1s_ref,
    b1_ref,
    w2_ref,
    b2_ref,
    even0_ref,
    odd0_ref,
    even1_ref,
    odd1_ref,
    out_ref,
    cols_ref,
    strip_ref,
    shift_ref,
    side_ref,
):
    del even0_in, odd0_in, even1_in, odd1_in
    f32, bf16 = jnp.float32, jnp.bfloat16
    band = band_ref[0]
    north, south = band == 0, band == 3
    first = jnp.where(north, 2, 0)
    flipped = (first, 1, 2 - first)
    dot = functools.partial(jnp.dot, preferred_element_type=f32)
    bias = b1_ref[...]
    bias2 = jnp.concatenate([bias, bias], axis=-1)

    body = (
        west_ref[pl.ds(0, 128), :],
        west_ref[pl.ds(128, 128), :],
        left_ref[pl.ds(0, 128), :],
        near_ref[...],
        right_ref[pl.ds(0, 128), :],
        right_ref[pl.ds(128, 128), :],
        east_ref[pl.ds(0, 128), :],
    )
    for n, col in enumerate(body):
        cols_ref[n, pl.ds(2, 128), :] = col.astype(f32)

    def wide(ref, n):
        return ref[n].astype(f32)

    rows = (
        jnp.where(north, wide(across_ref, 1), wide(down_ref, 0)),
        jnp.where(north, wide(across_ref, 0), wide(down_ref, 1)),
        wide(own_ref, 0),
        wide(own_ref, 1),
        wide(own_ref, 2),
        wide(own_ref, 3),
        jnp.where(south, wide(across_ref, 3), wide(up_ref, 0)),
    )
    where = (128, 129, 64, 0, 127, 63, 130)
    lhs = []
    for n, row in enumerate(rows):
        strip_ref[n, pl.ds(ODD, 64), :] = row[0:64]
        strip_ref[n, pl.ds(EVEN, 64), :] = row[64:128]
        strip_ref[n, pl.ds(ODD - 1, 1), :] = row[129:130]
        strip_ref[n, pl.ds(EVEN + 64, 1), :] = row[130:131]
        if n in (0, 1, 6):
            slab = 130 if n == 6 else n
            for m, at in enumerate(where):
                cols_ref[m, pl.ds(slab, 1), :] = row[at : at + 1]
        parts = [strip_ref[n, pl.ds(at, 64), :].astype(bf16) for at in (ODD - 1, EVEN, ODD, EVEN + 1)]
        lhs.append(jnp.concatenate(parts, axis=-1))

    for n, at in enumerate((0, 1, 4)):
        total = jnp.zeros((136, 128), f32) + bias
        top = jnp.zeros((8, 128), f32) + bias
        for di in range(3):
            window = jnp.concatenate(
                [cols_ref[at + m, pl.ds(di, 136), :].astype(bf16) for m in range(3)], axis=-1
            )
            total = total + dot(window, w1s_ref[di])
            if n == 0:
                top = top + dot(window[0:8], w1s_ref[flipped[di]])
        side_ref[n, pl.ds(0, 136), :] = gelu(total)
        if n == 0:
            side_ref[n, pl.ds(0, 1), :] = gelu(top)[0:1]

    odd1_ref[0] = odd0_ref[32]
    for r, at, taps in ((-1, 0, flipped), (0, 1, (0, 1, 2)), (127, 4, (0, 1, 2))):
        pre = bias2
        for di in range(3):
            pre = pre + dot(lhs[at + di], w1_ref[taps[di]])
        hid = gelu(pre)
        shift_ref[pl.ds(8, 64), :] = hid[:, 128:]
        shift_ref[pl.ds(7, 1), :] = side_ref[0, pl.ds(r + 1, 1), :]
        line = jnp.concatenate([shift_ref[pl.ds(7, 64), :], hid[:, :128], hid[:, 128:]], axis=-1).astype(bf16)
        if r == -1:
            odd0_ref[0] = line
        elif r == 0:
            even0_ref[0] = line
        else:
            odd1_ref[32] = line

    head = lax.broadcasted_iota(jnp.int32, (16, 256), 0) == 0
    foot = lax.broadcasted_iota(jnp.int32, (16, 128), 0) == 15

    def mend(ref, p, r):
        here = pl.ds(r + 1, 1)
        new = jnp.concatenate([side_ref[0, here, :], side_ref[1, here, :]], axis=-1)
        old = ref[p, pl.ds(0, 16), pl.ds(0, 256)].astype(f32)
        ref[p, pl.ds(0, 16), pl.ds(0, 256)] = jnp.where(head, new, old).astype(bf16)
        old = ref[p, pl.ds(48, 16), pl.ds(256, 128)].astype(f32)
        ref[p, pl.ds(48, 16), pl.ds(256, 128)] = jnp.where(foot, side_ref[2, here, :], old).astype(bf16)

    def mend_step(p, carry):
        mend(even0_ref, p, 2 * p)
        mend(odd0_ref, p + 1, 2 * p + 1)
        mend(even1_ref, p, 2 * p + 64)
        mend(odd1_ref, p + 1, 2 * p + 65)
        return carry

    lax.fori_loop(0, 32, mend_step, 0, unroll=2)
    odd1_ref[0] = odd0_ref[32]

    for half, (even_ref, odd_ref) in enumerate(((even0_ref, odd0_ref), (even1_ref, odd1_ref))):

        def finish(b, carry):
            total = jnp.broadcast_to(b2_ref[...], (256, 128))
            total = total + dot(odd_ref[pl.ds(b * 4, 4)].reshape(256, 384), w2_ref[0])
            total = total + dot(even_ref[pl.ds(b * 4, 4)].reshape(256, 384), w2_ref[1])
            total = total + dot(odd_ref[pl.ds(b * 4 + 1, 4)].reshape(256, 384), w2_ref[2])
            out_ref[pl.ds(half * 32 + b * 4, 4)] = total.reshape(4, 64, 128).astype(bf16)
            return carry

        lax.fori_loop(0, 8, finish, 0)


def rim(band, blocks, *rest):
    return pl.pallas_call(
        rim_kernel,
        out_shape=[pltpu.VMEM(b.shape, b.dtype) for b in blocks] + [jax.ShapeDtypeStruct((64, 64, 128), jnp.bfloat16)],
        in_specs=[SMEM] + [VMEM] * 18,
        out_specs=[VMEM] * 5,
        scratch_shapes=[
            pltpu.VMEM((7, 144, 128), jnp.float32),
            pltpu.VMEM((7, PITCH, 128), jnp.float32),
            pltpu.VMEM((72, 128), jnp.float32),
            pltpu.VMEM((3, 136, 128), jnp.float32),
        ],
        input_output_aliases={1: 0, 2: 1, 3: 2, 4: 3},
        compiler_params=pltpu.CompilerParams(vmem_limit_bytes=16 << 20),
        name="rim",
    )(band, *map(on_chip, blocks), *rest)[4]


def shards(background, values, cells, counts, w1, b1, w2, b2):
    lat, lon = lax.axis_size("lat"), lax.axis_size("lon")
    band = lax.axis_index("lat")[None]
    east_pairs = [(i, (i + 1) % lon) for i in range(lon)]
    west_pairs = [(j, i) for i, j in east_pairs]
    down_pairs = [(i, i + 1) for i in range(lat - 1)]
    up_pairs = [(j, i) for i, j in down_pairs]
    pole_pairs = [(b * lon + i, b * lon + (i + lon // 2) % lon) for b in (0, lat - 1) for i in range(lon)]

    sent = pack(values[0], cells[0], counts[0][:, None])
    got = lax.all_to_all(sent, ("lat", "lon"), split_axis=0, concat_axis=0, tiled=True)
    field, right, left, near, rows = scatter(band, got, spread(background))

    flat = w1.reshape(3, 384, 128)
    blank = jnp.zeros((3, 128, 128), jnp.bfloat16)
    paired = jnp.concatenate(
        [jnp.concatenate([flat, blank], axis=1), jnp.concatenate([blank, flat], axis=1)], axis=2
    )
    west = lax.ppermute(right, "lon", east_pairs)
    east = lax.ppermute(left, "lon", west_pairs)
    *upper, mark = inner(0, field, paired, b1[None])
    lower_rows, upper_rows, own = frame(mark, rows, west, east)
    down = lax.ppermute(lower_rows, "lat", down_pairs)
    up = lax.ppermute(upper_rows, "lat", up_pairs)
    across = lax.ppermute(own, ("lat", "lon"), pole_pairs)
    *lower, _ = inner(64, field, paired, b1[None])
    return rim(
        band,
        (*upper, *lower),
        right,
        left,
        near,
        west,
        east,
        own,
        down,
        up,
        across,
        paired,
        flat,
        b1[None],
        w2.reshape(3, 384, 128),
        b2[None],
    )


def solution(mesh):
    placed = (
        P("lat", "lon", None),
        P(("lat", "lon"), None, None, None),
        P(("lat", "lon"), None, None),
        P(("lat", "lon"), None),
        P(),
        P(),
        P(),
        P(),
    )
    return jax.shard_map(
        shards, mesh=mesh, in_specs=placed, out_specs=P("lat", "lon", None), check_vma=False
    )
```

```python
import functools

import jax
import jax.numpy as jnp
from jax import lax
from jax.experimental import pallas as pl
from jax.experimental.pallas import tpu as pltpu
from jax.sharding import PartitionSpec as P

PITCH, ODD, EVEN = 152, 8, 80
SLABS = 131
BATCH = 8
GROUP = 8
META = 8
GELU_A, GELU_B = 0.7978845608028654, 0.044715
VMEM = pl.BlockSpec(memory_space=pltpu.VMEM)
SMEM = pl.BlockSpec(memory_space=pltpu.SMEM)
ANY = pl.BlockSpec(memory_space=pl.ANY)


def on_chip(x):
    return pltpu.with_memory_space_constraint(x, pltpu.VMEM)


def gelu(x):
    return 0.5 * x * (1.0 + jnp.tanh(GELU_A * (x + GELU_B * (x * x * x))))


def pack_kernel(values_ref, cells_ref, counts_ref, out_ref, meta_ref, sem):
    slots = values_ref.shape[1]
    body = pltpu.make_async_copy(values_ref, out_ref.at[:, pl.ds(0, slots), :], sem.at[0])
    body.start()
    cells = cells_ref[...]
    live = lax.broadcasted_iota(jnp.int32, cells.shape, 1) < counts_ref[...]
    row = cells >> 7
    col = cells & 127
    high = jnp.where(live, row + 2, 0).astype(jnp.float32)
    low = jnp.where(live, (col >> 1) + jnp.where((col & 1) == 1, ODD, EVEN), 0).astype(jnp.float32)
    again = jnp.zeros(cells.shape, jnp.float32)
    place = lax.broadcasted_iota(jnp.int32, cells.shape, 1) % BATCH
    marked = jnp.where(live, cells, -1)
    for back in range(1, BATCH):
        same = (pltpu.roll(marked, back, 1) == marked) & live & (place >= back)
        again = jnp.where(same, 1.0, again)
    both = jnp.concatenate(
        [
            high[:, None, :],
            low[:, None, :],
            again[:, None, :],
            jnp.zeros((cells.shape[0], META - 3, 128), jnp.float32),
        ],
        axis=1,
    )
    meta_ref[...] = both.astype(jnp.bfloat16)
    tail = pltpu.make_async_copy(meta_ref, out_ref.at[:, pl.ds(slots, META), :], sem.at[1])
    tail.start()
    body.wait()
    tail.wait()


def pack(values, cells, counts):
    owners, slots, chans = values.shape
    return pl.pallas_call(
        pack_kernel,
        out_shape=jax.ShapeDtypeStruct((owners, slots + META, chans), jnp.bfloat16),
        in_specs=[ANY, VMEM, VMEM],
        out_specs=ANY,
        scratch_shapes=[
            pltpu.VMEM((owners, META, chans), jnp.bfloat16),
            pltpu.SemaphoreType.DMA((2,)),
        ],
        compiler_params=pltpu.CompilerParams(vmem_limit_bytes=8 << 20),
        name="pack",
    )(values, jnp.pad(cells, ((0, 0), (0, 128 - slots))), counts)


def spread_kernel(field_ref, acc_ref, wide_ref):
    def step(r, carry):
        wide_ref[...] = field_ref[r].astype(jnp.float32)
        base = pl.multiple_of((r + 2) * PITCH, 8)
        acc_ref[pl.ds(base + ODD, 64), :] = wide_ref[pl.ds(1, 64, stride=2), :]
        acc_ref[pl.ds(base + EVEN, 64), :] = wide_ref[pl.ds(0, 64, stride=2), :]
        for at in (0, EVEN - 8, EVEN + 64):
            acc_ref[pl.ds(base + at, 8), :] = jnp.zeros((8, 128), jnp.float32)
        return carry

    lax.fori_loop(0, field_ref.shape[0], step, 0)


def spread(field):
    return pl.pallas_call(
        spread_kernel,
        out_shape=jax.ShapeDtypeStruct((SLABS * PITCH, 128), jnp.float32),
        in_specs=[VMEM],
        out_specs=VMEM,
        scratch_shapes=[pltpu.VMEM((128, 128), jnp.float32)],
        compiler_params=pltpu.CompilerParams(vmem_limit_bytes=12 << 20),
        name="spread",
    )(field)


def scatter_kernel(band_ref, got_ref, start_ref, acc_ref, right_ref, left_ref, near_ref, rows_ref, *rest):
    other_ref, wide_ref, meta_ref, index_ref, late_ref, cells0_ref, cells1_ref, list_ref, sem = rest
    del band_ref
    sources, slots = got_ref.shape[0], got_ref.shape[1] - META
    first = pltpu.make_async_copy(start_ref, acc_ref, sem.at[0])
    first.start()

    def unpack(s, carry):
        meta_ref[pl.ds(pl.multiple_of(s * META, META), META), :] = got_ref[s, pl.ds(slots, META), :].astype(jnp.float32)
        return carry

    lax.fori_loop(0, sources, unpack, 0, unroll=8)
    high = meta_ref[pl.ds(0, sources, stride=META), :]
    low = meta_ref[pl.ds(1, sources, stride=META), :]
    again = meta_ref[pl.ds(2, sources, stride=META), :]
    spot = high * PITCH + low
    index_ref[...] = jnp.where(again > 0, 0.0, spot).astype(jnp.int32)
    lane = lax.broadcasted_iota(jnp.int32, again.shape, 1)
    inside = lane < slots
    count = jnp.sum(jnp.where(inside, again, 0.0), axis=1, keepdims=True)
    late = jnp.where(inside, again * spot, jnp.broadcast_to(count, again.shape))
    late_ref[...] = late.astype(jnp.int32)

    cells = (cells0_ref, cells1_ref)

    def fetch(group, half):
        return pltpu.make_async_copy(index_ref.at[pl.ds(group * GROUP, GROUP), :], cells[half], sem.at[1 + half])

    fetch(0, 0).start()
    fetch(1, 1).start()
    listed = pltpu.make_async_copy(late_ref, list_ref, sem.at[3])
    listed.start()

    def clear(r, carry):
        other_ref[pl.ds(pl.multiple_of((r + 2) * PITCH, 8), PITCH), :] = jnp.zeros((PITCH, 128), jnp.float32)
        return carry

    lax.fori_loop(0, 128, clear, 0)
    first.wait()
    accs = (acc_ref, other_ref)

    def add(step, carry):
        for half in range(2):
            group = step * 2 + half
            fetch(group, half).wait()
            for t in range(GROUP):
                wide = wide_ref.at[t % 2]
                wide[...] = got_ref[group * GROUP + t, pl.ds(0, slots), :].astype(jnp.float32)
                for n, k in enumerate(range(0, slots, BATCH)):
                    acc = accs[n % 2]
                    where = [cells[half][t, k + m] for m in range(BATCH)]
                    sums = [acc[pl.ds(i, 1), :] + wide[pl.ds(k + m, 1), :] for m, i in enumerate(where)]
                    for i, total in zip(where, sums):
                        acc[pl.ds(i, 1), :] = total

            @pl.when(group + 2 < sources // GROUP)
            def _():
                fetch(group + 2, half).start()

        return carry

    lax.fori_loop(0, sources // (2 * GROUP), add, 0)
    listed.wait()

    def rest_of(s, carry):
        @pl.when(list_ref[s, slots] > 0)
        def _():
            wide_ref[0] = got_ref[s, pl.ds(0, slots), :].astype(jnp.float32)

            def one(k, carry):
                i = list_ref[s, k]

                @pl.when(i > 0)
                def _():
                    acc_ref[pl.ds(i, 1), :] = acc_ref[pl.ds(i, 1), :] + wide_ref[0, pl.ds(k, 1), :]

                return carry

            lax.fori_loop(0, slots, one, 0)

        return carry

    lax.fori_loop(0, sources, rest_of, 0)

    def merge(r, carry):
        here = pl.ds(pl.multiple_of((r + 2) * PITCH, 8), PITCH)
        acc_ref[here, :] = acc_ref[here, :] + other_ref[here, :]
        return carry

    lax.fori_loop(0, 128, merge, 0)
    bf16 = jnp.bfloat16
    ends = (0, 1, 126, 127)
    for n, at in enumerate((EVEN + 63, ODD + 63)):
        right_ref[pl.ds(n * 128, 128), :] = acc_ref[pl.ds(2 * PITCH + at, 128, stride=PITCH), :].astype(bf16)
    left_ref[pl.ds(0, 128), :] = acc_ref[pl.ds(2 * PITCH + EVEN, 128, stride=PITCH), :].astype(bf16)
    near_ref[...] = acc_ref[pl.ds(2 * PITCH + ODD, 128, stride=PITCH), :].astype(bf16)
    east = [acc_ref[pl.ds((r + 2) * PITCH + at, 1), :] for r in ends for at in (EVEN + 63, ODD + 63)]
    west = [acc_ref[pl.ds((r + 2) * PITCH + EVEN, 1), :] for r in ends]
    right_ref[pl.ds(256, 8), :] = jnp.concatenate(east, axis=0).astype(bf16)
    left_ref[pl.ds(128, 8), :] = jnp.concatenate(west + west, axis=0).astype(bf16)
    for n, r in enumerate(ends):
        base = (r + 2) * PITCH
        rows_ref[n, pl.ds(0, 64), :] = acc_ref[pl.ds(base + ODD, 64), :].astype(bf16)
        rows_ref[n, pl.ds(64, 64), :] = acc_ref[pl.ds(base + EVEN, 64), :].astype(bf16)


def scatter(band, got, start):
    return pl.pallas_call(
        scatter_kernel,
        out_shape=[
            pltpu.VMEM(start.shape, jnp.float32),
            jax.ShapeDtypeStruct((264, 128), jnp.bfloat16),
            jax.ShapeDtypeStruct((136, 128), jnp.bfloat16),
            jax.ShapeDtypeStruct((128, 128), jnp.bfloat16),
            jax.ShapeDtypeStruct((4, 128, 128), jnp.bfloat16),
        ],
        in_specs=[SMEM, VMEM, ANY],
        out_specs=[VMEM] * 5,
        scratch_shapes=[
            pltpu.VMEM((130 * PITCH, 128), jnp.float32),
            pltpu.VMEM((2, 96, 128), jnp.float32),
            pltpu.VMEM((128 * META, 128), jnp.float32),
            pltpu.VMEM((128, 128), jnp.int32),
            pltpu.VMEM((128, 128), jnp.int32),
            pltpu.SMEM((GROUP, 128), jnp.int32),
            pltpu.SMEM((GROUP, 128), jnp.int32),
            pltpu.SMEM((128, 128), jnp.int32),
            pltpu.SemaphoreType.DMA((4,)),
        ],
        compiler_params=pltpu.CompilerParams(vmem_limit_bytes=24 << 20),
        name="scatter",
    )(band, on_chip(got), start)


def frame_kernel(after_ref, rows_ref, west_ref, east_ref, down_ref, up_ref, all_ref):
    del after_ref
    f32, bf16 = jnp.float32, jnp.bfloat16
    west = west_ref[pl.ds(256, 8), :].astype(f32)
    east = east_ref[pl.ds(128, 8), :].astype(f32)
    for n in range(4):
        tail = jnp.concatenate([west[2 * n : 2 * n + 2], east[n : n + 1], jnp.zeros((5, 128), f32)], axis=0)
        for ref, at in ((all_ref, n), (up_ref, n) if n < 2 else (down_ref, n - 2)):
            ref[at, pl.ds(0, 128), :] = rows_ref[n]
            ref[at, pl.ds(128, 8), :] = tail.astype(bf16)


def frame(after, rows, west, east):
    return pl.pallas_call(
        frame_kernel,
        out_shape=[
            jax.ShapeDtypeStruct((2, 136, 128), jnp.bfloat16),
            jax.ShapeDtypeStruct((2, 136, 128), jnp.bfloat16),
            jax.ShapeDtypeStruct((4, 136, 128), jnp.bfloat16),
        ],
        in_specs=[ANY] + [VMEM] * 3,
        out_specs=[VMEM] * 3,
        compiler_params=pltpu.CompilerParams(vmem_limit_bytes=4 << 20),
        name="frame",
    )(after, rows, west, east)


def inner_kernel(low, field_ref, w1_ref, b1_ref, even_ref, odd_ref, mark_ref, lhs_ref, shift_ref):
    f32, bf16 = jnp.float32, jnp.bfloat16

    def fill(t, carry):
        base = pl.multiple_of((low + 1 + t) * PITCH, 8)
        parts = [field_ref[pl.ds(base + at, 64), :].astype(bf16) for at in (ODD - 1, EVEN, ODD, EVEN + 1)]
        lhs_ref[t] = jnp.concatenate(parts, axis=-1)
        return carry

    lax.fori_loop(0, 66, fill, 0)
    bias = jnp.concatenate([b1_ref[...], b1_ref[...]], axis=-1)

    def step(b, carry):
        pre = jnp.broadcast_to(bias, (512, 256))
        for di in range(3):
            window = lhs_ref[pl.ds(b * 8 + di, 8)].reshape(512, 512)
            pre = pre + jnp.dot(window, w1_ref[di], preferred_element_type=f32)
        hid = gelu(pre).reshape(8, 64, 256)
        shift_ref[:, pl.ds(8, 64), :] = hid[:, :, 128:]
        wide = jnp.concatenate([shift_ref[:, pl.ds(7, 64), :], hid[:, :, :128], hid[:, :, 128:]], axis=-1)
        wide = wide.astype(bf16).reshape(4, 2, 64, 384)
        even_ref[pl.ds(b * 4, 4)] = wide[:, 0]
        odd_ref[pl.ds(b * 4 + 1, 4)] = wide[:, 1]
        return carry

    lax.fori_loop(0, 8, step, 0)
    mark_ref[...] = jnp.zeros(mark_ref.shape, mark_ref.dtype)


def inner(low, field, w1, b1):
    return pl.pallas_call(
        functools.partial(inner_kernel, low),
        out_shape=[
            pltpu.VMEM((32, 64, 384), jnp.bfloat16),
            pltpu.VMEM((33, 64, 384), jnp.bfloat16),
            jax.ShapeDtypeStruct((8, 128), jnp.float32),
        ],
        in_specs=[VMEM] * 3,
        out_specs=[VMEM] * 3,
        scratch_shapes=[pltpu.VMEM((66, 64, 512), jnp.bfloat16), pltpu.VMEM((8, 72, 128), jnp.float32)],
        compiler_params=pltpu.CompilerParams(vmem_limit_bytes=24 << 20),
        name="inner",
    )(on_chip(field), w1, b1)


def rim_kernel(
    band_ref,
    even0_in,
    odd0_in,
    even1_in,
    odd1_in,
    right_ref,
    left_ref,
    near_ref,
    west_ref,
    east_ref,
    own_ref,
    down_ref,
    up_ref,
    across_ref,
    w1_ref,
    w1s_ref,
    b1_ref,
    w2_ref,
    b2_ref,
    even0_ref,
    odd0_ref,
    even1_ref,
    odd1_ref,
    out_ref,
    cols_ref,
    strip_ref,
    shift_ref,
    side_ref,
):
    del even0_in, odd0_in, even1_in, odd1_in
    f32, bf16 = jnp.float32, jnp.bfloat16
    band = band_ref[0]
    north, south = band == 0, band == 3
    first = jnp.where(north, 2, 0)
    flipped = (first, 1, 2 - first)
    dot = functools.partial(jnp.dot, preferred_element_type=f32)
    bias = b1_ref[...]
    bias2 = jnp.concatenate([bias, bias], axis=-1)

    body = (
        west_ref[pl.ds(0, 128), :],
        west_ref[pl.ds(128, 128), :],
        left_ref[pl.ds(0, 128), :],
        near_ref[...],
        right_ref[pl.ds(0, 128), :],
        right_ref[pl.ds(128, 128), :],
        east_ref[pl.ds(0, 128), :],
    )
    for n, col in enumerate(body):
        cols_ref[n, pl.ds(2, 128), :] = col.astype(f32)

    def wide(ref, n):
        return ref[n].astype(f32)

    rows = (
        jnp.where(north, wide(across_ref, 1), wide(down_ref, 0)),
        jnp.where(north, wide(across_ref, 0), wide(down_ref, 1)),
        wide(own_ref, 0),
        wide(own_ref, 1),
        wide(own_ref, 2),
        wide(own_ref, 3),
        jnp.where(south, wide(across_ref, 3), wide(up_ref, 0)),
    )
    where = (128, 129, 64, 0, 127, 63, 130)
    lhs = []
    for n, row in enumerate(rows):
        strip_ref[n, pl.ds(ODD, 64), :] = row[0:64]
        strip_ref[n, pl.ds(EVEN, 64), :] = row[64:128]
        strip_ref[n, pl.ds(ODD - 1, 1), :] = row[129:130]
        strip_ref[n, pl.ds(EVEN + 64, 1), :] = row[130:131]
        if n in (0, 1, 6):
            slab = 130 if n == 6 else n
            for m, at in enumerate(where):
                cols_ref[m, pl.ds(slab, 1), :] = row[at : at + 1]
        parts = [strip_ref[n, pl.ds(at, 64), :].astype(bf16) for at in (ODD - 1, EVEN, ODD, EVEN + 1)]
        lhs.append(jnp.concatenate(parts, axis=-1))

    for n, at in enumerate((0, 1, 4)):
        total = jnp.zeros((136, 128), f32) + bias
        top = jnp.zeros((8, 128), f32) + bias
        for di in range(3):
            window = jnp.concatenate(
                [cols_ref[at + m, pl.ds(di, 136), :].astype(bf16) for m in range(3)], axis=-1
            )
            total = total + dot(window, w1s_ref[di])
            if n == 0:
                top = top + dot(window[0:8], w1s_ref[flipped[di]])
        side_ref[n, pl.ds(0, 136), :] = gelu(total)
        if n == 0:
            side_ref[n, pl.ds(0, 1), :] = gelu(top)[0:1]

    odd1_ref[0] = odd0_ref[32]
    for r, at, taps in ((-1, 0, flipped), (0, 1, (0, 1, 2)), (127, 4, (0, 1, 2))):
        pre = bias2
        for di in range(3):
            pre = pre + dot(lhs[at + di], w1_ref[taps[di]])
        hid = gelu(pre)
        shift_ref[pl.ds(8, 64), :] = hid[:, 128:]
        shift_ref[pl.ds(7, 1), :] = side_ref[0, pl.ds(r + 1, 1), :]
        line = jnp.concatenate([shift_ref[pl.ds(7, 64), :], hid[:, :128], hid[:, 128:]], axis=-1).astype(bf16)
        if r == -1:
            odd0_ref[0] = line
        elif r == 0:
            even0_ref[0] = line
        else:
            odd1_ref[32] = line

    head = lax.broadcasted_iota(jnp.int32, (16, 256), 0) == 0
    foot = lax.broadcasted_iota(jnp.int32, (16, 128), 0) == 15

    def mend(ref, p, r):
        here = pl.ds(r + 1, 1)
        new = jnp.concatenate([side_ref[0, here, :], side_ref[1, here, :]], axis=-1)
        old = ref[p, pl.ds(0, 16), pl.ds(0, 256)].astype(f32)
        ref[p, pl.ds(0, 16), pl.ds(0, 256)] = jnp.where(head, new, old).astype(bf16)
        old = ref[p, pl.ds(48, 16), pl.ds(256, 128)].astype(f32)
        ref[p, pl.ds(48, 16), pl.ds(256, 128)] = jnp.where(foot, side_ref[2, here, :], old).astype(bf16)

    def mend_step(p, carry):
        mend(even0_ref, p, 2 * p)
        mend(odd0_ref, p + 1, 2 * p + 1)
        mend(even1_ref, p, 2 * p + 64)
        mend(odd1_ref, p + 1, 2 * p + 65)
        return carry

    lax.fori_loop(0, 32, mend_step, 0, unroll=2)
    odd1_ref[0] = odd0_ref[32]

    for half, (even_ref, odd_ref) in enumerate(((even0_ref, odd0_ref), (even1_ref, odd1_ref))):

        def finish(b, carry):
            total = jnp.broadcast_to(b2_ref[...], (256, 128))
            total = total + dot(odd_ref[pl.ds(b * 4, 4)].reshape(256, 384), w2_ref[0])
            total = total + dot(even_ref[pl.ds(b * 4, 4)].reshape(256, 384), w2_ref[1])
            total = total + dot(odd_ref[pl.ds(b * 4 + 1, 4)].reshape(256, 384), w2_ref[2])
            out_ref[pl.ds(half * 32 + b * 4, 4)] = total.reshape(4, 64, 128).astype(bf16)
            return carry

        lax.fori_loop(0, 8, finish, 0)


def rim(band, blocks, *rest):
    return pl.pallas_call(
        rim_kernel,
        out_shape=[pltpu.VMEM(b.shape, b.dtype) for b in blocks] + [jax.ShapeDtypeStruct((64, 64, 128), jnp.bfloat16)],
        in_specs=[SMEM] + [VMEM] * 18,
        out_specs=[VMEM] * 5,
        scratch_shapes=[
            pltpu.VMEM((7, 144, 128), jnp.float32),
            pltpu.VMEM((7, PITCH, 128), jnp.float32),
            pltpu.VMEM((72, 128), jnp.float32),
            pltpu.VMEM((3, 136, 128), jnp.float32),
        ],
        input_output_aliases={1: 0, 2: 1, 3: 2, 4: 3},
        compiler_params=pltpu.CompilerParams(vmem_limit_bytes=16 << 20),
        name="rim",
    )(band, *map(on_chip, blocks), *rest)[4]


def shards(background, values, cells, counts, w1, b1, w2, b2):
    lat, lon = lax.axis_size("lat"), lax.axis_size("lon")
    band = lax.axis_index("lat")[None]
    east_pairs = [(i, (i + 1) % lon) for i in range(lon)]
    west_pairs = [(j, i) for i, j in east_pairs]
    down_pairs = [(i, i + 1) for i in range(lat - 1)]
    up_pairs = [(j, i) for i, j in down_pairs]
    pole_pairs = [(b * lon + i, b * lon + (i + lon // 2) % lon) for b in (0, lat - 1) for i in range(lon)]

    sent = pack(values[0], cells[0], counts[0][:, None])
    got = lax.all_to_all(sent, ("lat", "lon"), split_axis=0, concat_axis=0, tiled=True)
    field, right, left, near, rows = scatter(band, got, spread(background))

    flat = w1.reshape(3, 384, 128)
    blank = jnp.zeros((3, 128, 128), jnp.bfloat16)
    paired = jnp.concatenate(
        [jnp.concatenate([flat, blank], axis=1), jnp.concatenate([blank, flat], axis=1)], axis=2
    )
    west = lax.ppermute(right, "lon", east_pairs)
    east = lax.ppermute(left, "lon", west_pairs)
    *upper, mark = inner(0, field, paired, b1[None])
    lower_rows, upper_rows, own = frame(mark, rows, west, east)
    down = lax.ppermute(lower_rows, "lat", down_pairs)
    up = lax.ppermute(upper_rows, "lat", up_pairs)
    across = lax.ppermute(own, ("lat", "lon"), pole_pairs)
    *lower, _ = inner(64, field, paired, b1[None])
    return rim(
        band,
        (*upper, *lower),
        right,
        left,
        near,
        west,
        east,
        own,
        down,
        up,
        across,
        paired,
        flat,
        b1[None],
        w2.reshape(3, 384, 128),
        b2[None],
    )


def solution(mesh):
    placed = (
        P("lat", "lon", None),
        P(("lat", "lon"), None, None, None),
        P(("lat", "lon"), None, None),
        P(("lat", "lon"), None),
        P(),
        P(),
        P(),
        P(),
    )
    return jax.shard_map(
        shards, mesh=mesh, in_specs=placed, out_specs=P("lat", "lon", None), check_vma=False
    )
```

```python
import functools

import jax
import jax.numpy as jnp
from jax import lax
from jax.experimental import pallas as pl
from jax.experimental.pallas import tpu as pltpu
from jax.sharding import PartitionSpec as P

PITCH, ODD, EVEN = 152, 8, 80
SLABS = 131
BATCH = 8
CHUNKS = 4
GROUP = 8
META = 8
ROWS = 16
GELU_A, GELU_B = 0.7978845608028654, 0.044715
VMEM = pl.BlockSpec(memory_space=pltpu.VMEM)
SMEM = pl.BlockSpec(memory_space=pltpu.SMEM)
ANY = pl.BlockSpec(memory_space=pl.ANY)


def on_chip(x):
    return pltpu.with_memory_space_constraint(x, pltpu.VMEM)


def off_chip(x):
    return pltpu.with_memory_space_constraint(x, pltpu.HBM)


def gelu(x):
    return 0.5 * x * (1.0 + jnp.tanh(GELU_A * (x + GELU_B * (x * x * x))))


def pack_kernel(values_ref, cells_ref, counts_ref, out_ref, held_ref, where_ref, live_ref, meta_ref, sem):
    owners, slots = values_ref.shape[0], values_ref.shape[1]
    part = owners // CHUNKS
    numbers = pltpu.make_async_copy(cells_ref, where_ref, sem.at[2 * CHUNKS])
    numbers.start()
    totals = pltpu.make_async_copy(counts_ref, live_ref, sem.at[2 * CHUNKS + 1])
    totals.start()
    arrive, leave = [], []
    for n in range(CHUNKS):
        here = pl.ds(n * part, part)
        arrive.append(
            pltpu.make_async_copy(values_ref.at[here], held_ref.at[here, pl.ds(0, slots), :], sem.at[n])
        )
        leave.append(pltpu.make_async_copy(held_ref.at[here], out_ref.at[here], sem.at[CHUNKS + n]))
        arrive[-1].start()
    numbers.wait()
    totals.wait()
    cells = where_ref[...]
    across = jnp.broadcast_to(live_ref[...], (owners, owners))
    down = lax.broadcasted_iota(jnp.int32, (owners, owners), 0)
    lane = lax.broadcasted_iota(jnp.int32, (owners, owners), 1)
    counts = jnp.sum(jnp.where(down == lane, across, 0).astype(jnp.float32), axis=1, keepdims=True)
    place = lax.broadcasted_iota(jnp.int32, cells.shape, 1)
    live = place.astype(jnp.float32) < counts
    row = cells >> 7
    col = cells & 127
    high = jnp.where(live, row + 2, 0).astype(jnp.float32)
    low = jnp.where(live, (col >> 1) + jnp.where((col & 1) == 1, ODD, EVEN), 0).astype(jnp.float32)
    blank = jnp.zeros((owners, 128 - slots), jnp.int32)
    marked = jnp.concatenate([jnp.where(live, cells, -1), blank - 1], axis=1)
    again = jnp.zeros(marked.shape, jnp.float32)
    for back in range(1, BATCH):
        same = (pltpu.roll(marked, back, 1) == marked) & (marked >= 0) & (lane % BATCH >= back)
        again = jnp.where(same, 1.0, again)
    blank = blank.astype(jnp.float32)
    meta_ref[pl.ds(0, owners, stride=META), :] = jnp.concatenate([high, blank], axis=1)
    meta_ref[pl.ds(1, owners, stride=META), :] = jnp.concatenate([low, blank], axis=1)
    meta_ref[pl.ds(2, owners, stride=META), :] = again
    for m in range(3, META):
        meta_ref[pl.ds(m, owners, stride=META), :] = jnp.zeros((owners, 128), jnp.float32)
    held_ref[:, pl.ds(slots, META), :] = meta_ref[...].reshape(owners, META, 128).astype(jnp.bfloat16)
    for came, goes in zip(arrive, leave):
        came.wait()
        goes.start()
    for goes in leave:
        goes.wait()


def pack(values, cells, counts):
    owners, slots, chans = values.shape
    return pl.pallas_call(
        pack_kernel,
        out_shape=pltpu.HBM((owners, slots + META, chans), jnp.bfloat16),
        in_specs=[ANY] * 3,
        out_specs=ANY,
        scratch_shapes=[
            pltpu.VMEM((owners, slots + META, chans), jnp.bfloat16),
            pltpu.VMEM((owners, slots), jnp.int32),
            pltpu.VMEM((1, owners), jnp.int32),
            pltpu.VMEM((owners * META, chans), jnp.float32),
            pltpu.SemaphoreType.DMA((2 * CHUNKS + 2,)),
        ],
        compiler_params=pltpu.CompilerParams(vmem_limit_bytes=12 << 20),
        name="pack",
    )(off_chip(values), off_chip(cells), off_chip(counts))


def spread_kernel(field_ref, acc_ref, wide_ref):
    def step(r, carry):
        wide_ref[...] = field_ref[r].astype(jnp.float32)
        base = pl.multiple_of((r + 2) * PITCH, 8)
        acc_ref[pl.ds(base + ODD, 64), :] = wide_ref[pl.ds(1, 64, stride=2), :]
        acc_ref[pl.ds(base + EVEN, 64), :] = wide_ref[pl.ds(0, 64, stride=2), :]
        for at in (0, EVEN - 8, EVEN + 64):
            acc_ref[pl.ds(base + at, 8), :] = jnp.zeros((8, 128), jnp.float32)
        return carry

    lax.fori_loop(0, field_ref.shape[0], step, 0)


def spread(field):
    return pl.pallas_call(
        spread_kernel,
        out_shape=pltpu.HBM((SLABS * PITCH, 128), jnp.float32),
        in_specs=[VMEM],
        out_specs=VMEM,
        scratch_shapes=[pltpu.VMEM((128, 128), jnp.float32)],
        compiler_params=pltpu.CompilerParams(vmem_limit_bytes=12 << 20),
        name="spread",
    )(field)


def scatter_kernel(band_ref, got_ref, start_ref, acc_ref, right_ref, left_ref, near_ref, rows_ref, *rest):
    other_ref, wide_ref, meta_ref, index_ref, late_ref, cells0_ref, cells1_ref, list_ref, sem = rest
    del band_ref
    sources, slots = got_ref.shape[0], got_ref.shape[1] - META
    first = pltpu.make_async_copy(start_ref, acc_ref, sem.at[0])
    first.start()

    def unpack(s, carry):
        meta_ref[pl.ds(pl.multiple_of(s * META, META), META), :] = got_ref[s, pl.ds(slots, META), :].astype(jnp.float32)
        return carry

    lax.fori_loop(0, sources, unpack, 0, unroll=8)
    high = meta_ref[pl.ds(0, sources, stride=META), :]
    low = meta_ref[pl.ds(1, sources, stride=META), :]
    again = meta_ref[pl.ds(2, sources, stride=META), :]
    spot = high * PITCH + low
    index_ref[...] = jnp.where(again > 0, 0.0, spot).astype(jnp.int32)
    lane = lax.broadcasted_iota(jnp.int32, again.shape, 1)
    inside = lane < slots
    count = jnp.sum(jnp.where(inside, again, 0.0), axis=1, keepdims=True)
    furthest = jnp.max(jnp.where(inside & (again > 0), lane, 0).astype(jnp.float32), axis=1, keepdims=True)
    notes = jnp.where(lane == slots, count, furthest)
    late = jnp.where(inside, again * spot, notes)
    late_ref[...] = late.astype(jnp.int32)

    cells = (cells0_ref, cells1_ref)

    def fetch(group, half):
        return pltpu.make_async_copy(index_ref.at[pl.ds(group * GROUP, GROUP), :], cells[half], sem.at[1 + half])

    fetch(0, 0).start()
    fetch(1, 1).start()
    listed = pltpu.make_async_copy(late_ref, list_ref, sem.at[3])
    listed.start()

    def clear(r, carry):
        other_ref[pl.ds(pl.multiple_of((r + 2) * PITCH, 8), PITCH), :] = jnp.zeros((PITCH, 128), jnp.float32)
        return carry

    lax.fori_loop(0, 128, clear, 0)
    first.wait()
    accs = (acc_ref, other_ref)

    def add(step, carry):
        for half in range(2):
            group = step * 2 + half
            fetch(group, half).wait()
            for t in range(GROUP):
                wide = wide_ref.at[t % 2]
                wide[...] = got_ref[group * GROUP + t, pl.ds(0, slots), :].astype(jnp.float32)
                for n, k in enumerate(range(0, slots, BATCH)):
                    acc = accs[n % 2]
                    where = [cells[half][t, k + m] for m in range(BATCH)]
                    sums = [acc[pl.ds(i, 1), :] + wide[pl.ds(k + m, 1), :] for m, i in enumerate(where)]
                    for i, total in zip(where, sums):
                        acc[pl.ds(i, 1), :] = total

            @pl.when(group + 2 < sources // GROUP)
            def _():
                fetch(group + 2, half).start()

        return carry

    lax.fori_loop(0, sources // (2 * GROUP), add, 0)
    listed.wait()

    def rest_of(s, carry):
        repeats = list_ref[s, slots]
        furthest = list_ref[s, slots + 1]

        @pl.when(repeats > 0)
        def _():
            wide_ref[0] = got_ref[s, pl.ds(0, slots), :].astype(jnp.float32)

            def one(k, carry):
                i = list_ref[s, k]

                @pl.when(i > 0)
                def _():
                    acc_ref[pl.ds(i, 1), :] = acc_ref[pl.ds(i, 1), :] + wide_ref[0, pl.ds(k, 1), :]

                return carry

            lax.fori_loop(jnp.where(repeats > 1, 0, furthest), furthest + 1, one, 0)

        return carry

    lax.fori_loop(0, sources, rest_of, 0)

    def merge(r, carry):
        here = pl.ds(pl.multiple_of((r + 2) * PITCH, 8), PITCH)
        acc_ref[here, :] = acc_ref[here, :] + other_ref[here, :]
        return carry

    lax.fori_loop(0, 128, merge, 0)
    bf16 = jnp.bfloat16
    ends = (0, 1, 126, 127)
    for n, at in enumerate((EVEN + 63, ODD + 63)):
        right_ref[pl.ds(n * 128, 128), :] = acc_ref[pl.ds(2 * PITCH + at, 128, stride=PITCH), :].astype(bf16)
    left_ref[pl.ds(0, 128), :] = acc_ref[pl.ds(2 * PITCH + EVEN, 128, stride=PITCH), :].astype(bf16)
    near_ref[...] = acc_ref[pl.ds(2 * PITCH + ODD, 128, stride=PITCH), :].astype(bf16)
    east = [acc_ref[pl.ds((r + 2) * PITCH + at, 1), :] for r in ends for at in (EVEN + 63, ODD + 63)]
    west = [acc_ref[pl.ds((r + 2) * PITCH + EVEN, 1), :] for r in ends]
    right_ref[pl.ds(256, 8), :] = jnp.concatenate(east, axis=0).astype(bf16)
    left_ref[pl.ds(128, 8), :] = jnp.concatenate(west + west, axis=0).astype(bf16)
    for n, r in enumerate(ends):
        base = (r + 2) * PITCH
        rows_ref[n, pl.ds(0, 64), :] = acc_ref[pl.ds(base + ODD, 64), :].astype(bf16)
        rows_ref[n, pl.ds(64, 64), :] = acc_ref[pl.ds(base + EVEN, 64), :].astype(bf16)


def scatter(band, got, start):
    return pl.pallas_call(
        scatter_kernel,
        out_shape=[
            pltpu.VMEM(start.shape, jnp.float32),
            jax.ShapeDtypeStruct((264, 128), jnp.bfloat16),
            jax.ShapeDtypeStruct((136, 128), jnp.bfloat16),
            jax.ShapeDtypeStruct((128, 128), jnp.bfloat16),
            jax.ShapeDtypeStruct((4, 128, 128), jnp.bfloat16),
        ],
        in_specs=[SMEM, VMEM, ANY],
        out_specs=[VMEM] * 5,
        scratch_shapes=[
            pltpu.VMEM((130 * PITCH, 128), jnp.float32),
            pltpu.VMEM((2, 96, 128), jnp.float32),
            pltpu.VMEM((128 * META, 128), jnp.float32),
            pltpu.VMEM((128, 128), jnp.int32),
            pltpu.VMEM((128, 128), jnp.int32),
            pltpu.SMEM((GROUP, 128), jnp.int32),
            pltpu.SMEM((GROUP, 128), jnp.int32),
            pltpu.SMEM((128, 128), jnp.int32),
            pltpu.SemaphoreType.DMA((4,)),
        ],
        compiler_params=pltpu.CompilerParams(vmem_limit_bytes=24 << 20),
        name="scatter",
    )(band, on_chip(got), off_chip(start))


def frame_kernel(after_ref, rows_ref, west_ref, east_ref, down_ref, up_ref, all_ref):
    del after_ref
    f32, bf16 = jnp.float32, jnp.bfloat16
    west = west_ref[pl.ds(256, 8), :].astype(f32)
    east = east_ref[pl.ds(128, 8), :].astype(f32)
    for n in range(4):
        tail = jnp.concatenate([west[2 * n : 2 * n + 2], east[n : n + 1], jnp.zeros((5, 128), f32)], axis=0)
        for ref, at in ((all_ref, n), (up_ref, n) if n < 2 else (down_ref, n - 2)):
            ref[at, pl.ds(0, 128), :] = rows_ref[n]
            ref[at, pl.ds(128, 8), :] = tail.astype(bf16)


def frame(after, rows, west, east):
    return pl.pallas_call(
        frame_kernel,
        out_shape=[
            jax.ShapeDtypeStruct((2, 136, 128), jnp.bfloat16),
            jax.ShapeDtypeStruct((2, 136, 128), jnp.bfloat16),
            jax.ShapeDtypeStruct((4, 136, 128), jnp.bfloat16),
        ],
        in_specs=[ANY] + [VMEM] * 3,
        out_specs=[VMEM] * 3,
        compiler_params=pltpu.CompilerParams(vmem_limit_bytes=4 << 20),
        name="frame",
    )(after, rows, west, east)


def inner_kernel(low, field_ref, w1_ref, b1_ref, even_ref, odd_ref, mark_ref, lhs_ref, shift_ref):
    f32, bf16 = jnp.float32, jnp.bfloat16
    bias = jnp.concatenate([b1_ref[...], b1_ref[...]], axis=-1)
    weight = w1_ref[...].reshape(1536, 256)

    def step(b, carry):
        for n in range(ROWS + 2):
            base = pl.multiple_of((low + 1 + b * ROWS + n) * PITCH, 8)
            parts = [field_ref[pl.ds(base + at, 64), :].astype(bf16) for at in (ODD - 1, EVEN, ODD, EVEN + 1)]
            lhs_ref[n] = jnp.concatenate(parts, axis=-1)
        window = jnp.concatenate([lhs_ref[pl.ds(di, ROWS)].reshape(ROWS * 64, 512) for di in range(3)], axis=-1)
        hid = gelu(jnp.dot(window, weight, preferred_element_type=f32) + bias).reshape(ROWS, 64, 256)
        shift_ref[:, pl.ds(8, 64), :] = hid[:, :, 128:]
        wide = jnp.concatenate([shift_ref[:, pl.ds(7, 64), :], hid[:, :, :128], hid[:, :, 128:]], axis=-1)
        wide = wide.astype(bf16).reshape(ROWS // 2, 2, 64, 384)
        even_ref[pl.ds(b * (ROWS // 2), ROWS // 2)] = wide[:, 0]
        odd_ref[pl.ds(b * (ROWS // 2) + 1, ROWS // 2)] = wide[:, 1]
        return carry

    lax.fori_loop(0, 64 // ROWS, step, 0)
    mark_ref[...] = jnp.zeros(mark_ref.shape, mark_ref.dtype)


def inner(low, field, w1, b1):
    return pl.pallas_call(
        functools.partial(inner_kernel, low),
        out_shape=[
            pltpu.VMEM((32, 64, 384), jnp.bfloat16),
            pltpu.VMEM((33, 64, 384), jnp.bfloat16),
            jax.ShapeDtypeStruct((8, 128), jnp.float32),
        ],
        in_specs=[VMEM] * 3,
        out_specs=[VMEM] * 3,
        scratch_shapes=[pltpu.VMEM((ROWS + 2, 64, 512), jnp.bfloat16), pltpu.VMEM((ROWS, 72, 128), jnp.float32)],
        compiler_params=pltpu.CompilerParams(vmem_limit_bytes=24 << 20),
        name="inner",
    )(on_chip(field), w1, b1)


def rim_kernel(
    band_ref,
    even0_in,
    odd0_in,
    even1_in,
    odd1_in,
    right_ref,
    left_ref,
    near_ref,
    west_ref,
    east_ref,
    own_ref,
    down_ref,
    up_ref,
    across_ref,
    w1_ref,
    w1s_ref,
    b1_ref,
    w2_ref,
    b2_ref,
    even0_ref,
    odd0_ref,
    even1_ref,
    odd1_ref,
    out_ref,
    cols_ref,
    strip_ref,
    shift_ref,
    side_ref,
):
    del even0_in, odd0_in, even1_in, odd1_in
    f32, bf16 = jnp.float32, jnp.bfloat16
    band = band_ref[0]
    north, south = band == 0, band == 3
    first = jnp.where(north, 2, 0)
    flipped = (first, 1, 2 - first)
    dot = functools.partial(jnp.dot, preferred_element_type=f32)
    bias = b1_ref[...]
    bias2 = jnp.concatenate([bias, bias], axis=-1)

    body = (
        west_ref[pl.ds(0, 128), :],
        west_ref[pl.ds(128, 128), :],
        left_ref[pl.ds(0, 128), :],
        near_ref[...],
        right_ref[pl.ds(0, 128), :],
        right_ref[pl.ds(128, 128), :],
        east_ref[pl.ds(0, 128), :],
    )
    for n, col in enumerate(body):
        cols_ref[n, pl.ds(2, 128), :] = col.astype(f32)

    def wide(ref, n):
        return ref[n].astype(f32)

    rows = (
        jnp.where(north, wide(across_ref, 1), wide(down_ref, 0)),
        jnp.where(north, wide(across_ref, 0), wide(down_ref, 1)),
        wide(own_ref, 0),
        wide(own_ref, 1),
        wide(own_ref, 2),
        wide(own_ref, 3),
        jnp.where(south, wide(across_ref, 3), wide(up_ref, 0)),
    )
    where = (128, 129, 64, 0, 127, 63, 130)
    lhs = []
    for n, row in enumerate(rows):
        strip_ref[n, pl.ds(ODD, 64), :] = row[0:64]
        strip_ref[n, pl.ds(EVEN, 64), :] = row[64:128]
        strip_ref[n, pl.ds(ODD - 1, 1), :] = row[129:130]
        strip_ref[n, pl.ds(EVEN + 64, 1), :] = row[130:131]
        if n in (0, 1, 6):
            slab = 130 if n == 6 else n
            for m, at in enumerate(where):
                cols_ref[m, pl.ds(slab, 1), :] = row[at : at + 1]
        parts = [strip_ref[n, pl.ds(at, 64), :].astype(bf16) for at in (ODD - 1, EVEN, ODD, EVEN + 1)]
        lhs.append(jnp.concatenate(parts, axis=-1))

    for n, at in enumerate((0, 1, 4)):
        total = jnp.zeros((136, 128), f32) + bias
        top = jnp.zeros((8, 128), f32) + bias
        for di in range(3):
            window = jnp.concatenate(
                [cols_ref[at + m, pl.ds(di, 136), :].astype(bf16) for m in range(3)], axis=-1
            )
            total = total + dot(window, w1s_ref[di])
            if n == 0:
                top = top + dot(window[0:8], w1s_ref[flipped[di]])
        side_ref[n, pl.ds(0, 136), :] = gelu(total)
        if n == 0:
            side_ref[n, pl.ds(0, 1), :] = gelu(top)[0:1]

    odd1_ref[0] = odd0_ref[32]
    for r, at, taps in ((-1, 0, flipped), (0, 1, (0, 1, 2)), (127, 4, (0, 1, 2))):
        pre = bias2
        for di in range(3):
            pre = pre + dot(lhs[at + di], w1_ref[taps[di]])
        hid = gelu(pre)
        shift_ref[pl.ds(8, 64), :] = hid[:, 128:]
        shift_ref[pl.ds(7, 1), :] = side_ref[0, pl.ds(r + 1, 1), :]
        line = jnp.concatenate([shift_ref[pl.ds(7, 64), :], hid[:, :128], hid[:, 128:]], axis=-1).astype(bf16)
        if r == -1:
            odd0_ref[0] = line
        elif r == 0:
            even0_ref[0] = line
        else:
            odd1_ref[32] = line

    head = lax.broadcasted_iota(jnp.int32, (16, 256), 0) == 0
    foot = lax.broadcasted_iota(jnp.int32, (16, 128), 0) == 15

    def mend(ref, p, r):
        here = pl.ds(r + 1, 1)
        new = jnp.concatenate([side_ref[0, here, :], side_ref[1, here, :]], axis=-1)
        old = ref[p, pl.ds(0, 16), pl.ds(0, 256)].astype(f32)
        ref[p, pl.ds(0, 16), pl.ds(0, 256)] = jnp.where(head, new, old).astype(bf16)
        old = ref[p, pl.ds(48, 16), pl.ds(256, 128)].astype(f32)
        ref[p, pl.ds(48, 16), pl.ds(256, 128)] = jnp.where(foot, side_ref[2, here, :], old).astype(bf16)

    def mend_step(p, carry):
        mend(even0_ref, p, 2 * p)
        mend(odd0_ref, p + 1, 2 * p + 1)
        mend(even1_ref, p, 2 * p + 64)
        mend(odd1_ref, p + 1, 2 * p + 65)
        return carry

    lax.fori_loop(0, 32, mend_step, 0, unroll=2)
    odd1_ref[0] = odd0_ref[32]

    for half, (even_ref, odd_ref) in enumerate(((even0_ref, odd0_ref), (even1_ref, odd1_ref))):

        def finish(b, carry):
            total = jnp.broadcast_to(b2_ref[...], (256, 128))
            total = total + dot(odd_ref[pl.ds(b * 4, 4)].reshape(256, 384), w2_ref[0])
            total = total + dot(even_ref[pl.ds(b * 4, 4)].reshape(256, 384), w2_ref[1])
            total = total + dot(odd_ref[pl.ds(b * 4 + 1, 4)].reshape(256, 384), w2_ref[2])
            out_ref[pl.ds(half * 32 + b * 4, 4)] = total.reshape(4, 64, 128).astype(bf16)
            return carry

        lax.fori_loop(0, 8, finish, 0)


def rim(band, blocks, *rest):
    return pl.pallas_call(
        rim_kernel,
        out_shape=[pltpu.VMEM(b.shape, b.dtype) for b in blocks] + [jax.ShapeDtypeStruct((64, 64, 128), jnp.bfloat16)],
        in_specs=[SMEM] + [VMEM] * 18,
        out_specs=[VMEM] * 5,
        scratch_shapes=[
            pltpu.VMEM((7, 144, 128), jnp.float32),
            pltpu.VMEM((7, PITCH, 128), jnp.float32),
            pltpu.VMEM((72, 128), jnp.float32),
            pltpu.VMEM((3, 136, 128), jnp.float32),
        ],
        input_output_aliases={1: 0, 2: 1, 3: 2, 4: 3},
        compiler_params=pltpu.CompilerParams(vmem_limit_bytes=16 << 20),
        name="rim",
    )(band, *map(on_chip, blocks), *rest)[4]


def shards(background, values, cells, counts, w1, b1, w2, b2):
    lat, lon = lax.axis_size("lat"), lax.axis_size("lon")
    band = lax.axis_index("lat")[None]
    east_pairs = [(i, (i + 1) % lon) for i in range(lon)]
    west_pairs = [(j, i) for i, j in east_pairs]
    down_pairs = [(i, i + 1) for i in range(lat - 1)]
    up_pairs = [(j, i) for i, j in down_pairs]
    pole_pairs = [(b * lon + i, b * lon + (i + lon // 2) % lon) for b in (0, lat - 1) for i in range(lon)]

    sent = pack(values[0], cells[0], counts)
    got = lax.all_to_all(sent, ("lat", "lon"), split_axis=0, concat_axis=0, tiled=True)
    field, right, left, near, rows = scatter(band, got, spread(background))

    flat = w1.reshape(3, 384, 128)
    blank = jnp.zeros((3, 128, 128), jnp.bfloat16)
    paired = jnp.concatenate(
        [jnp.concatenate([flat, blank], axis=1), jnp.concatenate([blank, flat], axis=1)], axis=2
    )
    west = lax.ppermute(right, "lon", east_pairs)
    east = lax.ppermute(left, "lon", west_pairs)
    *upper, mark = inner(0, field, paired, b1[None])
    lower_rows, upper_rows, own = frame(mark, rows, west, east)
    down = lax.ppermute(lower_rows, "lat", down_pairs)
    up = lax.ppermute(upper_rows, "lat", up_pairs)
    across = lax.ppermute(own, ("lat", "lon"), pole_pairs)
    *lower, _ = inner(64, field, paired, b1[None])
    return rim(
        band,
        (*upper, *lower),
        right,
        left,
        near,
        west,
        east,
        own,
        down,
        up,
        across,
        paired,
        flat,
        b1[None],
        w2.reshape(3, 384, 128),
        b2[None],
    )


def solution(mesh):
    placed = (
        P("lat", "lon", None),
        P(("lat", "lon"), None, None, None),
        P(("lat", "lon"), None, None),
        P(("lat", "lon"), None),
        P(),
        P(),
        P(),
        P(),
    )
    return jax.shard_map(
        shards, mesh=mesh, in_specs=placed, out_specs=P("lat", "lon", None), check_vma=False
    )
```

```python
import functools

import jax
import jax.numpy as jnp
from jax import lax
from jax.experimental import pallas as pl
from jax.experimental.pallas import tpu as pltpu
from jax.sharding import PartitionSpec as P

PITCH, ODD, EVEN = 152, 8, 80
SLABS = 131
BATCH = 8
CHUNKS = 4
GROUP = 8
META = 8
ROWS = 16
GELU_A, GELU_B = 0.7978845608028654, 0.044715
VMEM = pl.BlockSpec(memory_space=pltpu.VMEM)
SMEM = pl.BlockSpec(memory_space=pltpu.SMEM)
ANY = pl.BlockSpec(memory_space=pl.ANY)


def on_chip(x):
    return pltpu.with_memory_space_constraint(x, pltpu.VMEM)


def off_chip(x):
    return pltpu.with_memory_space_constraint(x, pltpu.HBM)


def gelu(x):
    return 0.5 * x * (1.0 + jnp.tanh(GELU_A * (x + GELU_B * (x * x * x))))


def pack_kernel(values_ref, cells_ref, counts_ref, out_ref, held_ref, where_ref, live_ref, meta_ref, sem):
    owners, slots = values_ref.shape[0], values_ref.shape[1]
    part = owners // CHUNKS
    numbers = pltpu.make_async_copy(cells_ref, where_ref, sem.at[2 * CHUNKS])
    numbers.start()
    totals = pltpu.make_async_copy(counts_ref, live_ref, sem.at[2 * CHUNKS + 1])
    totals.start()
    arrive, leave = [], []
    for n in range(CHUNKS):
        here = pl.ds(n * part, part)
        arrive.append(
            pltpu.make_async_copy(values_ref.at[here], held_ref.at[here, pl.ds(0, slots), :], sem.at[n])
        )
        leave.append(pltpu.make_async_copy(held_ref.at[here], out_ref.at[here], sem.at[CHUNKS + n]))
        arrive[-1].start()
    numbers.wait()
    totals.wait()
    cells = where_ref[...]
    place = lax.broadcasted_iota(jnp.int32, cells.shape, 0)
    live = place < live_ref[...]
    row = cells >> 7
    col = cells & 127
    high = jnp.where(live, row + 2, 0)
    low = jnp.where(live, (col >> 1) + jnp.where((col & 1) == 1, ODD, EVEN), 0)
    marked = jnp.where(live, cells, -1)
    again = jnp.zeros(cells.shape, jnp.int32)
    for back in range(1, BATCH):
        same = (pltpu.roll(marked, back, 0) == marked) & live & (place % BATCH >= back)
        again = jnp.where(same, 1, again)
    blank = jnp.zeros((128 - slots, owners), jnp.float32)

    def turned(x):
        return jnp.concatenate([x.astype(jnp.float32), blank], axis=0).T

    meta_ref[pl.ds(0, owners, stride=META), :] = turned(high)
    meta_ref[pl.ds(1, owners, stride=META), :] = turned(low)
    meta_ref[pl.ds(2, owners, stride=META), :] = turned(again)
    for m in range(3, META):
        meta_ref[pl.ds(m, owners, stride=META), :] = jnp.zeros((owners, 128), jnp.float32)
    held_ref[:, pl.ds(slots, META), :] = meta_ref[...].reshape(owners, META, 128).astype(jnp.bfloat16)
    for came, goes in zip(arrive, leave):
        came.wait()
        goes.start()
    for goes in leave:
        goes.wait()


def pack(values, cells, counts):
    owners, slots, chans = values.shape
    return pl.pallas_call(
        pack_kernel,
        out_shape=pltpu.HBM((owners, slots + META, chans), jnp.bfloat16),
        in_specs=[ANY] * 3,
        out_specs=ANY,
        scratch_shapes=[
            pltpu.VMEM((owners, slots + META, chans), jnp.bfloat16),
            pltpu.VMEM((slots, owners), jnp.int32),
            pltpu.VMEM((1, owners), jnp.int32),
            pltpu.VMEM((owners * META, chans), jnp.float32),
            pltpu.SemaphoreType.DMA((2 * CHUNKS + 2,)),
        ],
        compiler_params=pltpu.CompilerParams(vmem_limit_bytes=12 << 20),
        name="pack",
    )(off_chip(values), off_chip(cells), off_chip(counts))


def spread_kernel(field_ref, parted_ref, wide_ref):
    def step(r, carry):
        wide_ref[...] = field_ref[r].astype(jnp.float32)
        parted_ref[r, pl.ds(0, 64), :] = wide_ref[pl.ds(1, 64, stride=2), :].astype(jnp.bfloat16)
        parted_ref[r, pl.ds(64, 64), :] = wide_ref[pl.ds(0, 64, stride=2), :].astype(jnp.bfloat16)
        return carry

    lax.fori_loop(0, field_ref.shape[0], step, 0)


def spread(field):
    return pl.pallas_call(
        spread_kernel,
        out_shape=pltpu.HBM(field.shape, field.dtype),
        in_specs=[VMEM],
        out_specs=VMEM,
        scratch_shapes=[pltpu.VMEM((128, 128), jnp.float32)],
        compiler_params=pltpu.CompilerParams(vmem_limit_bytes=12 << 20),
        name="spread",
    )(field)


def scatter_kernel(band_ref, got_ref, parted_ref, acc_ref, right_ref, left_ref, near_ref, rows_ref, *rest):
    other_ref, start_ref, wide_ref, meta_ref, index_ref, late_ref, cells0_ref, cells1_ref, list_ref, sem = rest
    del band_ref
    sources, slots = got_ref.shape[0], got_ref.shape[1] - META
    part = 128 // CHUNKS
    pieces = []
    for n in range(CHUNKS):
        here = pl.ds(n * part, part)
        pieces.append(pltpu.make_async_copy(parted_ref.at[here], start_ref.at[here], sem.at[3 + n]))
        pieces[-1].start()

    def unpack(s, carry):
        meta_ref[pl.ds(pl.multiple_of(s * META, META), META), :] = got_ref[s, pl.ds(slots, META), :].astype(jnp.float32)
        return carry

    lax.fori_loop(0, sources, unpack, 0, unroll=8)
    high = meta_ref[pl.ds(0, sources, stride=META), :]
    low = meta_ref[pl.ds(1, sources, stride=META), :]
    again = meta_ref[pl.ds(2, sources, stride=META), :]
    spot = high * PITCH + low
    index_ref[...] = jnp.where(again > 0, 0.0, spot).astype(jnp.int32)
    lane = lax.broadcasted_iota(jnp.int32, again.shape, 1)
    inside = lane < slots
    count = jnp.sum(jnp.where(inside, again, 0.0), axis=1, keepdims=True)
    furthest = jnp.max(jnp.where(inside & (again > 0), lane, 0).astype(jnp.float32), axis=1, keepdims=True)
    crowd = jnp.sum(count.reshape(sources // GROUP, GROUP, 1), axis=1, keepdims=True)
    crowd = jnp.broadcast_to(crowd, (sources // GROUP, GROUP, 128)).reshape(sources, 128)
    notes = jnp.where(lane == slots, count, jnp.where(lane == slots + 1, furthest, crowd))
    late = jnp.where(inside, again * spot, notes)
    late_ref[...] = late.astype(jnp.int32)

    cells = (cells0_ref, cells1_ref)

    def fetch(group, half):
        return pltpu.make_async_copy(index_ref.at[pl.ds(group * GROUP, GROUP), :], cells[half], sem.at[half])

    fetch(0, 0).start()
    fetch(1, 1).start()
    listed = pltpu.make_async_copy(late_ref, list_ref, sem.at[2])
    listed.start()

    def clear(r, carry):
        base = pl.multiple_of((r + 2) * PITCH, 8)
        for at in (ODD, EVEN):
            other_ref[pl.ds(base + at, 64), :] = jnp.zeros((64, 128), jnp.float32)
        return carry

    lax.fori_loop(0, 128, clear, 0)

    def widen(r, carry):
        base = pl.multiple_of((r + 2) * PITCH, 8)
        for at in (0, EVEN - 8, EVEN + 64):
            acc_ref[pl.ds(base + at, 8), :] = jnp.zeros((8, 128), jnp.float32)
        acc_ref[pl.ds(base + ODD, 64), :] = start_ref[r, pl.ds(0, 64), :].astype(jnp.float32)
        acc_ref[pl.ds(base + EVEN, 64), :] = start_ref[r, pl.ds(64, 64), :].astype(jnp.float32)
        return carry

    for n, piece in enumerate(pieces):
        piece.wait()
        lax.fori_loop(n * part, (n + 1) * part, widen, 0)
    accs = (acc_ref, other_ref)

    def add(step, carry):
        for half in range(2):
            group = step * 2 + half
            fetch(group, half).wait()
            for t in range(GROUP):
                wide = wide_ref.at[t % 2]
                wide[...] = got_ref[group * GROUP + t, pl.ds(0, slots), :].astype(jnp.float32)
                for n, k in enumerate(range(0, slots, BATCH)):
                    acc = accs[n % 2]
                    where = [cells[half][t, k + m] for m in range(BATCH)]
                    sums = [acc[pl.ds(i, 1), :] + wide[pl.ds(k + m, 1), :] for m, i in enumerate(where)]
                    for i, total in zip(where, sums):
                        acc[pl.ds(i, 1), :] = total

            @pl.when(group + 2 < sources // GROUP)
            def _():
                fetch(group + 2, half).start()

        return carry

    lax.fori_loop(0, sources // (2 * GROUP), add, 0)
    listed.wait()

    def rest_of(s, carry):
        repeats = list_ref[s, slots]
        furthest = list_ref[s, slots + 1]

        @pl.when(repeats > 0)
        def _():
            wide_ref[0] = got_ref[s, pl.ds(0, slots), :].astype(jnp.float32)

            def one(k, carry):
                i = list_ref[s, k]

                @pl.when(i > 0)
                def _():
                    acc_ref[pl.ds(i, 1), :] = acc_ref[pl.ds(i, 1), :] + wide_ref[0, pl.ds(k, 1), :]

                return carry

            lax.fori_loop(jnp.where(repeats > 1, 0, furthest), furthest + 1, one, 0)

        return carry

    for group in range(sources // GROUP):

        @pl.when(list_ref[group * GROUP, slots + 2] > 0)
        def _():
            lax.fori_loop(group * GROUP, (group + 1) * GROUP, rest_of, 0)


    def merge(r, carry):
        base = pl.multiple_of((r + 2) * PITCH, 8)
        for at in (ODD, EVEN):
            here = pl.ds(base + at, 64)
            acc_ref[here, :] = acc_ref[here, :] + other_ref[here, :]
        return carry

    lax.fori_loop(0, 128, merge, 0)
    bf16 = jnp.bfloat16
    ends = (0, 1, 126, 127)
    for n, at in enumerate((EVEN + 63, ODD + 63)):
        right_ref[pl.ds(n * 128, 128), :] = acc_ref[pl.ds(2 * PITCH + at, 128, stride=PITCH), :].astype(bf16)
    left_ref[pl.ds(0, 128), :] = acc_ref[pl.ds(2 * PITCH + EVEN, 128, stride=PITCH), :].astype(bf16)
    near_ref[...] = acc_ref[pl.ds(2 * PITCH + ODD, 128, stride=PITCH), :].astype(bf16)
    east = [acc_ref[pl.ds((r + 2) * PITCH + at, 1), :] for r in ends for at in (EVEN + 63, ODD + 63)]
    west = [acc_ref[pl.ds((r + 2) * PITCH + EVEN, 1), :] for r in ends]
    right_ref[pl.ds(256, 8), :] = jnp.concatenate(east, axis=0).astype(bf16)
    left_ref[pl.ds(128, 8), :] = jnp.concatenate(west + west, axis=0).astype(bf16)
    for n, r in enumerate(ends):
        base = (r + 2) * PITCH
        rows_ref[n, pl.ds(0, 64), :] = acc_ref[pl.ds(base + ODD, 64), :].astype(bf16)
        rows_ref[n, pl.ds(64, 64), :] = acc_ref[pl.ds(base + EVEN, 64), :].astype(bf16)


def scatter(band, got, start):
    return pl.pallas_call(
        scatter_kernel,
        out_shape=[
            pltpu.VMEM((SLABS * PITCH, 128), jnp.float32),
            jax.ShapeDtypeStruct((264, 128), jnp.bfloat16),
            jax.ShapeDtypeStruct((136, 128), jnp.bfloat16),
            jax.ShapeDtypeStruct((128, 128), jnp.bfloat16),
            jax.ShapeDtypeStruct((4, 128, 128), jnp.bfloat16),
        ],
        in_specs=[SMEM, VMEM, ANY],
        out_specs=[VMEM] * 5,
        scratch_shapes=[
            pltpu.VMEM((130 * PITCH, 128), jnp.float32),
            pltpu.VMEM((128, 128, 128), jnp.bfloat16),
            pltpu.VMEM((2, 96, 128), jnp.float32),
            pltpu.VMEM((128 * META, 128), jnp.float32),
            pltpu.VMEM((128, 128), jnp.int32),
            pltpu.VMEM((128, 128), jnp.int32),
            pltpu.SMEM((GROUP, 128), jnp.int32),
            pltpu.SMEM((GROUP, 128), jnp.int32),
            pltpu.SMEM((128, 128), jnp.int32),
            pltpu.SemaphoreType.DMA((3 + CHUNKS,)),
        ],
        compiler_params=pltpu.CompilerParams(vmem_limit_bytes=24 << 20),
        name="scatter",
    )(band, on_chip(got), off_chip(start))


def frame_kernel(after_ref, rows_ref, west_ref, east_ref, down_ref, up_ref, all_ref):
    del after_ref
    f32, bf16 = jnp.float32, jnp.bfloat16
    west = west_ref[pl.ds(256, 8), :].astype(f32)
    east = east_ref[pl.ds(128, 8), :].astype(f32)
    for n in range(4):
        tail = jnp.concatenate([west[2 * n : 2 * n + 2], east[n : n + 1], jnp.zeros((5, 128), f32)], axis=0)
        for ref, at in ((all_ref, n), (up_ref, n) if n < 2 else (down_ref, n - 2)):
            ref[at, pl.ds(0, 128), :] = rows_ref[n]
            ref[at, pl.ds(128, 8), :] = tail.astype(bf16)


def frame(after, rows, west, east):
    return pl.pallas_call(
        frame_kernel,
        out_shape=[
            jax.ShapeDtypeStruct((2, 136, 128), jnp.bfloat16),
            jax.ShapeDtypeStruct((2, 136, 128), jnp.bfloat16),
            jax.ShapeDtypeStruct((4, 136, 128), jnp.bfloat16),
        ],
        in_specs=[ANY] + [VMEM] * 3,
        out_specs=[VMEM] * 3,
        compiler_params=pltpu.CompilerParams(vmem_limit_bytes=4 << 20),
        name="frame",
    )(after, rows, west, east)


def inner_kernel(low, field_ref, w1_ref, b1_ref, even_ref, odd_ref, mark_ref, lhs_ref, shift_ref):
    f32, bf16 = jnp.float32, jnp.bfloat16
    bias = jnp.concatenate([b1_ref[...], b1_ref[...]], axis=-1)
    weight = w1_ref[...].reshape(1536, 256)

    def step(b, carry):
        for n in range(ROWS + 2):
            base = pl.multiple_of((low + 1 + b * ROWS + n) * PITCH, 8)
            parts = [field_ref[pl.ds(base + at, 64), :].astype(bf16) for at in (ODD - 1, EVEN, ODD, EVEN + 1)]
            lhs_ref[n] = jnp.concatenate(parts, axis=-1)
        window = jnp.concatenate([lhs_ref[pl.ds(di, ROWS)].reshape(ROWS * 64, 512) for di in range(3)], axis=-1)
        hid = gelu(jnp.dot(window, weight, preferred_element_type=f32) + bias).reshape(ROWS, 64, 256)
        shift_ref[:, pl.ds(8, 64), :] = hid[:, :, 128:]
        wide = jnp.concatenate([shift_ref[:, pl.ds(7, 64), :], hid[:, :, :128], hid[:, :, 128:]], axis=-1)
        wide = wide.astype(bf16).reshape(ROWS // 2, 2, 64, 384)
        even_ref[pl.ds(b * (ROWS // 2), ROWS // 2)] = wide[:, 0]
        odd_ref[pl.ds(b * (ROWS // 2) + 1, ROWS // 2)] = wide[:, 1]
        return carry

    lax.fori_loop(0, 64 // ROWS, step, 0)
    mark_ref[...] = jnp.zeros(mark_ref.shape, mark_ref.dtype)


def inner(low, field, w1, b1):
    return pl.pallas_call(
        functools.partial(inner_kernel, low),
        out_shape=[
            pltpu.VMEM((32, 64, 384), jnp.bfloat16),
            pltpu.VMEM((33, 64, 384), jnp.bfloat16),
            jax.ShapeDtypeStruct((8, 128), jnp.float32),
        ],
        in_specs=[VMEM] * 3,
        out_specs=[VMEM] * 3,
        scratch_shapes=[pltpu.VMEM((ROWS + 2, 64, 512), jnp.bfloat16), pltpu.VMEM((ROWS, 72, 128), jnp.float32)],
        compiler_params=pltpu.CompilerParams(vmem_limit_bytes=24 << 20),
        name="inner",
    )(on_chip(field), w1, b1)


def rim_kernel(
    band_ref,
    even0_in,
    odd0_in,
    even1_in,
    odd1_in,
    right_ref,
    left_ref,
    near_ref,
    west_ref,
    east_ref,
    own_ref,
    down_ref,
    up_ref,
    across_ref,
    w1_ref,
    w1s_ref,
    b1_ref,
    w2_ref,
    b2_ref,
    even0_ref,
    odd0_ref,
    even1_ref,
    odd1_ref,
    out_ref,
    cols_ref,
    strip_ref,
    shift_ref,
    side_ref,
):
    del even0_in, odd0_in, even1_in, odd1_in
    f32, bf16 = jnp.float32, jnp.bfloat16
    band = band_ref[0]
    north, south = band == 0, band == 3
    first = jnp.where(north, 2, 0)
    flipped = (first, 1, 2 - first)
    dot = functools.partial(jnp.dot, preferred_element_type=f32)
    bias = b1_ref[...]
    bias2 = jnp.concatenate([bias, bias], axis=-1)

    body = (
        west_ref[pl.ds(0, 128), :],
        west_ref[pl.ds(128, 128), :],
        left_ref[pl.ds(0, 128), :],
        near_ref[...],
        right_ref[pl.ds(0, 128), :],
        right_ref[pl.ds(128, 128), :],
        east_ref[pl.ds(0, 128), :],
    )
    for n, col in enumerate(body):
        cols_ref[n, pl.ds(2, 128), :] = col.astype(f32)

    def wide(ref, n):
        return ref[n].astype(f32)

    rows = (
        jnp.where(north, wide(across_ref, 1), wide(down_ref, 0)),
        jnp.where(north, wide(across_ref, 0), wide(down_ref, 1)),
        wide(own_ref, 0),
        wide(own_ref, 1),
        wide(own_ref, 2),
        wide(own_ref, 3),
        jnp.where(south, wide(across_ref, 3), wide(up_ref, 0)),
    )
    where = (128, 129, 64, 0, 127, 63, 130)
    lhs = []
    for n, row in enumerate(rows):
        strip_ref[n, pl.ds(ODD, 64), :] = row[0:64]
        strip_ref[n, pl.ds(EVEN, 64), :] = row[64:128]
        strip_ref[n, pl.ds(ODD - 1, 1), :] = row[129:130]
        strip_ref[n, pl.ds(EVEN + 64, 1), :] = row[130:131]
        if n in (0, 1, 6):
            slab = 130 if n == 6 else n
            for m, at in enumerate(where):
                cols_ref[m, pl.ds(slab, 1), :] = row[at : at + 1]
        parts = [strip_ref[n, pl.ds(at, 64), :].astype(bf16) for at in (ODD - 1, EVEN, ODD, EVEN + 1)]
        lhs.append(jnp.concatenate(parts, axis=-1))

    for n, at in enumerate((0, 1, 4)):
        total = jnp.zeros((136, 128), f32) + bias
        top = jnp.zeros((8, 128), f32) + bias
        for di in range(3):
            window = jnp.concatenate(
                [cols_ref[at + m, pl.ds(di, 136), :].astype(bf16) for m in range(3)], axis=-1
            )
            total = total + dot(window, w1s_ref[di])
            if n == 0:
                top = top + dot(window[0:8], w1s_ref[flipped[di]])
        side_ref[n, pl.ds(0, 136), :] = gelu(total)
        if n == 0:
            side_ref[n, pl.ds(0, 1), :] = gelu(top)[0:1]

    odd1_ref[0] = odd0_ref[32]
    for r, at, taps in ((-1, 0, flipped), (0, 1, (0, 1, 2)), (127, 4, (0, 1, 2))):
        pre = bias2
        for di in range(3):
            pre = pre + dot(lhs[at + di], w1_ref[taps[di]])
        hid = gelu(pre)
        shift_ref[pl.ds(8, 64), :] = hid[:, 128:]
        shift_ref[pl.ds(7, 1), :] = side_ref[0, pl.ds(r + 1, 1), :]
        line = jnp.concatenate([shift_ref[pl.ds(7, 64), :], hid[:, :128], hid[:, 128:]], axis=-1).astype(bf16)
        if r == -1:
            odd0_ref[0] = line
        elif r == 0:
            even0_ref[0] = line
        else:
            odd1_ref[32] = line

    head = lax.broadcasted_iota(jnp.int32, (16, 256), 0) == 0
    foot = lax.broadcasted_iota(jnp.int32, (16, 128), 0) == 15

    def mend(ref, p, r):
        here = pl.ds(r + 1, 1)
        new = jnp.concatenate([side_ref[0, here, :], side_ref[1, here, :]], axis=-1)
        old = ref[p, pl.ds(0, 16), pl.ds(0, 256)].astype(f32)
        ref[p, pl.ds(0, 16), pl.ds(0, 256)] = jnp.where(head, new, old).astype(bf16)
        old = ref[p, pl.ds(48, 16), pl.ds(256, 128)].astype(f32)
        ref[p, pl.ds(48, 16), pl.ds(256, 128)] = jnp.where(foot, side_ref[2, here, :], old).astype(bf16)

    def mend_step(p, carry):
        mend(even0_ref, p, 2 * p)
        mend(odd0_ref, p + 1, 2 * p + 1)
        mend(even1_ref, p, 2 * p + 64)
        mend(odd1_ref, p + 1, 2 * p + 65)
        return carry

    lax.fori_loop(0, 32, mend_step, 0, unroll=2)
    odd1_ref[0] = odd0_ref[32]

    for half, (even_ref, odd_ref) in enumerate(((even0_ref, odd0_ref), (even1_ref, odd1_ref))):

        def finish(b, carry):
            total = jnp.broadcast_to(b2_ref[...], (256, 128))
            total = total + dot(odd_ref[pl.ds(b * 4, 4)].reshape(256, 384), w2_ref[0])
            total = total + dot(even_ref[pl.ds(b * 4, 4)].reshape(256, 384), w2_ref[1])
            total = total + dot(odd_ref[pl.ds(b * 4 + 1, 4)].reshape(256, 384), w2_ref[2])
            out_ref[pl.ds(half * 32 + b * 4, 4)] = total.reshape(4, 64, 128).astype(bf16)
            return carry

        lax.fori_loop(0, 8, finish, 0)


def rim(band, blocks, *rest):
    return pl.pallas_call(
        rim_kernel,
        out_shape=[pltpu.VMEM(b.shape, b.dtype) for b in blocks] + [jax.ShapeDtypeStruct((64, 64, 128), jnp.bfloat16)],
        in_specs=[SMEM] + [VMEM] * 18,
        out_specs=[VMEM] * 5,
        scratch_shapes=[
            pltpu.VMEM((7, 144, 128), jnp.float32),
            pltpu.VMEM((7, PITCH, 128), jnp.float32),
            pltpu.VMEM((72, 128), jnp.float32),
            pltpu.VMEM((3, 136, 128), jnp.float32),
        ],
        input_output_aliases={1: 0, 2: 1, 3: 2, 4: 3},
        compiler_params=pltpu.CompilerParams(vmem_limit_bytes=16 << 20),
        name="rim",
    )(band, *map(on_chip, blocks), *rest)[4]


def shards(background, values, cells, counts, w1, b1, w2, b2):
    lat, lon = lax.axis_size("lat"), lax.axis_size("lon")
    band = lax.axis_index("lat")[None]
    east_pairs = [(i, (i + 1) % lon) for i in range(lon)]
    west_pairs = [(j, i) for i, j in east_pairs]
    down_pairs = [(i, i + 1) for i in range(lat - 1)]
    up_pairs = [(j, i) for i, j in down_pairs]
    pole_pairs = [(b * lon + i, b * lon + (i + lon // 2) % lon) for b in (0, lat - 1) for i in range(lon)]

    sent = pack(values[0], cells[0].T, counts)
    got = lax.all_to_all(sent, ("lat", "lon"), split_axis=0, concat_axis=0, tiled=True)
    field, right, left, near, rows = scatter(band, got, spread(background))

    flat = w1.reshape(3, 384, 128)
    blank = jnp.zeros((3, 128, 128), jnp.bfloat16)
    paired = jnp.concatenate(
        [jnp.concatenate([flat, blank], axis=1), jnp.concatenate([blank, flat], axis=1)], axis=2
    )
    west = lax.ppermute(right, "lon", east_pairs)
    east = lax.ppermute(left, "lon", west_pairs)
    *upper, mark = inner(0, field, paired, b1[None])
    lower_rows, upper_rows, own = frame(mark, rows, west, east)
    down = lax.ppermute(lower_rows, "lat", down_pairs)
    up = lax.ppermute(upper_rows, "lat", up_pairs)
    across = lax.ppermute(own, ("lat", "lon"), pole_pairs)
    *lower, _ = inner(64, field, paired, b1[None])
    return rim(
        band,
        (*upper, *lower),
        right,
        left,
        near,
        west,
        east,
        own,
        down,
        up,
        across,
        paired,
        flat,
        b1[None],
        w2.reshape(3, 384, 128),
        b2[None],
    )


def solution(mesh):
    placed = (
        P("lat", "lon", None),
        P(("lat", "lon"), None, None, None),
        P(("lat", "lon"), None, None),
        P(("lat", "lon"), None),
        P(),
        P(),
        P(),
        P(),
    )
    return jax.shard_map(
        shards, mesh=mesh, in_specs=placed, out_specs=P("lat", "lon", None), check_vma=False
    )
```

```python
import functools

import jax
import jax.numpy as jnp
from jax import lax
from jax.experimental import pallas as pl
from jax.experimental.pallas import tpu as pltpu
from jax.sharding import PartitionSpec as P

PITCH, ODD, EVEN = 152, 8, 80
SLABS = 131
BATCH = 8
CHUNKS = 4
GROUP = 8
META = 8
ROWS = 16
GELU_A, GELU_B = 0.7978845608028654, 0.044715
VMEM = pl.BlockSpec(memory_space=pltpu.VMEM)
SMEM = pl.BlockSpec(memory_space=pltpu.SMEM)
ANY = pl.BlockSpec(memory_space=pl.ANY)


def on_chip(x):
    return pltpu.with_memory_space_constraint(x, pltpu.VMEM)


def off_chip(x):
    return pltpu.with_memory_space_constraint(x, pltpu.HBM)


def gelu(x):
    return 0.5 * x * (1.0 + jnp.tanh(GELU_A * (x + GELU_B * (x * x * x))))


def pack_kernel(values_ref, cells_ref, counts_ref, out_ref, held_ref, where_ref, live_ref, meta_ref, sem):
    owners, slots = values_ref.shape[0], values_ref.shape[1]
    part = owners // CHUNKS
    numbers = pltpu.make_async_copy(cells_ref, where_ref, sem.at[2 * CHUNKS])
    numbers.start()
    totals = pltpu.make_async_copy(counts_ref, live_ref, sem.at[2 * CHUNKS + 1])
    totals.start()
    arrive, leave = [], []
    for n in range(CHUNKS):
        here = pl.ds(n * part, part)
        arrive.append(
            pltpu.make_async_copy(values_ref.at[here], held_ref.at[here, pl.ds(0, slots), :], sem.at[n])
        )
        leave.append(pltpu.make_async_copy(held_ref.at[here], out_ref.at[here], sem.at[CHUNKS + n]))
        arrive[-1].start()
    numbers.wait()
    totals.wait()
    cells = where_ref[...]
    place = lax.broadcasted_iota(jnp.int32, cells.shape, 0)
    live = place < live_ref[...]
    row = cells >> 7
    col = cells & 127
    high = jnp.where(live, row + 2, 0)
    low = jnp.where(live, (col >> 1) + jnp.where((col & 1) == 1, ODD, EVEN), 0)
    marked = jnp.where(live, cells, -1)
    again = jnp.zeros(cells.shape, jnp.int32)
    for back in range(1, BATCH):
        same = (pltpu.roll(marked, back, 0) == marked) & live & (place % BATCH >= back)
        again = jnp.where(same, 1, again)
    blank = jnp.zeros((128 - slots, owners), jnp.float32)

    def turned(x):
        return jnp.concatenate([x.astype(jnp.float32), blank], axis=0).T

    meta_ref[pl.ds(0, owners, stride=META), :] = turned(high)
    meta_ref[pl.ds(1, owners, stride=META), :] = turned(low)
    meta_ref[pl.ds(2, owners, stride=META), :] = turned(again)
    for m in range(3, META):
        meta_ref[pl.ds(m, owners, stride=META), :] = jnp.zeros((owners, 128), jnp.float32)
    held_ref[:, pl.ds(slots, META), :] = meta_ref[...].reshape(owners, META, 128).astype(jnp.bfloat16)
    for came, goes in zip(arrive, leave):
        came.wait()
        goes.start()
    for goes in leave:
        goes.wait()


def pack(values, cells, counts):
    owners, slots, chans = values.shape
    return pl.pallas_call(
        pack_kernel,
        out_shape=pltpu.HBM((owners, slots + META, chans), jnp.bfloat16),
        in_specs=[ANY] * 3,
        out_specs=ANY,
        scratch_shapes=[
            pltpu.VMEM((owners, slots + META, chans), jnp.bfloat16),
            pltpu.VMEM((slots, owners), jnp.int32),
            pltpu.VMEM((1, owners), jnp.int32),
            pltpu.VMEM((owners * META, chans), jnp.float32),
            pltpu.SemaphoreType.DMA((2 * CHUNKS + 2,)),
        ],
        compiler_params=pltpu.CompilerParams(vmem_limit_bytes=12 << 20),
        name="pack",
    )(off_chip(values), off_chip(cells), off_chip(counts))


def spread_kernel(field_ref, parted_ref, wide_ref):
    def step(r, carry):
        wide_ref[...] = field_ref[r].astype(jnp.float32)
        parted_ref[r, pl.ds(0, 64), :] = wide_ref[pl.ds(1, 64, stride=2), :].astype(jnp.bfloat16)
        parted_ref[r, pl.ds(64, 64), :] = wide_ref[pl.ds(0, 64, stride=2), :].astype(jnp.bfloat16)
        return carry

    lax.fori_loop(0, field_ref.shape[0], step, 0)


def spread(field):
    return pl.pallas_call(
        spread_kernel,
        out_shape=pltpu.HBM(field.shape, field.dtype),
        in_specs=[VMEM],
        out_specs=VMEM,
        scratch_shapes=[pltpu.VMEM((128, 128), jnp.float32)],
        compiler_params=pltpu.CompilerParams(vmem_limit_bytes=12 << 20),
        name="spread",
    )(field)


def scatter_kernel(band_ref, got_ref, parted_ref, acc_ref, right_ref, left_ref, near_ref, rows_ref, *rest):
    other_ref, start_ref, wide_ref, meta_ref, index_ref, late_ref, cells0_ref, cells1_ref, list_ref, sem = rest
    del band_ref
    sources, slots = got_ref.shape[0], got_ref.shape[1] - META
    part = 128 // CHUNKS
    pieces = []
    for n in range(CHUNKS):
        here = pl.ds(n * part, part)
        pieces.append(pltpu.make_async_copy(parted_ref.at[here], start_ref.at[here], sem.at[3 + n]))
        pieces[-1].start()

    def unpack(s, carry):
        meta_ref[pl.ds(pl.multiple_of(s * META, META), META), :] = got_ref[s, pl.ds(slots, META), :].astype(jnp.float32)
        return carry

    lax.fori_loop(0, sources, unpack, 0, unroll=8)
    high = meta_ref[pl.ds(0, sources, stride=META), :]
    low = meta_ref[pl.ds(1, sources, stride=META), :]
    again = meta_ref[pl.ds(2, sources, stride=META), :]
    spot = high * PITCH + low
    index_ref[...] = jnp.where(again > 0, 0.0, spot).astype(jnp.int32)
    lane = lax.broadcasted_iota(jnp.int32, again.shape, 1)
    inside = lane < slots
    count = jnp.sum(jnp.where(inside, again, 0.0), axis=1, keepdims=True)
    furthest = jnp.max(jnp.where(inside & (again > 0), lane, 0).astype(jnp.float32), axis=1, keepdims=True)
    crowd = jnp.sum(count.reshape(sources // GROUP, GROUP, 1), axis=1, keepdims=True)
    crowd = jnp.broadcast_to(crowd, (sources // GROUP, GROUP, 128)).reshape(sources, 128)
    notes = jnp.where(lane == slots, count, jnp.where(lane == slots + 1, furthest, crowd))
    late = jnp.where(inside, again * spot, notes)
    late_ref[...] = late.astype(jnp.int32)

    cells = (cells0_ref, cells1_ref)

    def fetch(group, half):
        return pltpu.make_async_copy(index_ref.at[pl.ds(group * GROUP, GROUP), :], cells[half], sem.at[half])

    fetch(0, 0).start()
    fetch(1, 1).start()
    listed = pltpu.make_async_copy(late_ref, list_ref, sem.at[2])
    listed.start()

    def clear(r, carry):
        base = pl.multiple_of((r + 2) * PITCH, 8)
        for at in (ODD, EVEN):
            other_ref[pl.ds(base + at, 64), :] = jnp.zeros((64, 128), jnp.float32)
        return carry

    lax.fori_loop(0, 128, clear, 0)

    def widen(r, carry):
        base = pl.multiple_of((r + 2) * PITCH, 8)
        for at in (0, EVEN - 8, EVEN + 64):
            acc_ref[pl.ds(base + at, 8), :] = jnp.zeros((8, 128), jnp.float32)
        acc_ref[pl.ds(base + ODD, 64), :] = start_ref[r, pl.ds(0, 64), :].astype(jnp.float32)
        acc_ref[pl.ds(base + EVEN, 64), :] = start_ref[r, pl.ds(64, 64), :].astype(jnp.float32)
        return carry

    for n, piece in enumerate(pieces):
        piece.wait()
        lax.fori_loop(n * part, (n + 1) * part, widen, 0)
    accs = (acc_ref, other_ref)

    def add(step, carry):
        for half in range(2):
            group = step * 2 + half
            fetch(group, half).wait()
            for t in range(GROUP):
                wide = wide_ref.at[t % 2]
                wide[...] = got_ref[group * GROUP + t, pl.ds(0, slots), :].astype(jnp.float32)
                for n, k in enumerate(range(0, slots, BATCH)):
                    acc = accs[n % 2]
                    where = [cells[half][t, k + m] for m in range(BATCH)]
                    sums = [acc[pl.ds(i, 1), :] + wide[pl.ds(k + m, 1), :] for m, i in enumerate(where)]
                    for i, total in zip(where, sums):
                        acc[pl.ds(i, 1), :] = total

            @pl.when(group + 2 < sources // GROUP)
            def _():
                fetch(group + 2, half).start()

        return carry

    lax.fori_loop(0, sources // (2 * GROUP), add, 0)
    listed.wait()

    def rest_of(s, carry):
        repeats = list_ref[s, slots]
        furthest = list_ref[s, slots + 1]

        @pl.when(repeats > 0)
        def _():
            wide_ref[0] = got_ref[s, pl.ds(0, slots), :].astype(jnp.float32)

            def one(k, carry):
                i = list_ref[s, k]

                @pl.when(i > 0)
                def _():
                    acc_ref[pl.ds(i, 1), :] = acc_ref[pl.ds(i, 1), :] + wide_ref[0, pl.ds(k, 1), :]

                return carry

            lax.fori_loop(jnp.where(repeats > 1, 0, furthest), furthest + 1, one, 0)

        return carry

    for group in range(sources // GROUP):

        @pl.when(list_ref[group * GROUP, slots + 2] > 0)
        def _():
            lax.fori_loop(group * GROUP, (group + 1) * GROUP, rest_of, 0)


    def merge(r, carry):
        base = pl.multiple_of((r + 2) * PITCH, 8)
        for at in (ODD, EVEN):
            here = pl.ds(base + at, 64)
            acc_ref[here, :] = acc_ref[here, :] + other_ref[here, :]
        return carry

    lax.fori_loop(0, 128, merge, 0)
    bf16 = jnp.bfloat16
    ends = (0, 1, 126, 127)
    for n, at in enumerate((EVEN + 63, ODD + 63)):
        right_ref[pl.ds(n * 128, 128), :] = acc_ref[pl.ds(2 * PITCH + at, 128, stride=PITCH), :].astype(bf16)
    left_ref[pl.ds(0, 128), :] = acc_ref[pl.ds(2 * PITCH + EVEN, 128, stride=PITCH), :].astype(bf16)
    near_ref[...] = acc_ref[pl.ds(2 * PITCH + ODD, 128, stride=PITCH), :].astype(bf16)
    east = [acc_ref[pl.ds((r + 2) * PITCH + at, 1), :] for r in ends for at in (EVEN + 63, ODD + 63)]
    west = [acc_ref[pl.ds((r + 2) * PITCH + EVEN, 1), :] for r in ends]
    right_ref[pl.ds(256, 8), :] = jnp.concatenate(east, axis=0).astype(bf16)
    left_ref[pl.ds(128, 8), :] = jnp.concatenate(west + west, axis=0).astype(bf16)
    for n, r in enumerate(ends):
        base = (r + 2) * PITCH
        rows_ref[n, pl.ds(0, 64), :] = acc_ref[pl.ds(base + ODD, 64), :].astype(bf16)
        rows_ref[n, pl.ds(64, 64), :] = acc_ref[pl.ds(base + EVEN, 64), :].astype(bf16)


def scatter(band, got, start):
    return pl.pallas_call(
        scatter_kernel,
        out_shape=[
            pltpu.VMEM((SLABS * PITCH, 128), jnp.float32),
            jax.ShapeDtypeStruct((264, 128), jnp.bfloat16),
            jax.ShapeDtypeStruct((136, 128), jnp.bfloat16),
            jax.ShapeDtypeStruct((128, 128), jnp.bfloat16),
            jax.ShapeDtypeStruct((4, 128, 128), jnp.bfloat16),
        ],
        in_specs=[SMEM, VMEM, ANY],
        out_specs=[VMEM] * 5,
        scratch_shapes=[
            pltpu.VMEM((130 * PITCH, 128), jnp.float32),
            pltpu.VMEM((128, 128, 128), jnp.bfloat16),
            pltpu.VMEM((2, 96, 128), jnp.float32),
            pltpu.VMEM((128 * META, 128), jnp.float32),
            pltpu.VMEM((128, 128), jnp.int32),
            pltpu.VMEM((128, 128), jnp.int32),
            pltpu.SMEM((GROUP, 128), jnp.int32),
            pltpu.SMEM((GROUP, 128), jnp.int32),
            pltpu.SMEM((128, 128), jnp.int32),
            pltpu.SemaphoreType.DMA((3 + CHUNKS,)),
        ],
        compiler_params=pltpu.CompilerParams(vmem_limit_bytes=24 << 20),
        name="scatter",
    )(band, on_chip(got), off_chip(start))


def frame_kernel(after_ref, rows_ref, west_ref, east_ref, down_ref, up_ref, all_ref):
    del after_ref
    f32, bf16 = jnp.float32, jnp.bfloat16
    west = west_ref[pl.ds(256, 8), :].astype(f32)
    east = east_ref[pl.ds(128, 8), :].astype(f32)
    for n in range(4):
        tail = jnp.concatenate([west[2 * n : 2 * n + 2], east[n : n + 1], jnp.zeros((5, 128), f32)], axis=0)
        for ref, at in ((all_ref, n), (up_ref, n) if n < 2 else (down_ref, n - 2)):
            ref[at, pl.ds(0, 128), :] = rows_ref[n]
            ref[at, pl.ds(128, 8), :] = tail.astype(bf16)


def frame(after, rows, west, east):
    return pl.pallas_call(
        frame_kernel,
        out_shape=[
            jax.ShapeDtypeStruct((2, 136, 128), jnp.bfloat16),
            jax.ShapeDtypeStruct((2, 136, 128), jnp.bfloat16),
            jax.ShapeDtypeStruct((4, 136, 128), jnp.bfloat16),
        ],
        in_specs=[ANY] + [VMEM] * 3,
        out_specs=[VMEM] * 3,
        compiler_params=pltpu.CompilerParams(vmem_limit_bytes=4 << 20),
        name="frame",
    )(after, rows, west, east)


def inner_kernel(low, field_ref, w1_ref, b1_ref, even_ref, odd_ref, edge_ref, lhs_ref, shift_ref, tail_ref):
    f32, bf16 = jnp.float32, jnp.bfloat16
    bias = jnp.concatenate([b1_ref[...], b1_ref[...]], axis=-1)
    weight = w1_ref[...].reshape(1536, 256)

    def step(b, carry):
        for n in range(ROWS + 2):
            base = pl.multiple_of((low + 1 + b * ROWS + n) * PITCH, 8)
            parts = [field_ref[pl.ds(base + at, 64), :].astype(bf16) for at in (ODD - 1, EVEN, ODD, EVEN + 1)]
            lhs_ref[n] = jnp.concatenate(parts, axis=-1)
        window = jnp.concatenate([lhs_ref[pl.ds(di, ROWS)].reshape(ROWS * 64, 512) for di in range(3)], axis=-1)
        hid = gelu(jnp.dot(window, weight, preferred_element_type=f32) + bias).reshape(ROWS, 64, 256)
        shift_ref[:, pl.ds(8, 64), :] = hid[:, :, 128:]
        tail_ref[...] = hid[:, 56:, :128]
        for n in range(ROWS):
            line = pl.ds(b * ROWS + n, 1)
            edge_ref[0, line, :] = shift_ref[n, pl.ds(8, 1), :]
            edge_ref[1, line, :] = shift_ref[n, pl.ds(70, 1), :]
            edge_ref[2, line, :] = tail_ref[n, pl.ds(7, 1), :]
        wide = jnp.concatenate([shift_ref[:, pl.ds(7, 64), :], hid[:, :, :128], hid[:, :, 128:]], axis=-1)
        wide = wide.astype(bf16).reshape(ROWS // 2, 2, 64, 384)
        even_ref[pl.ds(b * (ROWS // 2), ROWS // 2)] = wide[:, 0]
        odd_ref[pl.ds(b * (ROWS // 2) + 1, ROWS // 2)] = wide[:, 1]
        return carry

    lax.fori_loop(0, 64 // ROWS, step, 0)


def inner(low, field, w1, b1):
    return pl.pallas_call(
        functools.partial(inner_kernel, low),
        out_shape=[
            pltpu.VMEM((32, 64, 384), jnp.bfloat16),
            pltpu.VMEM((33, 64, 384), jnp.bfloat16),
            jax.ShapeDtypeStruct((3, 64, 128), jnp.float32),
        ],
        in_specs=[VMEM] * 3,
        out_specs=[VMEM] * 3,
        scratch_shapes=[pltpu.VMEM((ROWS + 2, 64, 512), jnp.bfloat16), pltpu.VMEM((ROWS, 72, 128), jnp.float32), pltpu.VMEM((ROWS, 8, 128), jnp.float32)],
        compiler_params=pltpu.CompilerParams(vmem_limit_bytes=24 << 20),
        name="inner",
    )(on_chip(field), w1, b1)


def rim_kernel(
    band_ref,
    even0_in,
    odd0_in,
    even1_in,
    odd1_in,
    edge0_ref,
    edge1_ref,
    right_ref,
    left_ref,
    near_ref,
    west_ref,
    east_ref,
    own_ref,
    down_ref,
    up_ref,
    across_ref,
    w1_ref,
    w1s_ref,
    b1_ref,
    w2_ref,
    b2_ref,
    even0_ref,
    odd0_ref,
    even1_ref,
    odd1_ref,
    out_ref,
    cols_ref,
    strip_ref,
    shift_ref,
    side_ref,
    ends_ref,
    total_ref,
):
    del even0_in, odd0_in, even1_in, odd1_in
    f32, bf16 = jnp.float32, jnp.bfloat16
    band = band_ref[0]
    north, south = band == 0, band == 3
    dot = functools.partial(jnp.dot, preferred_element_type=f32)
    bias = b1_ref[...]
    bias2 = jnp.concatenate([bias, bias], axis=-1)
    pairs = w1_ref[...].reshape(1536, 256)
    taps1 = w1s_ref[...].reshape(1152, 128)
    taps2 = w2_ref[...].reshape(1152, 128)

    body = (
        west_ref[pl.ds(0, 128), :],
        west_ref[pl.ds(128, 128), :],
        left_ref[pl.ds(0, 128), :],
        near_ref[...],
        right_ref[pl.ds(0, 128), :],
        right_ref[pl.ds(128, 128), :],
        east_ref[pl.ds(0, 128), :],
    )
    for n, col in enumerate(body):
        cols_ref[n, pl.ds(2, 128), :] = col.astype(f32)

    def wide(ref, n):
        return ref[n].astype(f32)

    second = jnp.where(north, wide(across_ref, 1), wide(down_ref, 0))
    first = jnp.where(north, wide(across_ref, 0), wide(down_ref, 1))
    own = [wide(own_ref, n) for n in range(4)]
    below = jnp.where(south, wide(across_ref, 3), wide(up_ref, 0))
    top = (jnp.where(north, own[0], second), first, jnp.where(north, second, own[0]))
    for slab, row in ((0, second), (1, first), (130, below)):
        for m, at in enumerate((128, 129, 64, 0, 127, 63, 130)):
            cols_ref[m, pl.ds(slab, 1), :] = row[at : at + 1]

    def lines(n, row):
        strip_ref[n, pl.ds(ODD, 64), :] = row[0:64]
        strip_ref[n, pl.ds(EVEN, 64), :] = row[64:128]
        strip_ref[n, pl.ds(ODD - 1, 1), :] = row[129:130]
        strip_ref[n, pl.ds(EVEN + 64, 1), :] = row[130:131]
        parts = [strip_ref[n, pl.ds(at, 64), :].astype(bf16) for at in (ODD - 1, EVEN, ODD, EVEN + 1)]
        return jnp.concatenate(parts, axis=-1)

    lhs = [lines(n, row) for n, row in enumerate((top[0], first, top[2], *own, below))]
    corner = []
    for row in top:
        corner.append(jnp.zeros((8, 128), f32))
        corner.extend(jnp.broadcast_to(row[at : at + 1], (8, 128)) for at in (128, 129, 64))
    corner = jnp.concatenate(corner, axis=-1).astype(bf16)
    stack = [jnp.concatenate([lhs[n] for n in picks], axis=-1) for picks in ((0, 1, 2), (1, 3, 4), (5, 6, 7))]
    hid = gelu(dot(jnp.concatenate([*stack, corner, corner], axis=0), pairs) + bias2)

    windows = []
    for at in (0, 1, 4):
        parts = [cols_ref[at + m, pl.ds(di, 136), :] for di in range(3) for m in range(3)]
        windows.append(jnp.concatenate(parts, axis=-1))
    cols = gelu(dot(jnp.concatenate(windows, axis=0).astype(bf16), taps1) + bias)
    for n, to in enumerate((0, 1, 5)):
        side_ref[to] = cols[n * 136 : (n + 1) * 136]
    for n in range(3):
        side_ref[n + 2, pl.ds(1, 64), :] = edge0_ref[n]
        side_ref[n + 2, pl.ds(65, 64), :] = edge1_ref[n]
    for n, r in enumerate((-1, 0, 127)):
        here = pl.ds(r + 1, 1)
        even, odd = hid[n * 64 : n * 64 + 64, :128], hid[n * 64 : n * 64 + 64, 128:]
        side_ref[1, here, :] = even[0:1]
        side_ref[2, here, :] = odd[0:1]
        side_ref[3, here, :] = odd[62:63]
        side_ref[4, here, :] = even[63:64]
        side_ref[5, here, :] = odd[63:64]
        shift_ref[pl.ds(8, 64), :] = odd
        line = jnp.concatenate([shift_ref[pl.ds(7, 64), :], even, odd], axis=-1).astype(bf16)
        if r == -1:
            odd0_ref[0] = line
        elif r == 0:
            even0_ref[0] = line
        else:
            odd1_ref[32] = line
    side_ref[0, pl.ds(0, 1), :] = hid[192:193, 128:]
    odd1_ref[0] = odd0_ref[32]

    windows = []
    for at in (0, 3):
        parts = [side_ref[at + m, pl.ds(a, 64, stride=2), :] for a in range(3) for m in range(3)]
        windows.append(jnp.concatenate(parts, axis=-1))
    ends_ref[...] = dot(jnp.concatenate(windows, axis=0).astype(bf16), taps2) + b2_ref[...]

    for half, (even_ref, odd_ref) in enumerate(((even0_ref, odd0_ref), (even1_ref, odd1_ref))):

        def finish(b, carry):
            p = b * 8
            window = jnp.concatenate(
                [
                    odd_ref[pl.ds(p, 8)].reshape(512, 384),
                    even_ref[pl.ds(p, 8)].reshape(512, 384),
                    odd_ref[pl.ds(p + 1, 8)].reshape(512, 384),
                ],
                axis=-1,
            )
            total_ref[...] = (dot(window, taps2) + b2_ref[...]).reshape(8, 64, 128)
            for n in range(8):
                total_ref[n, pl.ds(0, 1), :] = ends_ref[pl.ds(half * 32 + p + n, 1), :]
                total_ref[n, pl.ds(63, 1), :] = ends_ref[pl.ds(64 + half * 32 + p + n, 1), :]
            out_ref[pl.ds(half * 32 + p, 8)] = total_ref[...].astype(bf16)
            return carry

        lax.fori_loop(0, 4, finish, 0)


def rim(band, blocks, *rest):
    return pl.pallas_call(
        rim_kernel,
        out_shape=[pltpu.VMEM(b.shape, b.dtype) for b in blocks] + [jax.ShapeDtypeStruct((64, 64, 128), jnp.bfloat16)],
        in_specs=[SMEM] + [VMEM] * 20,
        out_specs=[VMEM] * 5,
        scratch_shapes=[
            pltpu.VMEM((7, 144, 128), jnp.float32),
            pltpu.VMEM((8, PITCH, 128), jnp.float32),
            pltpu.VMEM((72, 128), jnp.float32),
            pltpu.VMEM((6, 136, 128), jnp.float32),
            pltpu.VMEM((128, 128), jnp.float32),
            pltpu.VMEM((8, 64, 128), jnp.float32),
        ],
        input_output_aliases={1: 0, 2: 1, 3: 2, 4: 3},
        compiler_params=pltpu.CompilerParams(vmem_limit_bytes=20 << 20),
        name="rim",
    )(band, *map(on_chip, blocks), *rest)[4]


def shards(background, values, cells, counts, w1, b1, w2, b2):
    lat, lon = lax.axis_size("lat"), lax.axis_size("lon")
    band = lax.axis_index("lat")[None]
    east_pairs = [(i, (i + 1) % lon) for i in range(lon)]
    west_pairs = [(j, i) for i, j in east_pairs]
    down_pairs = [(i, i + 1) for i in range(lat - 1)]
    up_pairs = [(j, i) for i, j in down_pairs]
    pole_pairs = [(b * lon + i, b * lon + (i + lon // 2) % lon) for b in (0, lat - 1) for i in range(lon)]

    sent = pack(values[0], cells[0].T, counts)
    got = lax.all_to_all(sent, ("lat", "lon"), split_axis=0, concat_axis=0, tiled=True)
    field, right, left, near, rows = scatter(band, got, spread(background))

    flat = w1.reshape(3, 384, 128)
    blank = jnp.zeros((3, 128, 128), jnp.bfloat16)
    paired = jnp.concatenate(
        [jnp.concatenate([flat, blank], axis=1), jnp.concatenate([blank, flat], axis=1)], axis=2
    )
    west = lax.ppermute(right, "lon", east_pairs)
    east = lax.ppermute(left, "lon", west_pairs)
    *upper, upper_edge = inner(0, field, paired, b1[None])
    lower_rows, upper_rows, own = frame(upper_edge, rows, west, east)
    down = lax.ppermute(lower_rows, "lat", down_pairs)
    up = lax.ppermute(upper_rows, "lat", up_pairs)
    across = lax.ppermute(own, ("lat", "lon"), pole_pairs)
    *lower, lower_edge = inner(64, field, paired, b1[None])
    return rim(
        band,
        (*upper, *lower),
        upper_edge,
        lower_edge,
        right,
        left,
        near,
        west,
        east,
        own,
        down,
        up,
        across,
        paired,
        flat,
        b1[None],
        w2.reshape(3, 384, 128),
        b2[None],
    )


def solution(mesh):
    placed = (
        P("lat", "lon", None),
        P(("lat", "lon"), None, None, None),
        P(("lat", "lon"), None, None),
        P(("lat", "lon"), None),
        P(),
        P(),
        P(),
        P(),
    )
    return jax.shard_map(
        shards, mesh=mesh, in_specs=placed, out_specs=P("lat", "lon", None), check_vma=False
    )
```

```python
import functools

import jax
import jax.numpy as jnp
from jax import lax
from jax.experimental import pallas as pl
from jax.experimental.pallas import tpu as pltpu
from jax.sharding import PartitionSpec as P

PITCH, ODD, EVEN = 152, 8, 80
SLABS = 131
BATCH = 8
CHUNKS = 4
GROUP = 8
META = 8
ROWS = 16
GELU_A, GELU_B = 0.7978845608028654, 0.044715
VMEM = pl.BlockSpec(memory_space=pltpu.VMEM)
SMEM = pl.BlockSpec(memory_space=pltpu.SMEM)
ANY = pl.BlockSpec(memory_space=pl.ANY)


def on_chip(x):
    return pltpu.with_memory_space_constraint(x, pltpu.VMEM)


def off_chip(x):
    return pltpu.with_memory_space_constraint(x, pltpu.HBM)


def gelu(x):
    return 0.5 * x * (1.0 + jnp.tanh(GELU_A * (x + GELU_B * (x * x * x))))


def pack_kernel(values_ref, cells_ref, counts_ref, out_ref, held_ref, where_ref, live_ref, meta_ref, tail_ref, sem):
    owners, slots = values_ref.shape[0], values_ref.shape[1]
    part = owners // CHUNKS
    numbers = pltpu.make_async_copy(cells_ref, where_ref, sem.at[2 * CHUNKS])
    numbers.start()
    totals = pltpu.make_async_copy(counts_ref, live_ref, sem.at[2 * CHUNKS + 1])
    totals.start()
    arrive, leave = [], []
    for n in range(CHUNKS):
        here = pl.ds(n * part, part)
        arrive.append(
            pltpu.make_async_copy(values_ref.at[here], held_ref.at[here], sem.at[n])
        )
        leave.append(
            pltpu.make_async_copy(
                held_ref.at[here], out_ref.at[here, pl.ds(0, slots), :], sem.at[CHUNKS + n]
            )
        )
        arrive[-1].start()
    for came, goes in zip(arrive, leave):
        came.wait()
        goes.start()
    numbers.wait()
    totals.wait()
    cells = where_ref[...]
    place = lax.broadcasted_iota(jnp.int32, cells.shape, 0)
    live = place < live_ref[...]
    row = cells >> 7
    col = cells & 127
    high = jnp.where(live, row + 2, 0)
    low = jnp.where(live, (col >> 1) + jnp.where((col & 1) == 1, ODD, EVEN), 0)
    marked = jnp.where(live, cells, -1)
    again = jnp.zeros(cells.shape, jnp.int32)
    for back in range(1, BATCH):
        same = (pltpu.roll(marked, back, 0) == marked) & live & (place % BATCH >= back)
        again = jnp.where(same, 1, again)
    blank = jnp.zeros((128 - slots, owners), jnp.float32)

    def turned(x):
        return jnp.concatenate([x.astype(jnp.float32), blank], axis=0).T

    meta_ref[pl.ds(0, owners, stride=META), :] = turned(high)
    meta_ref[pl.ds(1, owners, stride=META), :] = turned(low)
    meta_ref[pl.ds(2, owners, stride=META), :] = turned(again)
    for m in range(3, META):
        meta_ref[pl.ds(m, owners, stride=META), :] = jnp.zeros((owners, 128), jnp.float32)
    tail_ref[...] = meta_ref[...].reshape(owners, META, 128).astype(jnp.bfloat16)
    last = pltpu.make_async_copy(tail_ref, out_ref.at[:, pl.ds(slots, META), :], sem.at[2 * CHUNKS + 2])
    last.start()
    for goes in (*leave, last):
        goes.wait()


def pack(values, cells, counts):
    owners, slots, chans = values.shape
    return pl.pallas_call(
        pack_kernel,
        out_shape=pltpu.HBM((owners, slots + META, chans), jnp.bfloat16),
        in_specs=[ANY] * 3,
        out_specs=ANY,
        scratch_shapes=[
            pltpu.VMEM((owners, slots, chans), jnp.bfloat16),
            pltpu.VMEM((slots, owners), jnp.int32),
            pltpu.VMEM((1, owners), jnp.int32),
            pltpu.VMEM((owners * META, chans), jnp.float32),
            pltpu.VMEM((owners, META, chans), jnp.bfloat16),
            pltpu.SemaphoreType.DMA((2 * CHUNKS + 3,)),
        ],
        compiler_params=pltpu.CompilerParams(vmem_limit_bytes=12 << 20),
        name="pack",
    )(off_chip(values), off_chip(cells), off_chip(counts))


def spread_kernel(field_ref, parted_ref, wide_ref):
    def step(r, carry):
        wide_ref[...] = field_ref[r].astype(jnp.float32)
        parted_ref[r, pl.ds(0, 64), :] = wide_ref[pl.ds(1, 64, stride=2), :].astype(jnp.bfloat16)
        parted_ref[r, pl.ds(64, 64), :] = wide_ref[pl.ds(0, 64, stride=2), :].astype(jnp.bfloat16)
        return carry

    lax.fori_loop(0, field_ref.shape[0], step, 0)


def spread(field):
    return pl.pallas_call(
        spread_kernel,
        out_shape=pltpu.HBM(field.shape, field.dtype),
        in_specs=[VMEM],
        out_specs=VMEM,
        scratch_shapes=[pltpu.VMEM((128, 128), jnp.float32)],
        compiler_params=pltpu.CompilerParams(vmem_limit_bytes=12 << 20),
        name="spread",
    )(field)


def scatter_kernel(place_ref, got_ref, parted_ref, acc_ref, right_ref, left_ref, near_ref, rows_ref, *rest):
    other_ref, start_ref, wide_ref, meta_ref, index_ref, late_ref, cells0_ref, cells1_ref, list_ref, sem = rest
    del place_ref
    sources, slots = got_ref.shape[0], got_ref.shape[1] - META
    part = 128 // CHUNKS
    pieces = []
    for n in range(CHUNKS):
        here = pl.ds(n * part, part)
        pieces.append(pltpu.make_async_copy(parted_ref.at[here], start_ref.at[here], sem.at[3 + n]))
        pieces[-1].start()

    def unpack(s, carry):
        meta_ref[pl.ds(pl.multiple_of(s * META, META), META), :] = got_ref[s, pl.ds(slots, META), :].astype(jnp.float32)
        return carry

    lax.fori_loop(0, sources, unpack, 0, unroll=8)
    high = meta_ref[pl.ds(0, sources, stride=META), :]
    low = meta_ref[pl.ds(1, sources, stride=META), :]
    again = meta_ref[pl.ds(2, sources, stride=META), :]
    spot = high * PITCH + low
    index_ref[...] = jnp.where(again > 0, 0.0, spot).astype(jnp.int32)
    lane = lax.broadcasted_iota(jnp.int32, again.shape, 1)
    inside = lane < slots
    count = jnp.sum(jnp.where(inside, again, 0.0), axis=1, keepdims=True)
    furthest = jnp.max(jnp.where(inside & (again > 0), lane, 0).astype(jnp.float32), axis=1, keepdims=True)
    crowd = jnp.sum(count.reshape(sources // GROUP, GROUP, 1), axis=1, keepdims=True)
    crowd = jnp.broadcast_to(crowd, (sources // GROUP, GROUP, 128)).reshape(sources, 128)
    notes = jnp.where(lane == slots, count, jnp.where(lane == slots + 1, furthest, crowd))
    late = jnp.where(inside, again * spot, notes)
    late_ref[...] = late.astype(jnp.int32)

    cells = (cells0_ref, cells1_ref)

    def fetch(group, half):
        return pltpu.make_async_copy(index_ref.at[pl.ds(group * GROUP, GROUP), :], cells[half], sem.at[half])

    fetch(0, 0).start()
    fetch(1, 1).start()
    listed = pltpu.make_async_copy(late_ref, list_ref, sem.at[2])
    listed.start()

    def clear(r, carry):
        base = pl.multiple_of((r + 2) * PITCH, 8)
        for at in (ODD, EVEN):
            other_ref[pl.ds(base + at, 64), :] = jnp.zeros((64, 128), jnp.float32)
        return carry

    lax.fori_loop(0, 128, clear, 0)

    def widen(r, carry):
        base = pl.multiple_of((r + 2) * PITCH, 8)
        for at in (0, EVEN - 8, EVEN + 64):
            acc_ref[pl.ds(base + at, 8), :] = jnp.zeros((8, 128), jnp.float32)
        acc_ref[pl.ds(base + ODD, 64), :] = start_ref[r, pl.ds(0, 64), :].astype(jnp.float32)
        acc_ref[pl.ds(base + EVEN, 64), :] = start_ref[r, pl.ds(64, 64), :].astype(jnp.float32)
        return carry

    for n, piece in enumerate(pieces):
        piece.wait()
        lax.fori_loop(n * part, (n + 1) * part, widen, 0)
    accs = (acc_ref, other_ref)

    def add(step, carry):
        for half in range(2):
            group = step * 2 + half
            fetch(group, half).wait()
            for t in range(GROUP):
                wide = wide_ref.at[t % 2]
                wide[...] = got_ref[group * GROUP + t, pl.ds(0, slots), :].astype(jnp.float32)
                for n, k in enumerate(range(0, slots, BATCH)):
                    acc = accs[n % 2]
                    where = [cells[half][t, k + m] for m in range(BATCH)]
                    sums = [acc[pl.ds(i, 1), :] + wide[pl.ds(k + m, 1), :] for m, i in enumerate(where)]
                    for i, total in zip(where, sums):
                        acc[pl.ds(i, 1), :] = total

            @pl.when(group + 2 < sources // GROUP)
            def _():
                fetch(group + 2, half).start()

        return carry

    lax.fori_loop(0, sources // (2 * GROUP), add, 0)
    listed.wait()

    def rest_of(s, carry):
        repeats = list_ref[s, slots]
        furthest = list_ref[s, slots + 1]

        @pl.when(repeats > 0)
        def _():
            wide_ref[0] = got_ref[s, pl.ds(0, slots), :].astype(jnp.float32)

            def one(k, carry):
                i = list_ref[s, k]

                @pl.when(i > 0)
                def _():
                    acc_ref[pl.ds(i, 1), :] = acc_ref[pl.ds(i, 1), :] + wide_ref[0, pl.ds(k, 1), :]

                return carry

            lax.fori_loop(jnp.where(repeats > 1, 0, furthest), furthest + 1, one, 0)

        return carry

    for group in range(sources // GROUP):

        @pl.when(list_ref[group * GROUP, slots + 2] > 0)
        def _():
            lax.fori_loop(group * GROUP, (group + 1) * GROUP, rest_of, 0)


    def merge(r, carry):
        base = pl.multiple_of((r + 2) * PITCH, 8)
        for at in (ODD, EVEN):
            here = pl.ds(base + at, 64)
            acc_ref[here, :] = acc_ref[here, :] + other_ref[here, :]
        return carry

    lax.fori_loop(0, 128, merge, 0)
    bf16 = jnp.bfloat16
    ends = (0, 1, 126, 127)
    for n, at in enumerate((EVEN + 63, ODD + 63)):
        right_ref[pl.ds(n * 128, 128), :] = acc_ref[pl.ds(2 * PITCH + at, 128, stride=PITCH), :].astype(bf16)
    left_ref[pl.ds(0, 128), :] = acc_ref[pl.ds(2 * PITCH + EVEN, 128, stride=PITCH), :].astype(bf16)
    near_ref[...] = acc_ref[pl.ds(2 * PITCH + ODD, 128, stride=PITCH), :].astype(bf16)
    east = [acc_ref[pl.ds((r + 2) * PITCH + at, 1), :] for r in ends for at in (EVEN + 63, ODD + 63)]
    west = [acc_ref[pl.ds((r + 2) * PITCH + EVEN, 1), :] for r in ends]
    right_ref[pl.ds(256, 8), :] = jnp.concatenate(east, axis=0).astype(bf16)
    left_ref[pl.ds(128, 8), :] = jnp.concatenate(west + west, axis=0).astype(bf16)
    for n, r in enumerate(ends):
        base = (r + 2) * PITCH
        rows_ref[n, pl.ds(0, 64), :] = acc_ref[pl.ds(base + ODD, 64), :].astype(bf16)
        rows_ref[n, pl.ds(64, 64), :] = acc_ref[pl.ds(base + EVEN, 64), :].astype(bf16)


def scatter(place, got, start):
    return pl.pallas_call(
        scatter_kernel,
        out_shape=[
            pltpu.VMEM((SLABS * PITCH, 128), jnp.float32),
            jax.ShapeDtypeStruct((264, 128), jnp.bfloat16),
            jax.ShapeDtypeStruct((136, 128), jnp.bfloat16),
            jax.ShapeDtypeStruct((128, 128), jnp.bfloat16),
            jax.ShapeDtypeStruct((4, 128, 128), jnp.bfloat16),
        ],
        in_specs=[SMEM, VMEM, ANY],
        out_specs=[VMEM] * 5,
        scratch_shapes=[
            pltpu.VMEM((130 * PITCH, 128), jnp.float32),
            pltpu.VMEM((128, 128, 128), jnp.bfloat16),
            pltpu.VMEM((2, 96, 128), jnp.float32),
            pltpu.VMEM((128 * META, 128), jnp.float32),
            pltpu.VMEM((128, 128), jnp.int32),
            pltpu.VMEM((128, 128), jnp.int32),
            pltpu.SMEM((GROUP, 128), jnp.int32),
            pltpu.SMEM((GROUP, 128), jnp.int32),
            pltpu.SMEM((128, 128), jnp.int32),
            pltpu.SemaphoreType.DMA((3 + CHUNKS,)),
        ],
        compiler_params=pltpu.CompilerParams(vmem_limit_bytes=24 << 20),
        name="scatter",
    )(place, on_chip(got), off_chip(start))


def frame_kernel(place_ref, after_ref, rows_ref, west_ref, east_ref, round_ref, back_ref, own_ref):
    del after_ref
    f32, bf16 = jnp.float32, jnp.bfloat16
    west = west_ref[pl.ds(256, 8), :].astype(f32)
    east = east_ref[pl.ds(128, 8), :].astype(f32)
    for n in range(4):
        tail = jnp.concatenate([west[2 * n : 2 * n + 2], east[n : n + 1], jnp.zeros((5, 128), f32)], axis=0)
        own_ref[n, pl.ds(0, 128), :] = rows_ref[n]
        own_ref[n, pl.ds(128, 8), :] = tail.astype(bf16)
    descends = place_ref[1] < place_ref[2]
    for n in range(2):
        top, bottom = own_ref[n].astype(f32), own_ref[n + 2].astype(f32)
        round_ref[n] = jnp.where(descends, bottom, top).astype(bf16)
        back_ref[n] = jnp.where(descends, top, bottom).astype(bf16)


def frame(place, after, rows, west, east):
    return pl.pallas_call(
        frame_kernel,
        out_shape=[
            jax.ShapeDtypeStruct((2, 136, 128), jnp.bfloat16),
            jax.ShapeDtypeStruct((2, 136, 128), jnp.bfloat16),
            jax.ShapeDtypeStruct((4, 136, 128), jnp.bfloat16),
        ],
        in_specs=[SMEM, ANY] + [VMEM] * 3,
        out_specs=[VMEM] * 3,
        compiler_params=pltpu.CompilerParams(vmem_limit_bytes=4 << 20),
        name="frame",
    )(place, after, rows, west, east)


def inner_kernel(low, field_ref, w1_ref, b1_ref, even_ref, odd_ref, edge_ref, lhs_ref, shift_ref, tail_ref):
    f32, bf16 = jnp.float32, jnp.bfloat16
    bias = jnp.concatenate([b1_ref[...], b1_ref[...]], axis=-1)
    weight = w1_ref[...].reshape(1536, 256)

    def step(b, carry):
        for n in range(ROWS + 2):
            base = pl.multiple_of((low + 1 + b * ROWS + n) * PITCH, 8)
            parts = [field_ref[pl.ds(base + at, 64), :].astype(bf16) for at in (ODD - 1, EVEN, ODD, EVEN + 1)]
            lhs_ref[n] = jnp.concatenate(parts, axis=-1)
        window = jnp.concatenate([lhs_ref[pl.ds(di, ROWS)].reshape(ROWS * 64, 512) for di in range(3)], axis=-1)
        hid = gelu(jnp.dot(window, weight, preferred_element_type=f32) + bias).reshape(ROWS, 64, 256)
        shift_ref[:, pl.ds(8, 64), :] = hid[:, :, 128:]
        tail_ref[...] = hid[:, 56:, :128]
        for n in range(ROWS):
            line = pl.ds(b * ROWS + n, 1)
            edge_ref[0, line, :] = shift_ref[n, pl.ds(8, 1), :]
            edge_ref[1, line, :] = shift_ref[n, pl.ds(70, 1), :]
            edge_ref[2, line, :] = tail_ref[n, pl.ds(7, 1), :]
        wide = jnp.concatenate([shift_ref[:, pl.ds(7, 64), :], hid[:, :, :128], hid[:, :, 128:]], axis=-1)
        wide = wide.astype(bf16).reshape(ROWS // 2, 2, 64, 384)
        even_ref[pl.ds(b * (ROWS // 2), ROWS // 2)] = wide[:, 0]
        odd_ref[pl.ds(b * (ROWS // 2) + 1, ROWS // 2)] = wide[:, 1]
        return carry

    lax.fori_loop(0, 64 // ROWS, step, 0)


def inner(low, field, w1, b1):
    return pl.pallas_call(
        functools.partial(inner_kernel, low),
        out_shape=[
            pltpu.VMEM((32, 64, 384), jnp.bfloat16),
            pltpu.VMEM((33, 64, 384), jnp.bfloat16),
            jax.ShapeDtypeStruct((3, 64, 128), jnp.float32),
        ],
        in_specs=[VMEM] * 3,
        out_specs=[VMEM] * 3,
        scratch_shapes=[pltpu.VMEM((ROWS + 2, 64, 512), jnp.bfloat16), pltpu.VMEM((ROWS, 72, 128), jnp.float32), pltpu.VMEM((ROWS, 8, 128), jnp.float32)],
        compiler_params=pltpu.CompilerParams(vmem_limit_bytes=24 << 20),
        name="inner",
    )(on_chip(field), w1, b1)


def rim_kernel(
    place_ref,
    even0_in,
    odd0_in,
    even1_in,
    odd1_in,
    edge0_ref,
    edge1_ref,
    right_ref,
    left_ref,
    near_ref,
    west_ref,
    east_ref,
    own_ref,
    round_ref,
    back_ref,
    w1_ref,
    w1s_ref,
    b1_ref,
    w2_ref,
    b2_ref,
    even0_ref,
    odd0_ref,
    even1_ref,
    odd1_ref,
    out_ref,
    cols_ref,
    strip_ref,
    shift_ref,
    side_ref,
    ends_ref,
    total_ref,
):
    del even0_in, odd0_in, even1_in, odd1_in
    f32, bf16 = jnp.float32, jnp.bfloat16
    north, south = place_ref[0] == 0, place_ref[0] == 3
    descends = place_ref[1] < place_ref[2]
    dot = functools.partial(jnp.dot, preferred_element_type=f32)
    bias = b1_ref[...]
    bias2 = jnp.concatenate([bias, bias], axis=-1)
    pairs = w1_ref[...].reshape(1536, 256)
    taps1 = w1s_ref[...].reshape(1152, 128)
    taps2 = w2_ref[...].reshape(1152, 128)

    body = (
        west_ref[pl.ds(0, 128), :],
        west_ref[pl.ds(128, 128), :],
        left_ref[pl.ds(0, 128), :],
        near_ref[...],
        right_ref[pl.ds(0, 128), :],
        right_ref[pl.ds(128, 128), :],
        east_ref[pl.ds(0, 128), :],
    )
    for n, col in enumerate(body):
        cols_ref[n, pl.ds(2, 128), :] = col.astype(f32)

    def wide(ref, n):
        return ref[n].astype(f32)

    above = [jnp.where(descends, wide(round_ref, n), wide(back_ref, n)) for n in range(2)]
    beneath = [jnp.where(descends, wide(back_ref, n), wide(round_ref, n)) for n in range(2)]
    second = jnp.where(north, above[1], above[0])
    first = jnp.where(north, above[0], above[1])
    own = [wide(own_ref, n) for n in range(4)]
    below = jnp.where(south, beneath[1], beneath[0])
    top = (jnp.where(north, own[0], second), first, jnp.where(north, second, own[0]))
    for slab, row in ((0, second), (1, first), (130, below)):
        for m, at in enumerate((128, 129, 64, 0, 127, 63, 130)):
            cols_ref[m, pl.ds(slab, 1), :] = row[at : at + 1]

    def lines(n, row):
        strip_ref[n, pl.ds(ODD, 64), :] = row[0:64]
        strip_ref[n, pl.ds(EVEN, 64), :] = row[64:128]
        strip_ref[n, pl.ds(ODD - 1, 1), :] = row[129:130]
        strip_ref[n, pl.ds(EVEN + 64, 1), :] = row[130:131]
        parts = [strip_ref[n, pl.ds(at, 64), :].astype(bf16) for at in (ODD - 1, EVEN, ODD, EVEN + 1)]
        return jnp.concatenate(parts, axis=-1)

    lhs = [lines(n, row) for n, row in enumerate((top[0], first, top[2], *own, below))]
    corner = []
    for row in top:
        corner.append(jnp.zeros((8, 128), f32))
        corner.extend(jnp.broadcast_to(row[at : at + 1], (8, 128)) for at in (128, 129, 64))
    corner = jnp.concatenate(corner, axis=-1).astype(bf16)
    stack = [jnp.concatenate([lhs[n] for n in picks], axis=-1) for picks in ((0, 1, 2), (1, 3, 4), (5, 6, 7))]
    hid = gelu(dot(jnp.concatenate([*stack, corner, corner], axis=0), pairs) + bias2)

    windows = []
    for at in (0, 1, 4):
        parts = [cols_ref[at + m, pl.ds(di, 136), :] for di in range(3) for m in range(3)]
        windows.append(jnp.concatenate(parts, axis=-1))
    cols = gelu(dot(jnp.concatenate(windows, axis=0).astype(bf16), taps1) + bias)
    for n, to in enumerate((0, 1, 5)):
        side_ref[to] = cols[n * 136 : (n + 1) * 136]
    for n in range(3):
        side_ref[n + 2, pl.ds(1, 64), :] = edge0_ref[n]
        side_ref[n + 2, pl.ds(65, 64), :] = edge1_ref[n]
    for n, r in enumerate((-1, 0, 127)):
        here = pl.ds(r + 1, 1)
        even, odd = hid[n * 64 : n * 64 + 64, :128], hid[n * 64 : n * 64 + 64, 128:]
        side_ref[1, here, :] = even[0:1]
        side_ref[2, here, :] = odd[0:1]
        side_ref[3, here, :] = odd[62:63]
        side_ref[4, here, :] = even[63:64]
        side_ref[5, here, :] = odd[63:64]
        shift_ref[pl.ds(8, 64), :] = odd
        line = jnp.concatenate([shift_ref[pl.ds(7, 64), :], even, odd], axis=-1).astype(bf16)
        if r == -1:
            odd0_ref[0] = line
        elif r == 0:
            even0_ref[0] = line
        else:
            odd1_ref[32] = line
    side_ref[0, pl.ds(0, 1), :] = hid[192:193, 128:]
    odd1_ref[0] = odd0_ref[32]

    windows = []
    for at in (0, 3):
        parts = [side_ref[at + m, pl.ds(a, 64, stride=2), :] for a in range(3) for m in range(3)]
        windows.append(jnp.concatenate(parts, axis=-1))
    ends_ref[...] = dot(jnp.concatenate(windows, axis=0).astype(bf16), taps2) + b2_ref[...]

    for half, (even_ref, odd_ref) in enumerate(((even0_ref, odd0_ref), (even1_ref, odd1_ref))):

        def finish(b, carry):
            p = b * 8
            window = jnp.concatenate(
                [
                    odd_ref[pl.ds(p, 8)].reshape(512, 384),
                    even_ref[pl.ds(p, 8)].reshape(512, 384),
                    odd_ref[pl.ds(p + 1, 8)].reshape(512, 384),
                ],
                axis=-1,
            )
            total_ref[...] = (dot(window, taps2) + b2_ref[...]).reshape(8, 64, 128)
            for n in range(8):
                total_ref[n, pl.ds(0, 1), :] = ends_ref[pl.ds(half * 32 + p + n, 1), :]
                total_ref[n, pl.ds(63, 1), :] = ends_ref[pl.ds(64 + half * 32 + p + n, 1), :]
            out_ref[pl.ds(half * 32 + p, 8)] = total_ref[...].astype(bf16)
            return carry

        lax.fori_loop(0, 4, finish, 0)


def rim(place, blocks, *rest):
    return pl.pallas_call(
        rim_kernel,
        out_shape=[pltpu.VMEM(b.shape, b.dtype) for b in blocks] + [jax.ShapeDtypeStruct((64, 64, 128), jnp.bfloat16)],
        in_specs=[SMEM] + [VMEM] * 19,
        out_specs=[VMEM] * 5,
        scratch_shapes=[
            pltpu.VMEM((7, 144, 128), jnp.float32),
            pltpu.VMEM((8, PITCH, 128), jnp.float32),
            pltpu.VMEM((72, 128), jnp.float32),
            pltpu.VMEM((6, 136, 128), jnp.float32),
            pltpu.VMEM((128, 128), jnp.float32),
            pltpu.VMEM((8, 64, 128), jnp.float32),
        ],
        input_output_aliases={1: 0, 2: 1, 3: 2, 4: 3},
        compiler_params=pltpu.CompilerParams(vmem_limit_bytes=20 << 20),
        name="rim",
    )(place, *map(on_chip, blocks), *rest)[4]


def shards(background, values, cells, counts, w1, b1, w2, b2):
    lat, lon = lax.axis_size("lat"), lax.axis_size("lon")
    half = lon // 2
    place = jnp.stack([lax.axis_index("lat"), lax.axis_index("lon"), jnp.int32(half)])
    east_pairs = [(i, (i + 1) % lon) for i in range(lon)]
    west_pairs = [(j, i) for i, j in east_pairs]
    round_pairs = []
    for i in range(half):
        circle = [b * lon + i for b in range(lat)] + [b * lon + i + half for b in reversed(range(lat))]
        round_pairs += zip(circle, circle[1:] + circle[:1])
    back_pairs = [(j, i) for i, j in round_pairs]

    sent = pack(values[0], cells[0].T, counts)
    got = lax.all_to_all(sent, ("lat", "lon"), split_axis=0, concat_axis=0, tiled=True)
    field, right, left, near, rows = scatter(place, got, spread(background))

    flat = w1.reshape(3, 384, 128)
    blank = jnp.zeros((3, 128, 128), jnp.bfloat16)
    paired = jnp.concatenate(
        [jnp.concatenate([flat, blank], axis=1), jnp.concatenate([blank, flat], axis=1)], axis=2
    )
    west = lax.ppermute(right, "lon", east_pairs)
    east = lax.ppermute(left, "lon", west_pairs)
    *upper, upper_edge = inner(0, field, paired, b1[None])
    ahead, behind, own = frame(place, upper_edge, rows, west, east)
    ahead = lax.ppermute(ahead, ("lat", "lon"), round_pairs)
    behind = lax.ppermute(behind, ("lat", "lon"), back_pairs)
    *lower, lower_edge = inner(64, field, paired, b1[None])
    return rim(
        place,
        (*upper, *lower),
        upper_edge,
        lower_edge,
        right,
        left,
        near,
        west,
        east,
        own,
        ahead,
        behind,
        paired,
        flat,
        b1[None],
        w2.reshape(3, 384, 128),
        b2[None],
    )


def solution(mesh):
    placed = (
        P("lat", "lon", None),
        P(("lat", "lon"), None, None, None),
        P(("lat", "lon"), None, None),
        P(("lat", "lon"), None),
        P(),
        P(),
        P(),
        P(),
    )
    return jax.shard_map(
        shards, mesh=mesh, in_specs=placed, out_specs=P("lat", "lon", None), check_vma=False
    )
```

```python
import functools

import jax
import jax.numpy as jnp
from jax import lax
from jax.experimental import pallas as pl
from jax.experimental.pallas import tpu as pltpu
from jax.sharding import PartitionSpec as P

PITCH, ODD, EVEN = 152, 8, 80
SLABS = 131
BATCH = 8
CHUNKS = 4
GROUP = 8
META = 8
ROWS = 16
GELU_A, GELU_B = 0.7978845608028654, 0.044715
VMEM = pl.BlockSpec(memory_space=pltpu.VMEM)
SMEM = pl.BlockSpec(memory_space=pltpu.SMEM)
ANY = pl.BlockSpec(memory_space=pl.ANY)


def on_chip(x):
    return pltpu.with_memory_space_constraint(x, pltpu.VMEM)


def off_chip(x):
    return pltpu.with_memory_space_constraint(x, pltpu.HBM)


def gelu(x):
    return 0.5 * x * (1.0 + jnp.tanh(GELU_A * (x + GELU_B * (x * x * x))))


def pack_kernel(values_ref, cells_ref, counts_ref, out_ref, held_ref, where_ref, live_ref, meta_ref, tail_ref, sem):
    owners, slots = values_ref.shape[0], values_ref.shape[1]
    part = owners // CHUNKS
    numbers = pltpu.make_async_copy(cells_ref, where_ref, sem.at[2 * CHUNKS])
    numbers.start()
    totals = pltpu.make_async_copy(counts_ref, live_ref, sem.at[2 * CHUNKS + 1])
    totals.start()
    arrive, leave = [], []
    for n in range(CHUNKS):
        here = pl.ds(n * part, part)
        arrive.append(
            pltpu.make_async_copy(values_ref.at[here], held_ref.at[here], sem.at[n])
        )
        leave.append(
            pltpu.make_async_copy(
                held_ref.at[here], out_ref.at[here, pl.ds(0, slots), :], sem.at[CHUNKS + n]
            )
        )
        arrive[-1].start()
    for came, goes in zip(arrive, leave):
        came.wait()
        goes.start()
    numbers.wait()
    totals.wait()
    cells = where_ref[...]
    place = lax.broadcasted_iota(jnp.int32, cells.shape, 0)
    live = place < live_ref[...]
    row = cells >> 7
    col = cells & 127
    high = jnp.where(live, row + 2, 0)
    low = jnp.where(live, (col >> 1) + jnp.where((col & 1) == 1, ODD, EVEN), 0)
    marked = jnp.where(live, cells, -1)
    again = jnp.zeros(cells.shape, jnp.int32)
    for back in range(1, BATCH):
        same = (pltpu.roll(marked, back, 0) == marked) & live & (place % BATCH >= back)
        again = jnp.where(same, 1, again)
    again = again.astype(jnp.float32)
    count = jnp.sum(again, axis=0, keepdims=True)
    furthest = jnp.max(again * place.astype(jnp.float32), axis=0, keepdims=True)
    blank = jnp.zeros((128 - slots, owners), jnp.float32)
    notes = jnp.concatenate([count, furthest, count, blank[3:]], axis=0)

    def turned(x, spare):
        return jnp.concatenate([x.astype(jnp.float32), spare], axis=0).T

    meta_ref[pl.ds(0, owners, stride=META), :] = turned(high, blank)
    meta_ref[pl.ds(1, owners, stride=META), :] = turned(low, blank)
    meta_ref[pl.ds(2, owners, stride=META), :] = turned(again, notes)
    for m in range(3, META):
        meta_ref[pl.ds(m, owners, stride=META), :] = jnp.zeros((owners, 128), jnp.float32)
    tail_ref[...] = meta_ref[...].reshape(owners, META, 128).astype(jnp.bfloat16)
    last = pltpu.make_async_copy(tail_ref, out_ref.at[:, pl.ds(slots, META), :], sem.at[2 * CHUNKS + 2])
    last.start()
    for goes in (*leave, last):
        goes.wait()


def pack(values, cells, counts):
    owners, slots, chans = values.shape
    return pl.pallas_call(
        pack_kernel,
        out_shape=pltpu.HBM((owners, slots + META, chans), jnp.bfloat16),
        in_specs=[ANY] * 3,
        out_specs=ANY,
        scratch_shapes=[
            pltpu.VMEM((owners, slots, chans), jnp.bfloat16),
            pltpu.VMEM((slots, owners), jnp.int32),
            pltpu.VMEM((1, owners), jnp.int32),
            pltpu.VMEM((owners * META, chans), jnp.float32),
            pltpu.VMEM((owners, META, chans), jnp.bfloat16),
            pltpu.SemaphoreType.DMA((2 * CHUNKS + 3,)),
        ],
        compiler_params=pltpu.CompilerParams(vmem_limit_bytes=12 << 20),
        name="pack",
    )(off_chip(values), off_chip(cells), off_chip(counts))


def spread_kernel(field_ref, parted_ref, wide_ref):
    def step(r, carry):
        wide_ref[...] = field_ref[r].astype(jnp.float32)
        parted_ref[r, pl.ds(0, 64), :] = wide_ref[pl.ds(1, 64, stride=2), :].astype(jnp.bfloat16)
        parted_ref[r, pl.ds(64, 64), :] = wide_ref[pl.ds(0, 64, stride=2), :].astype(jnp.bfloat16)
        return carry

    lax.fori_loop(0, field_ref.shape[0], step, 0)


def spread(field):
    return pl.pallas_call(
        spread_kernel,
        out_shape=pltpu.HBM(field.shape, field.dtype),
        in_specs=[VMEM],
        out_specs=VMEM,
        scratch_shapes=[pltpu.VMEM((128, 128), jnp.float32)],
        compiler_params=pltpu.CompilerParams(vmem_limit_bytes=12 << 20),
        name="spread",
    )(field)


def scatter_kernel(place_ref, got_ref, parted_ref, acc_ref, other_ref, right_ref, left_ref, near_ref, rows_ref, *rest):
    start_ref, wide_ref, meta_ref, index_ref, late_ref, cells0_ref, cells1_ref, list_ref, sem = rest
    del place_ref
    sources, slots = got_ref.shape[0], got_ref.shape[1] - META
    part = 128 // CHUNKS
    pieces = []
    for n in range(CHUNKS):
        here = pl.ds(n * part, part)
        pieces.append(pltpu.make_async_copy(parted_ref.at[here], start_ref.at[here], sem.at[3 + n]))
        pieces[-1].start()

    def unpack(s, carry):
        meta_ref[pl.ds(pl.multiple_of(s * META, META), META), :] = got_ref[s, pl.ds(slots, META), :].astype(jnp.float32)
        return carry

    lax.fori_loop(0, sources, unpack, 0, unroll=8)
    high = meta_ref[pl.ds(0, sources, stride=META), :]
    low = meta_ref[pl.ds(1, sources, stride=META), :]
    again = meta_ref[pl.ds(2, sources, stride=META), :]
    spot = high * PITCH + low
    index_ref[...] = jnp.where(again > 0, 0.0, spot).astype(jnp.int32)
    lane = lax.broadcasted_iota(jnp.int32, again.shape, 1)
    crowd = jnp.sum(again.reshape(sources // GROUP, GROUP, 128), axis=1, keepdims=True)
    crowd = jnp.broadcast_to(crowd, (sources // GROUP, GROUP, 128)).reshape(sources, 128)
    late = jnp.where(lane < slots, again * spot, jnp.where(lane == slots + 2, crowd, again))
    late_ref[...] = late.astype(jnp.int32)

    cells = (cells0_ref, cells1_ref)

    def fetch(group, half):
        return pltpu.make_async_copy(index_ref.at[pl.ds(group * GROUP, GROUP), :], cells[half], sem.at[half])

    fetch(0, 0).start()
    fetch(1, 1).start()
    listed = pltpu.make_async_copy(late_ref, list_ref, sem.at[2])
    listed.start()

    def clear(r, carry):
        base = pl.multiple_of((r + 2) * PITCH, 8)
        for at, size in ((0, 72), (EVEN, 72)):
            other_ref[pl.ds(base + at, size), :] = jnp.zeros((size, 128), jnp.float32)
        return carry

    lax.fori_loop(0, 128, clear, 0)

    def widen(r, carry):
        base = pl.multiple_of((r + 2) * PITCH, 8)
        for at in (0, EVEN - 8, EVEN + 64):
            acc_ref[pl.ds(base + at, 8), :] = jnp.zeros((8, 128), jnp.float32)
        acc_ref[pl.ds(base + ODD, 64), :] = start_ref[r, pl.ds(0, 64), :].astype(jnp.float32)
        acc_ref[pl.ds(base + EVEN, 64), :] = start_ref[r, pl.ds(64, 64), :].astype(jnp.float32)
        return carry

    for n, piece in enumerate(pieces):
        piece.wait()
        lax.fori_loop(n * part, (n + 1) * part, widen, 0)
    accs = (acc_ref, other_ref)

    def add(step, carry):
        for half in range(2):
            group = step * 2 + half
            fetch(group, half).wait()
            for t in range(GROUP):
                wide = wide_ref.at[t % 2]
                wide[...] = got_ref[group * GROUP + t, pl.ds(0, slots), :].astype(jnp.float32)
                for n, k in enumerate(range(0, slots, BATCH)):
                    acc = accs[n % 2]
                    where = [cells[half][t, k + m] for m in range(BATCH)]
                    sums = [acc[pl.ds(i, 1), :] + wide[pl.ds(k + m, 1), :] for m, i in enumerate(where)]
                    for i, total in zip(where, sums):
                        acc[pl.ds(i, 1), :] = total

            @pl.when(group + 2 < sources // GROUP)
            def _():
                fetch(group + 2, half).start()

        return carry

    lax.fori_loop(0, sources // (2 * GROUP), add, 0)
    listed.wait()

    def rest_of(s, carry):
        repeats = list_ref[s, slots]
        furthest = list_ref[s, slots + 1]

        @pl.when(repeats > 0)
        def _():
            wide_ref[0] = got_ref[s, pl.ds(0, slots), :].astype(jnp.float32)

            def one(k, carry):
                i = list_ref[s, k]

                @pl.when(i > 0)
                def _():
                    acc_ref[pl.ds(i, 1), :] = acc_ref[pl.ds(i, 1), :] + wide_ref[0, pl.ds(k, 1), :]

                return carry

            lax.fori_loop(jnp.where(repeats > 1, 0, furthest), furthest + 1, one, 0)

        return carry

    for group in range(sources // GROUP):

        @pl.when(list_ref[group * GROUP, slots + 2] > 0)
        def _():
            lax.fori_loop(group * GROUP, (group + 1) * GROUP, rest_of, 0)


    def total(start, size, stride=1):
        here = pl.ds(start, size) if stride == 1 else pl.ds(start, size, stride=stride)
        return acc_ref[here, :] + other_ref[here, :]

    bf16 = jnp.bfloat16
    ends = (0, 1, 126, 127)
    for n, at in enumerate((EVEN + 63, ODD + 63)):
        right_ref[pl.ds(n * 128, 128), :] = total(2 * PITCH + at, 128, PITCH).astype(bf16)
    left_ref[pl.ds(0, 128), :] = total(2 * PITCH + EVEN, 128, PITCH).astype(bf16)
    near_ref[...] = total(2 * PITCH + ODD, 128, PITCH).astype(bf16)
    east = [total((r + 2) * PITCH + at, 1) for r in ends for at in (EVEN + 63, ODD + 63)]
    west = [total((r + 2) * PITCH + EVEN, 1) for r in ends]
    right_ref[pl.ds(256, 8), :] = jnp.concatenate(east, axis=0).astype(bf16)
    left_ref[pl.ds(128, 8), :] = jnp.concatenate(west + west, axis=0).astype(bf16)
    for n, r in enumerate(ends):
        base = (r + 2) * PITCH
        rows_ref[n, pl.ds(0, 64), :] = total(base + ODD, 64).astype(bf16)
        rows_ref[n, pl.ds(64, 64), :] = total(base + EVEN, 64).astype(bf16)


def scatter(place, got, start):
    return pl.pallas_call(
        scatter_kernel,
        out_shape=[
            pltpu.VMEM((SLABS * PITCH, 128), jnp.float32),
            pltpu.VMEM((SLABS * PITCH, 128), jnp.float32),
            jax.ShapeDtypeStruct((264, 128), jnp.bfloat16),
            jax.ShapeDtypeStruct((136, 128), jnp.bfloat16),
            jax.ShapeDtypeStruct((128, 128), jnp.bfloat16),
            jax.ShapeDtypeStruct((4, 128, 128), jnp.bfloat16),
        ],
        in_specs=[SMEM, VMEM, ANY],
        out_specs=[VMEM] * 6,
        scratch_shapes=[
            pltpu.VMEM((128, 128, 128), jnp.bfloat16),
            pltpu.VMEM((2, 96, 128), jnp.float32),
            pltpu.VMEM((128 * META, 128), jnp.float32),
            pltpu.VMEM((128, 128), jnp.int32),
            pltpu.VMEM((128, 128), jnp.int32),
            pltpu.SMEM((GROUP, 128), jnp.int32),
            pltpu.SMEM((GROUP, 128), jnp.int32),
            pltpu.SMEM((128, 128), jnp.int32),
            pltpu.SemaphoreType.DMA((3 + CHUNKS,)),
        ],
        compiler_params=pltpu.CompilerParams(vmem_limit_bytes=16 << 20),
        name="scatter",
    )(place, on_chip(got), off_chip(start))


def frame_kernel(place_ref, after_ref, rows_ref, west_ref, east_ref, round_ref, back_ref, own_ref):
    del after_ref
    f32, bf16 = jnp.float32, jnp.bfloat16
    west = west_ref[pl.ds(256, 8), :].astype(f32)
    east = east_ref[pl.ds(128, 8), :].astype(f32)
    for n in range(4):
        tail = jnp.concatenate([west[2 * n : 2 * n + 2], east[n : n + 1], jnp.zeros((5, 128), f32)], axis=0)
        own_ref[n, pl.ds(0, 128), :] = rows_ref[n]
        own_ref[n, pl.ds(128, 8), :] = tail.astype(bf16)
    descends = place_ref[1] < place_ref[2]
    for n in range(2):
        top, bottom = own_ref[n].astype(f32), own_ref[n + 2].astype(f32)
        round_ref[n] = jnp.where(descends, bottom, top).astype(bf16)
        back_ref[n] = jnp.where(descends, top, bottom).astype(bf16)


def frame(place, after, rows, west, east):
    return pl.pallas_call(
        frame_kernel,
        out_shape=[
            jax.ShapeDtypeStruct((2, 136, 128), jnp.bfloat16),
            jax.ShapeDtypeStruct((2, 136, 128), jnp.bfloat16),
            jax.ShapeDtypeStruct((4, 136, 128), jnp.bfloat16),
        ],
        in_specs=[SMEM, ANY] + [VMEM] * 3,
        out_specs=[VMEM] * 3,
        compiler_params=pltpu.CompilerParams(vmem_limit_bytes=4 << 20),
        name="frame",
    )(place, after, rows, west, east)


def inner_kernel(low, field_ref, other_ref, w1_ref, b1_ref, even_ref, odd_ref, edge_ref, lhs_ref, shift_ref, tail_ref):
    f32, bf16 = jnp.float32, jnp.bfloat16
    bias = jnp.concatenate([b1_ref[...], b1_ref[...]], axis=-1)
    weight = w1_ref[...].reshape(1536, 256)

    def step(b, carry):
        for n in range(ROWS + 2):
            base = pl.multiple_of((low + 1 + b * ROWS + n) * PITCH, 8)
            spans = [pl.ds(base + at, 64) for at in (ODD - 1, EVEN, ODD, EVEN + 1)]
            parts = [(field_ref[span, :] + other_ref[span, :]).astype(bf16) for span in spans]
            lhs_ref[n] = jnp.concatenate(parts, axis=-1)
        window = jnp.concatenate([lhs_ref[pl.ds(di, ROWS)].reshape(ROWS * 64, 512) for di in range(3)], axis=-1)
        hid = gelu(jnp.dot(window, weight, preferred_element_type=f32) + bias).reshape(ROWS, 64, 256)
        shift_ref[:, pl.ds(8, 64), :] = hid[:, :, 128:]
        tail_ref[...] = hid[:, 56:, :128]
        for n in range(ROWS):
            line = pl.ds(b * ROWS + n, 1)
            edge_ref[0, line, :] = shift_ref[n, pl.ds(8, 1), :]
            edge_ref[1, line, :] = shift_ref[n, pl.ds(70, 1), :]
            edge_ref[2, line, :] = tail_ref[n, pl.ds(7, 1), :]
        wide = jnp.concatenate([shift_ref[:, pl.ds(7, 64), :], hid[:, :, :128], hid[:, :, 128:]], axis=-1)
        wide = wide.astype(bf16).reshape(ROWS // 2, 2, 64, 384)
        even_ref[pl.ds(b * (ROWS // 2), ROWS // 2)] = wide[:, 0]
        odd_ref[pl.ds(b * (ROWS // 2) + 1, ROWS // 2)] = wide[:, 1]
        return carry

    lax.fori_loop(0, 64 // ROWS, step, 0)


def inner(low, field, other, w1, b1):
    return pl.pallas_call(
        functools.partial(inner_kernel, low),
        out_shape=[
            pltpu.VMEM((32, 64, 384), jnp.bfloat16),
            pltpu.VMEM((33, 64, 384), jnp.bfloat16),
            jax.ShapeDtypeStruct((3, 64, 128), jnp.float32),
        ],
        in_specs=[VMEM] * 4,
        out_specs=[VMEM] * 3,
        scratch_shapes=[pltpu.VMEM((ROWS + 2, 64, 512), jnp.bfloat16), pltpu.VMEM((ROWS, 72, 128), jnp.float32), pltpu.VMEM((ROWS, 8, 128), jnp.float32)],
        compiler_params=pltpu.CompilerParams(vmem_limit_bytes=24 << 20),
        name="inner",
    )(on_chip(field), on_chip(other), w1, b1)


def rim_kernel(
    place_ref,
    even0_in,
    odd0_in,
    even1_in,
    odd1_in,
    edge0_ref,
    edge1_ref,
    right_ref,
    left_ref,
    near_ref,
    west_ref,
    east_ref,
    own_ref,
    round_ref,
    back_ref,
    w1_ref,
    w1s_ref,
    b1_ref,
    w2_ref,
    b2_ref,
    even0_ref,
    odd0_ref,
    even1_ref,
    odd1_ref,
    out_ref,
    cols_ref,
    strip_ref,
    shift_ref,
    side_ref,
    ends_ref,
    total_ref,
):
    del even0_in, odd0_in, even1_in, odd1_in
    f32, bf16 = jnp.float32, jnp.bfloat16
    north, south = place_ref[0] == 0, place_ref[0] == 3
    descends = place_ref[1] < place_ref[2]
    dot = functools.partial(jnp.dot, preferred_element_type=f32)
    bias = b1_ref[...]
    bias2 = jnp.concatenate([bias, bias], axis=-1)
    pairs = w1_ref[...].reshape(1536, 256)
    taps1 = w1s_ref[...].reshape(1152, 128)
    taps2 = w2_ref[...].reshape(1152, 128)

    body = (
        west_ref[pl.ds(0, 128), :],
        west_ref[pl.ds(128, 128), :],
        left_ref[pl.ds(0, 128), :],
        near_ref[...],
        right_ref[pl.ds(0, 128), :],
        right_ref[pl.ds(128, 128), :],
        east_ref[pl.ds(0, 128), :],
    )
    for n, col in enumerate(body):
        cols_ref[n, pl.ds(2, 128), :] = col.astype(f32)

    def wide(ref, n):
        return ref[n].astype(f32)

    above = [jnp.where(descends, wide(round_ref, n), wide(back_ref, n)) for n in range(2)]
    beneath = [jnp.where(descends, wide(back_ref, n), wide(round_ref, n)) for n in range(2)]
    second = jnp.where(north, above[1], above[0])
    first = jnp.where(north, above[0], above[1])
    own = [wide(own_ref, n) for n in range(4)]
    below = jnp.where(south, beneath[1], beneath[0])
    top = (jnp.where(north, own[0], second), first, jnp.where(north, second, own[0]))
    for slab, row in ((0, second), (1, first), (130, below)):
        for m, at in enumerate((128, 129, 64, 0, 127, 63, 130)):
            cols_ref[m, pl.ds(slab, 1), :] = row[at : at + 1]

    def lines(n, row):
        strip_ref[n, pl.ds(ODD, 64), :] = row[0:64]
        strip_ref[n, pl.ds(EVEN, 64), :] = row[64:128]
        strip_ref[n, pl.ds(ODD - 1, 1), :] = row[129:130]
        strip_ref[n, pl.ds(EVEN + 64, 1), :] = row[130:131]
        parts = [strip_ref[n, pl.ds(at, 64), :].astype(bf16) for at in (ODD - 1, EVEN, ODD, EVEN + 1)]
        return jnp.concatenate(parts, axis=-1)

    lhs = [lines(n, row) for n, row in enumerate((top[0], first, top[2], *own, below))]
    corner = []
    for row in top:
        corner.append(jnp.zeros((8, 128), f32))
        corner.extend(jnp.broadcast_to(row[at : at + 1], (8, 128)) for at in (128, 129, 64))
    corner = jnp.concatenate(corner, axis=-1).astype(bf16)
    stack = [jnp.concatenate([lhs[n] for n in picks], axis=-1) for picks in ((0, 1, 2), (1, 3, 4), (5, 6, 7))]
    hid = gelu(dot(jnp.concatenate([*stack, corner, corner], axis=0), pairs) + bias2)

    windows = []
    for at in (0, 1, 4):
        parts = [cols_ref[at + m, pl.ds(di, 136), :] for di in range(3) for m in range(3)]
        windows.append(jnp.concatenate(parts, axis=-1))
    cols = gelu(dot(jnp.concatenate(windows, axis=0).astype(bf16), taps1) + bias)
    for n, to in enumerate((0, 1, 5)):
        side_ref[to] = cols[n * 136 : (n + 1) * 136]
    for n in range(3):
        side_ref[n + 2, pl.ds(1, 64), :] = edge0_ref[n]
        side_ref[n + 2, pl.ds(65, 64), :] = edge1_ref[n]
    for n, r in enumerate((-1, 0, 127)):
        here = pl.ds(r + 1, 1)
        even, odd = hid[n * 64 : n * 64 + 64, :128], hid[n * 64 : n * 64 + 64, 128:]
        side_ref[1, here, :] = even[0:1]
        side_ref[2, here, :] = odd[0:1]
        side_ref[3, here, :] = odd[62:63]
        side_ref[4, here, :] = even[63:64]
        side_ref[5, here, :] = odd[63:64]
        shift_ref[pl.ds(8, 64), :] = odd
        line = jnp.concatenate([shift_ref[pl.ds(7, 64), :], even, odd], axis=-1).astype(bf16)
        if r == -1:
            odd0_ref[0] = line
        elif r == 0:
            even0_ref[0] = line
        else:
            odd1_ref[32] = line
    side_ref[0, pl.ds(0, 1), :] = hid[192:193, 128:]
    odd1_ref[0] = odd0_ref[32]

    windows = []
    for at in (0, 3):
        parts = [side_ref[at + m, pl.ds(a, 64, stride=2), :] for a in range(3) for m in range(3)]
        windows.append(jnp.concatenate(parts, axis=-1))
    ends_ref[...] = dot(jnp.concatenate(windows, axis=0).astype(bf16), taps2) + b2_ref[...]

    for half, (even_ref, odd_ref) in enumerate(((even0_ref, odd0_ref), (even1_ref, odd1_ref))):

        def finish(b, carry):
            p = b * 8
            window = jnp.concatenate(
                [
                    odd_ref[pl.ds(p, 8)].reshape(512, 384),
                    even_ref[pl.ds(p, 8)].reshape(512, 384),
                    odd_ref[pl.ds(p + 1, 8)].reshape(512, 384),
                ],
                axis=-1,
            )
            total_ref[...] = (dot(window, taps2) + b2_ref[...]).reshape(8, 64, 128)
            for n in range(8):
                total_ref[n, pl.ds(0, 1), :] = ends_ref[pl.ds(half * 32 + p + n, 1), :]
                total_ref[n, pl.ds(63, 1), :] = ends_ref[pl.ds(64 + half * 32 + p + n, 1), :]
            out_ref[pl.ds(half * 32 + p, 8)] = total_ref[...].astype(bf16)
            return carry

        lax.fori_loop(0, 4, finish, 0)


def rim(place, blocks, *rest):
    return pl.pallas_call(
        rim_kernel,
        out_shape=[pltpu.VMEM(b.shape, b.dtype) for b in blocks] + [jax.ShapeDtypeStruct((64, 64, 128), jnp.bfloat16)],
        in_specs=[SMEM] + [VMEM] * 19,
        out_specs=[VMEM] * 5,
        scratch_shapes=[
            pltpu.VMEM((7, 144, 128), jnp.float32),
            pltpu.VMEM((8, PITCH, 128), jnp.float32),
            pltpu.VMEM((72, 128), jnp.float32),
            pltpu.VMEM((6, 136, 128), jnp.float32),
            pltpu.VMEM((128, 128), jnp.float32),
            pltpu.VMEM((8, 64, 128), jnp.float32),
        ],
        input_output_aliases={1: 0, 2: 1, 3: 2, 4: 3},
        compiler_params=pltpu.CompilerParams(vmem_limit_bytes=20 << 20),
        name="rim",
    )(place, *map(on_chip, blocks), *rest)[4]


def shards(background, values, cells, counts, w1, b1, w2, b2):
    lat, lon = lax.axis_size("lat"), lax.axis_size("lon")
    half = lon // 2
    place = jnp.stack([lax.axis_index("lat"), lax.axis_index("lon"), jnp.int32(half)])
    east_pairs = [(i, (i + 1) % lon) for i in range(lon)]
    west_pairs = [(j, i) for i, j in east_pairs]
    round_pairs = []
    for i in range(half):
        circle = [b * lon + i for b in range(lat)] + [b * lon + i + half for b in reversed(range(lat))]
        round_pairs += zip(circle, circle[1:] + circle[:1])
    back_pairs = [(j, i) for i, j in round_pairs]

    sent = pack(values[0], cells[0].T, counts)
    got = lax.all_to_all(sent, ("lat", "lon"), split_axis=0, concat_axis=0, tiled=True)
    field, other, right, left, near, rows = scatter(place, got, spread(background))

    flat = w1.reshape(3, 384, 128)
    blank = jnp.zeros((3, 128, 128), jnp.bfloat16)
    paired = jnp.concatenate(
        [jnp.concatenate([flat, blank], axis=1), jnp.concatenate([blank, flat], axis=1)], axis=2
    )
    west = lax.ppermute(right, "lon", east_pairs)
    east = lax.ppermute(left, "lon", west_pairs)
    *upper, upper_edge = inner(0, field, other, paired, b1[None])
    ahead, behind, own = frame(place, upper_edge, rows, west, east)
    ahead = lax.ppermute(ahead, ("lat", "lon"), round_pairs)
    behind = lax.ppermute(behind, ("lat", "lon"), back_pairs)
    *lower, lower_edge = inner(64, field, other, paired, b1[None])
    return rim(
        place,
        (*upper, *lower),
        upper_edge,
        lower_edge,
        right,
        left,
        near,
        west,
        east,
        own,
        ahead,
        behind,
        paired,
        flat,
        b1[None],
        w2.reshape(3, 384, 128),
        b2[None],
    )


def solution(mesh):
    placed = (
        P("lat", "lon", None),
        P(("lat", "lon"), None, None, None),
        P(("lat", "lon"), None, None),
        P(("lat", "lon"), None),
        P(),
        P(),
        P(),
        P(),
    )
    return jax.shard_map(
        shards, mesh=mesh, in_specs=placed, out_specs=P("lat", "lon", None), check_vma=False
    )
```

```python
import functools

import jax
import jax.numpy as jnp
from jax import lax
from jax.experimental import pallas as pl
from jax.experimental.pallas import tpu as pltpu
from jax.sharding import PartitionSpec as P

PITCH, ODD, EVEN = 152, 8, 80
SLABS = 131
BATCH = 8
CHUNKS = 4
GROUP = 8
META = 8
ROWS = 16
GELU_A, GELU_B = 0.7978845608028654, 0.044715
VMEM = pl.BlockSpec(memory_space=pltpu.VMEM)
SMEM = pl.BlockSpec(memory_space=pltpu.SMEM)
ANY = pl.BlockSpec(memory_space=pl.ANY)


def on_chip(x):
    return pltpu.with_memory_space_constraint(x, pltpu.VMEM)


def off_chip(x):
    return pltpu.with_memory_space_constraint(x, pltpu.HBM)


def gelu(x):
    return 0.5 * x * (1.0 + jnp.tanh(GELU_A * (x + GELU_B * (x * x * x))))


def pack_kernel(values_ref, cells_ref, counts_ref, out_ref, held_ref, where_ref, live_ref, meta_ref, tail_ref, sem):
    owners, slots = values_ref.shape[0], values_ref.shape[1]
    part = owners // CHUNKS
    numbers = pltpu.make_async_copy(cells_ref, where_ref, sem.at[2 * CHUNKS])
    numbers.start()
    totals = pltpu.make_async_copy(counts_ref, live_ref, sem.at[2 * CHUNKS + 1])
    totals.start()
    arrive, leave = [], []
    for n in range(CHUNKS):
        here = pl.ds(n * part, part)
        arrive.append(
            pltpu.make_async_copy(values_ref.at[here], held_ref.at[here], sem.at[n])
        )
        leave.append(
            pltpu.make_async_copy(
                held_ref.at[here], out_ref.at[here, pl.ds(0, slots), :], sem.at[CHUNKS + n]
            )
        )
        arrive[-1].start()
    for came, goes in zip(arrive, leave):
        came.wait()
        goes.start()
    numbers.wait()
    totals.wait()
    cells = where_ref[...]
    place = lax.broadcasted_iota(jnp.int32, cells.shape, 0)
    live = place < live_ref[...]
    row = cells >> 7
    col = cells & 127
    high = jnp.where(live, row + 2, 0)
    low = jnp.where(live, (col >> 1) + jnp.where((col & 1) == 1, ODD, EVEN), 0)
    marked = jnp.where(live, cells, -1)
    again = jnp.zeros(cells.shape, jnp.int32)
    for back in range(1, BATCH):
        same = (pltpu.roll(marked, back, 0) == marked) & live & (place % BATCH >= back)
        again = jnp.where(same, 1, again)
    again = again.astype(jnp.float32)
    count = jnp.sum(again, axis=0, keepdims=True)
    furthest = jnp.max(again * place.astype(jnp.float32), axis=0, keepdims=True)
    blank = jnp.zeros((128 - slots, owners), jnp.float32)
    notes = jnp.concatenate([count, furthest, count, blank[3:]], axis=0)

    def turned(x, spare):
        return jnp.concatenate([x.astype(jnp.float32), spare], axis=0).T

    meta_ref[pl.ds(0, owners, stride=META), :] = turned(high, blank)
    meta_ref[pl.ds(1, owners, stride=META), :] = turned(low, blank)
    meta_ref[pl.ds(2, owners, stride=META), :] = turned(again, notes)
    for m in range(3, META):
        meta_ref[pl.ds(m, owners, stride=META), :] = jnp.zeros((owners, 128), jnp.float32)
    tail_ref[...] = meta_ref[...].reshape(owners, META, 128).astype(jnp.bfloat16)
    last = pltpu.make_async_copy(tail_ref, out_ref.at[:, pl.ds(slots, META), :], sem.at[2 * CHUNKS + 2])
    last.start()
    for goes in (*leave, last):
        goes.wait()


def pack(values, cells, counts):
    owners, slots, chans = values.shape
    return pl.pallas_call(
        pack_kernel,
        out_shape=pltpu.HBM((owners, slots + META, chans), jnp.bfloat16),
        in_specs=[ANY] * 3,
        out_specs=ANY,
        scratch_shapes=[
            pltpu.VMEM((owners, slots, chans), jnp.bfloat16),
            pltpu.VMEM((slots, owners), jnp.int32),
            pltpu.VMEM((1, owners), jnp.int32),
            pltpu.VMEM((owners * META, chans), jnp.float32),
            pltpu.VMEM((owners, META, chans), jnp.bfloat16),
            pltpu.SemaphoreType.DMA((2 * CHUNKS + 3,)),
        ],
        compiler_params=pltpu.CompilerParams(vmem_limit_bytes=12 << 20),
        name="pack",
    )(off_chip(values), off_chip(cells), off_chip(counts))


def spread_kernel(field_ref, parted_ref, wide_ref):
    def step(r, carry):
        wide_ref[...] = field_ref[r].astype(jnp.float32)
        parted_ref[r, pl.ds(0, 64), :] = wide_ref[pl.ds(1, 64, stride=2), :].astype(jnp.bfloat16)
        parted_ref[r, pl.ds(64, 64), :] = wide_ref[pl.ds(0, 64, stride=2), :].astype(jnp.bfloat16)
        return carry

    lax.fori_loop(0, field_ref.shape[0], step, 0)


def spread(field):
    return pl.pallas_call(
        spread_kernel,
        out_shape=pltpu.HBM(field.shape, field.dtype),
        in_specs=[VMEM],
        out_specs=VMEM,
        scratch_shapes=[pltpu.VMEM((128, 128), jnp.float32)],
        compiler_params=pltpu.CompilerParams(vmem_limit_bytes=12 << 20),
        name="spread",
    )(field)


def scatter_kernel(place_ref, got_ref, parted_ref, acc_ref, other_ref, right_ref, left_ref, near_ref, rows_ref, *rest):
    start_ref, wide_ref, meta_ref, index_ref, late_ref, cells0_ref, cells1_ref, list_ref, sem = rest
    del place_ref
    sources, slots = got_ref.shape[0], got_ref.shape[1] - META
    part = 128 // CHUNKS
    pieces = []
    for n in range(CHUNKS):
        here = pl.ds(n * part, part)
        pieces.append(pltpu.make_async_copy(parted_ref.at[here], start_ref.at[here], sem.at[3 + n]))
        pieces[-1].start()

    def unpack(s, carry):
        meta_ref[pl.ds(pl.multiple_of(s * META, META), META), :] = got_ref[s, pl.ds(slots, META), :].astype(jnp.float32)
        return carry

    lax.fori_loop(0, sources, unpack, 0, unroll=8)
    high = meta_ref[pl.ds(0, sources, stride=META), :]
    low = meta_ref[pl.ds(1, sources, stride=META), :]
    again = meta_ref[pl.ds(2, sources, stride=META), :]
    spot = high * PITCH + low
    index_ref[...] = jnp.where(again > 0, 0.0, spot).astype(jnp.int32)
    lane = lax.broadcasted_iota(jnp.int32, again.shape, 1)
    crowd = jnp.sum(again.reshape(sources // GROUP, GROUP, 128), axis=1, keepdims=True)
    crowd = jnp.broadcast_to(crowd, (sources // GROUP, GROUP, 128)).reshape(sources, 128)
    late = jnp.where(lane < slots, again * spot, jnp.where(lane == slots + 2, crowd, again))
    late_ref[...] = late.astype(jnp.int32)

    cells = (cells0_ref, cells1_ref)

    def fetch(group, half):
        return pltpu.make_async_copy(index_ref.at[pl.ds(group * GROUP, GROUP), :], cells[half], sem.at[half])

    fetch(0, 0).start()
    fetch(1, 1).start()
    listed = pltpu.make_async_copy(late_ref, list_ref, sem.at[2])
    listed.start()

    def clear(r, carry):
        base = pl.multiple_of((r + 2) * PITCH, 8)
        for at, size in ((0, 72), (EVEN, 72)):
            other_ref[pl.ds(base + at, size), :] = jnp.zeros((size, 128), jnp.float32)
        return carry

    lax.fori_loop(0, 128, clear, 0)

    def widen(r, carry):
        base = pl.multiple_of((r + 2) * PITCH, 8)
        for at in (0, EVEN - 8, EVEN + 64):
            acc_ref[pl.ds(base + at, 8), :] = jnp.zeros((8, 128), jnp.float32)
        acc_ref[pl.ds(base + ODD, 64), :] = start_ref[r, pl.ds(0, 64), :].astype(jnp.float32)
        acc_ref[pl.ds(base + EVEN, 64), :] = start_ref[r, pl.ds(64, 64), :].astype(jnp.float32)
        return carry

    for n, piece in enumerate(pieces):
        piece.wait()
        lax.fori_loop(n * part, (n + 1) * part, widen, 0)
    accs = (acc_ref, other_ref)

    def add(step, carry):
        for half in range(2):
            group = step * 2 + half
            fetch(group, half).wait()
            for t in range(GROUP):
                wide = wide_ref.at[t % 2]
                wide[...] = got_ref[group * GROUP + t, pl.ds(0, slots), :].astype(jnp.float32)
                for n, k in enumerate(range(0, slots, BATCH)):
                    acc = accs[n % 2]
                    where = [cells[half][t, k + m] for m in range(BATCH)]
                    sums = [acc[pl.ds(i, 1), :] + wide[pl.ds(k + m, 1), :] for m, i in enumerate(where)]
                    for i, total in zip(where, sums):
                        acc[pl.ds(i, 1), :] = total

            @pl.when(group + 2 < sources // GROUP)
            def _():
                fetch(group + 2, half).start()

        return carry

    lax.fori_loop(0, sources // (2 * GROUP), add, 0)
    listed.wait()

    def rest_of(s, carry):
        repeats = list_ref[s, slots]
        furthest = list_ref[s, slots + 1]

        @pl.when(repeats > 0)
        def _():
            wide_ref[0] = got_ref[s, pl.ds(0, slots), :].astype(jnp.float32)

            def one(k, carry):
                i = list_ref[s, k]

                @pl.when(i > 0)
                def _():
                    acc_ref[pl.ds(i, 1), :] = acc_ref[pl.ds(i, 1), :] + wide_ref[0, pl.ds(k, 1), :]

                return carry

            lax.fori_loop(jnp.where(repeats > 1, 0, furthest), furthest + 1, one, 0)

        return carry

    for group in range(sources // GROUP):

        @pl.when(list_ref[group * GROUP, slots + 2] > 0)
        def _():
            lax.fori_loop(group * GROUP, (group + 1) * GROUP, rest_of, 0)


    def total(start, size, stride=1):
        here = pl.ds(start, size) if stride == 1 else pl.ds(start, size, stride=stride)
        return acc_ref[here, :] + other_ref[here, :]

    bf16 = jnp.bfloat16
    ends = (0, 1, 126, 127)
    for n, at in enumerate((EVEN + 63, ODD + 63)):
        right_ref[pl.ds(n * 128, 128), :] = total(2 * PITCH + at, 128, PITCH).astype(bf16)
    left_ref[pl.ds(0, 128), :] = total(2 * PITCH + EVEN, 128, PITCH).astype(bf16)
    near_ref[...] = total(2 * PITCH + ODD, 128, PITCH).astype(bf16)
    east = [total((r + 2) * PITCH + at, 1) for r in ends for at in (EVEN + 63, ODD + 63)]
    west = [total((r + 2) * PITCH + EVEN, 1) for r in ends]
    right_ref[pl.ds(256, 8), :] = jnp.concatenate(east, axis=0).astype(bf16)
    left_ref[pl.ds(128, 8), :] = jnp.concatenate(west + west, axis=0).astype(bf16)
    for n, r in enumerate(ends):
        base = (r + 2) * PITCH
        rows_ref[n, pl.ds(0, 64), :] = total(base + ODD, 64).astype(bf16)
        rows_ref[n, pl.ds(64, 64), :] = total(base + EVEN, 64).astype(bf16)


def scatter(place, got, start):
    return pl.pallas_call(
        scatter_kernel,
        out_shape=[
            pltpu.VMEM((SLABS * PITCH, 128), jnp.float32),
            pltpu.VMEM((SLABS * PITCH, 128), jnp.float32),
            jax.ShapeDtypeStruct((264, 128), jnp.bfloat16),
            jax.ShapeDtypeStruct((136, 128), jnp.bfloat16),
            jax.ShapeDtypeStruct((128, 128), jnp.bfloat16),
            jax.ShapeDtypeStruct((4, 128, 128), jnp.bfloat16),
        ],
        in_specs=[SMEM, VMEM, ANY],
        out_specs=[VMEM] * 6,
        scratch_shapes=[
            pltpu.VMEM((128, 128, 128), jnp.bfloat16),
            pltpu.VMEM((2, 96, 128), jnp.float32),
            pltpu.VMEM((128 * META, 128), jnp.float32),
            pltpu.VMEM((128, 128), jnp.int32),
            pltpu.VMEM((128, 128), jnp.int32),
            pltpu.SMEM((GROUP, 128), jnp.int32),
            pltpu.SMEM((GROUP, 128), jnp.int32),
            pltpu.SMEM((128, 128), jnp.int32),
            pltpu.SemaphoreType.DMA((3 + CHUNKS,)),
        ],
        compiler_params=pltpu.CompilerParams(vmem_limit_bytes=16 << 20),
        name="scatter",
    )(place, on_chip(got), off_chip(start))


def frame_kernel(place_ref, after_ref, rows_ref, west_ref, east_ref, round_ref, back_ref, own_ref):
    del after_ref
    f32, bf16 = jnp.float32, jnp.bfloat16
    west = west_ref[pl.ds(256, 8), :].astype(f32)
    east = east_ref[pl.ds(128, 8), :].astype(f32)
    for n in range(4):
        tail = jnp.concatenate([west[2 * n : 2 * n + 2], east[n : n + 1], jnp.zeros((5, 128), f32)], axis=0)
        own_ref[n, pl.ds(0, 128), :] = rows_ref[n]
        own_ref[n, pl.ds(128, 8), :] = tail.astype(bf16)
    descends = place_ref[1] < place_ref[2]
    for n in range(2):
        top, bottom = own_ref[n].astype(f32), own_ref[n + 2].astype(f32)
        round_ref[n] = jnp.where(descends, bottom, top).astype(bf16)
        back_ref[n] = jnp.where(descends, top, bottom).astype(bf16)


def frame(place, after, rows, west, east):
    return pl.pallas_call(
        frame_kernel,
        out_shape=[
            jax.ShapeDtypeStruct((2, 136, 128), jnp.bfloat16),
            jax.ShapeDtypeStruct((2, 136, 128), jnp.bfloat16),
            jax.ShapeDtypeStruct((4, 136, 128), jnp.bfloat16),
        ],
        in_specs=[SMEM, ANY] + [VMEM] * 3,
        out_specs=[VMEM] * 3,
        compiler_params=pltpu.CompilerParams(vmem_limit_bytes=4 << 20),
        name="frame",
    )(place, after, rows, west, east)


def inner_kernel(low, field_ref, other_ref, w1_ref, b1_ref, even_ref, odd_ref, edge_ref, lhs_ref, shift_ref, tail_ref):
    f32, bf16 = jnp.float32, jnp.bfloat16
    bias = jnp.concatenate([b1_ref[...], b1_ref[...]], axis=-1)
    weight = w1_ref[...].reshape(1536, 256)

    def step(b, carry):
        for n in range(ROWS + 2):
            base = pl.multiple_of((low + 1 + b * ROWS + n) * PITCH, 8)
            spans = [pl.ds(base + at, 64) for at in (ODD - 1, EVEN, ODD, EVEN + 1)]
            parts = [(field_ref[span, :] + other_ref[span, :]).astype(bf16) for span in spans]
            lhs_ref[n] = jnp.concatenate(parts, axis=-1)
        window = jnp.concatenate([lhs_ref[pl.ds(di, ROWS)].reshape(ROWS * 64, 512) for di in range(3)], axis=-1)
        hid = gelu(jnp.dot(window, weight, preferred_element_type=f32) + bias).reshape(ROWS, 64, 256)
        shift_ref[:, pl.ds(8, 64), :] = hid[:, :, 128:]
        tail_ref[...] = hid[:, 56:, :128]
        for n in range(ROWS):
            line = pl.ds(b * ROWS + n, 1)
            edge_ref[0, line, :] = shift_ref[n, pl.ds(8, 1), :]
            edge_ref[1, line, :] = shift_ref[n, pl.ds(70, 1), :]
            edge_ref[2, line, :] = tail_ref[n, pl.ds(7, 1), :]
        wide = jnp.concatenate([shift_ref[:, pl.ds(7, 64), :], hid[:, :, :128], hid[:, :, 128:]], axis=-1)
        wide = wide.astype(bf16).reshape(ROWS // 2, 2, 64, 384)
        even_ref[pl.ds(b * (ROWS // 2), ROWS // 2)] = wide[:, 0]
        odd_ref[pl.ds(b * (ROWS // 2) + 1, ROWS // 2)] = wide[:, 1]
        return carry

    lax.fori_loop(0, 64 // ROWS, step, 0)


def inner(low, field, other, w1, b1):
    return pl.pallas_call(
        functools.partial(inner_kernel, low),
        out_shape=[
            pltpu.VMEM((32, 64, 384), jnp.bfloat16),
            pltpu.VMEM((33, 64, 384), jnp.bfloat16),
            jax.ShapeDtypeStruct((3, 64, 128), jnp.float32),
        ],
        in_specs=[VMEM] * 4,
        out_specs=[VMEM] * 3,
        scratch_shapes=[pltpu.VMEM((ROWS + 2, 64, 512), jnp.bfloat16), pltpu.VMEM((ROWS, 72, 128), jnp.float32), pltpu.VMEM((ROWS, 8, 128), jnp.float32)],
        compiler_params=pltpu.CompilerParams(vmem_limit_bytes=24 << 20),
        name="inner",
    )(on_chip(field), on_chip(other), w1, b1)


def rim_kernel(
    place_ref,
    even0_in,
    odd0_in,
    even1_in,
    odd1_in,
    edge0_ref,
    edge1_ref,
    right_ref,
    left_ref,
    near_ref,
    west_ref,
    east_ref,
    own_ref,
    round_ref,
    back_ref,
    w1_ref,
    w1s_ref,
    b1_ref,
    w2_ref,
    b2_ref,
    even0_ref,
    odd0_ref,
    even1_ref,
    odd1_ref,
    out_ref,
    cols_ref,
    strip_ref,
    shift_ref,
    side_ref,
    ends_ref,
    total_ref,
):
    del even0_in, odd0_in, even1_in, odd1_in
    f32, bf16 = jnp.float32, jnp.bfloat16
    north, south = place_ref[0] == 0, place_ref[0] == 3
    descends = place_ref[1] < place_ref[2]
    dot = functools.partial(jnp.dot, preferred_element_type=f32)
    bias = b1_ref[...]
    bias2 = jnp.concatenate([bias, bias], axis=-1)
    pairs = w1_ref[...].reshape(1536, 256)
    taps1 = w1s_ref[...].reshape(1152, 128)
    taps2 = w2_ref[...].reshape(1152, 128)

    def second_layer(b):
        even_ref, odd_ref = ((even0_ref, odd0_ref), (even1_ref, odd1_ref))[b // 4]
        p = b % 4 * 8
        window = [
            odd_ref[pl.ds(p, 8)].reshape(512, 384),
            even_ref[pl.ds(p, 8)].reshape(512, 384),
            odd_ref[pl.ds(p + 1, 8)].reshape(512, 384),
        ]
        total = dot(jnp.concatenate(window, axis=-1), taps2) + b2_ref[...]
        total_ref[pl.ds(b * 8, 8)] = total.reshape(8, 64, 128)

    odd1_ref[0] = odd0_ref[32]
    second_layer(1)

    body = (
        west_ref[pl.ds(0, 128), :],
        west_ref[pl.ds(128, 128), :],
        left_ref[pl.ds(0, 128), :],
        near_ref[...],
        right_ref[pl.ds(0, 128), :],
        right_ref[pl.ds(128, 128), :],
        east_ref[pl.ds(0, 128), :],
    )
    for n, col in enumerate(body):
        cols_ref[n, pl.ds(2, 128), :] = col.astype(f32)

    def wide(ref, n):
        return ref[n].astype(f32)

    above = [jnp.where(descends, wide(round_ref, n), wide(back_ref, n)) for n in range(2)]
    beneath = [jnp.where(descends, wide(back_ref, n), wide(round_ref, n)) for n in range(2)]
    second = jnp.where(north, above[1], above[0])
    first = jnp.where(north, above[0], above[1])
    own = [wide(own_ref, n) for n in range(4)]
    below = jnp.where(south, beneath[1], beneath[0])
    top = (jnp.where(north, own[0], second), first, jnp.where(north, second, own[0]))
    for slab, row in ((0, second), (1, first), (130, below)):
        for m, at in enumerate((128, 129, 64, 0, 127, 63, 130)):
            cols_ref[m, pl.ds(slab, 1), :] = row[at : at + 1]

    def lines(n, row):
        strip_ref[n, pl.ds(ODD, 64), :] = row[0:64]
        strip_ref[n, pl.ds(EVEN, 64), :] = row[64:128]
        strip_ref[n, pl.ds(ODD - 1, 1), :] = row[129:130]
        strip_ref[n, pl.ds(EVEN + 64, 1), :] = row[130:131]
        parts = [strip_ref[n, pl.ds(at, 64), :].astype(bf16) for at in (ODD - 1, EVEN, ODD, EVEN + 1)]
        return jnp.concatenate(parts, axis=-1)

    lhs = [lines(n, row) for n, row in enumerate((top[0], first, top[2], *own, below))]
    corner = []
    for row in top:
        corner.append(jnp.zeros((8, 128), f32))
        corner.extend(jnp.broadcast_to(row[at : at + 1], (8, 128)) for at in (128, 129, 64))
    corner = jnp.concatenate(corner, axis=-1).astype(bf16)
    stack = [jnp.concatenate([lhs[n] for n in picks], axis=-1) for picks in ((0, 1, 2), (1, 3, 4), (5, 6, 7))]
    second_layer(2)
    hid = gelu(dot(jnp.concatenate([*stack, corner, corner], axis=0), pairs) + bias2)

    windows = []
    for at in (0, 1, 4):
        parts = [cols_ref[at + m, pl.ds(di, 136), :] for di in range(3) for m in range(3)]
        windows.append(jnp.concatenate(parts, axis=-1))
    cols = gelu(dot(jnp.concatenate(windows, axis=0).astype(bf16), taps1) + bias)
    second_layer(3)
    for n, to in enumerate((0, 1, 5)):
        side_ref[to] = cols[n * 136 : (n + 1) * 136]
    for n in range(3):
        side_ref[n + 2, pl.ds(1, 64), :] = edge0_ref[n]
        side_ref[n + 2, pl.ds(65, 64), :] = edge1_ref[n]
    for n, r in enumerate((-1, 0, 127)):
        here = pl.ds(r + 1, 1)
        even, odd = hid[n * 64 : n * 64 + 64, :128], hid[n * 64 : n * 64 + 64, 128:]
        side_ref[1, here, :] = even[0:1]
        side_ref[2, here, :] = odd[0:1]
        side_ref[3, here, :] = odd[62:63]
        side_ref[4, here, :] = even[63:64]
        side_ref[5, here, :] = odd[63:64]
        shift_ref[pl.ds(8, 64), :] = odd
        line = jnp.concatenate([shift_ref[pl.ds(7, 64), :], even, odd], axis=-1).astype(bf16)
        if r == -1:
            odd0_ref[0] = line
        elif r == 0:
            even0_ref[0] = line
        else:
            odd1_ref[32] = line
    side_ref[0, pl.ds(0, 1), :] = hid[192:193, 128:]
    second_layer(4)

    windows = []
    for at in (0, 3):
        parts = [side_ref[at + m, pl.ds(a, 64, stride=2), :] for a in range(3) for m in range(3)]
        windows.append(jnp.concatenate(parts, axis=-1))
    ends_ref[...] = dot(jnp.concatenate(windows, axis=0).astype(bf16), taps2) + b2_ref[...]

    for b in (5, 6, 0, 7):
        second_layer(b)

    def finish(p, carry):
        total_ref[p, pl.ds(0, 1), :] = ends_ref[pl.ds(p, 1), :]
        total_ref[p, pl.ds(63, 1), :] = ends_ref[pl.ds(64 + p, 1), :]
        out_ref[p] = total_ref[p].astype(bf16)
        return carry

    lax.fori_loop(0, 64, finish, 0, unroll=8)


def rim(place, blocks, *rest):
    return pl.pallas_call(
        rim_kernel,
        out_shape=[pltpu.VMEM(b.shape, b.dtype) for b in blocks] + [jax.ShapeDtypeStruct((64, 64, 128), jnp.bfloat16)],
        in_specs=[SMEM] + [VMEM] * 19,
        out_specs=[VMEM] * 5,
        scratch_shapes=[
            pltpu.VMEM((7, 144, 128), jnp.float32),
            pltpu.VMEM((8, PITCH, 128), jnp.float32),
            pltpu.VMEM((72, 128), jnp.float32),
            pltpu.VMEM((6, 136, 128), jnp.float32),
            pltpu.VMEM((128, 128), jnp.float32),
            pltpu.VMEM((64, 64, 128), jnp.float32),
        ],
        input_output_aliases={1: 0, 2: 1, 3: 2, 4: 3},
        compiler_params=pltpu.CompilerParams(vmem_limit_bytes=20 << 20),
        name="rim",
    )(place, *map(on_chip, blocks), *rest)[4]


def shards(background, values, cells, counts, w1, b1, w2, b2):
    lat, lon = lax.axis_size("lat"), lax.axis_size("lon")
    half = lon // 2
    place = jnp.stack([lax.axis_index("lat"), lax.axis_index("lon"), jnp.int32(half)])
    east_pairs = [(i, (i + 1) % lon) for i in range(lon)]
    west_pairs = [(j, i) for i, j in east_pairs]
    round_pairs = []
    for i in range(half):
        circle = [b * lon + i for b in range(lat)] + [b * lon + i + half for b in reversed(range(lat))]
        round_pairs += zip(circle, circle[1:] + circle[:1])
    back_pairs = [(j, i) for i, j in round_pairs]

    sent = pack(values[0], cells[0].T, counts)
    got = lax.all_to_all(sent, ("lat", "lon"), split_axis=0, concat_axis=0, tiled=True)
    field, other, right, left, near, rows = scatter(place, got, spread(background))

    flat = w1.reshape(3, 384, 128)
    blank = jnp.zeros((3, 128, 128), jnp.bfloat16)
    paired = jnp.concatenate(
        [jnp.concatenate([flat, blank], axis=1), jnp.concatenate([blank, flat], axis=1)], axis=2
    )
    west = lax.ppermute(right, "lon", east_pairs)
    east = lax.ppermute(left, "lon", west_pairs)
    *upper, upper_edge = inner(0, field, other, paired, b1[None])
    ahead, behind, own = frame(place, upper_edge, rows, west, east)
    ahead = lax.ppermute(ahead, ("lat", "lon"), round_pairs)
    behind = lax.ppermute(behind, ("lat", "lon"), back_pairs)
    *lower, lower_edge = inner(64, field, other, paired, b1[None])
    return rim(
        place,
        (*upper, *lower),
        upper_edge,
        lower_edge,
        right,
        left,
        near,
        west,
        east,
        own,
        ahead,
        behind,
        paired,
        flat,
        b1[None],
        w2.reshape(3, 384, 128),
        b2[None],
    )


def solution(mesh):
    placed = (
        P("lat", "lon", None),
        P(("lat", "lon"), None, None, None),
        P(("lat", "lon"), None, None),
        P(("lat", "lon"), None),
        P(),
        P(),
        P(),
        P(),
    )
    return jax.shard_map(
        shards, mesh=mesh, in_specs=placed, out_specs=P("lat", "lon", None), check_vma=False
    )
```

```python
import functools

import jax
import jax.numpy as jnp
from jax import lax
from jax.experimental import pallas as pl
from jax.experimental.pallas import tpu as pltpu
from jax.sharding import PartitionSpec as P

PITCH, ODD, EVEN = 152, 8, 80
SLABS = 131
BATCH = 8
CHUNKS = 4
GROUP = 8
META = 8
ROWS = 16
GELU_A, GELU_B = 0.7978845608028654, 0.044715
VMEM = pl.BlockSpec(memory_space=pltpu.VMEM)
SMEM = pl.BlockSpec(memory_space=pltpu.SMEM)
ANY = pl.BlockSpec(memory_space=pl.ANY)


def on_chip(x):
    return pltpu.with_memory_space_constraint(x, pltpu.VMEM)


def off_chip(x):
    return pltpu.with_memory_space_constraint(x, pltpu.HBM)


def gelu(x):
    return 0.5 * x * (1.0 + jnp.tanh(GELU_A * (x + GELU_B * (x * x * x))))


def pack_kernel(values_ref, cells_ref, counts_ref, out_ref, held_ref, where_ref, live_ref, meta_ref, tail_ref, sem):
    owners, slots = values_ref.shape[0], values_ref.shape[1]
    part = owners // CHUNKS
    numbers = pltpu.make_async_copy(cells_ref, where_ref, sem.at[2 * CHUNKS])
    numbers.start()
    totals = pltpu.make_async_copy(counts_ref, live_ref, sem.at[2 * CHUNKS + 1])
    totals.start()
    arrive, leave = [], []
    for n in range(CHUNKS):
        here = pl.ds(n * part, part)
        arrive.append(
            pltpu.make_async_copy(values_ref.at[here], held_ref.at[here], sem.at[n])
        )
        leave.append(
            pltpu.make_async_copy(
                held_ref.at[here], out_ref.at[here, pl.ds(0, slots), :], sem.at[CHUNKS + n]
            )
        )
        arrive[-1].start()
    for came, goes in zip(arrive, leave):
        came.wait()
        goes.start()
    numbers.wait()
    totals.wait()
    cells = where_ref[...]
    place = lax.broadcasted_iota(jnp.int32, cells.shape, 0)
    live = place < live_ref[...]
    row = cells >> 7
    col = cells & 127
    high = jnp.where(live, row + 2, 0)
    low = jnp.where(live, (col >> 1) + jnp.where((col & 1) == 1, ODD, EVEN), 0)
    marked = jnp.where(live, cells, -1)
    again = jnp.zeros(cells.shape, jnp.int32)
    for back in range(1, BATCH):
        same = (pltpu.roll(marked, back, 0) == marked) & live & (place % BATCH >= back)
        again = jnp.where(same, 1, again)
    again = again.astype(jnp.float32)
    count = jnp.sum(again, axis=0, keepdims=True)
    furthest = jnp.max(again * place.astype(jnp.float32), axis=0, keepdims=True)
    blank = jnp.zeros((128 - slots, owners), jnp.float32)
    notes = jnp.concatenate([count, furthest, count, blank[3:]], axis=0)

    def turned(x, spare):
        return jnp.concatenate([x.astype(jnp.float32), spare], axis=0).T

    meta_ref[pl.ds(0, owners, stride=META), :] = turned(high, blank)
    meta_ref[pl.ds(1, owners, stride=META), :] = turned(low, blank)
    meta_ref[pl.ds(2, owners, stride=META), :] = turned(again, notes)
    for m in range(3, META):
        meta_ref[pl.ds(m, owners, stride=META), :] = jnp.zeros((owners, 128), jnp.float32)
    tail_ref[...] = meta_ref[...].reshape(owners, META, 128).astype(jnp.bfloat16)
    last = pltpu.make_async_copy(tail_ref, out_ref.at[:, pl.ds(slots, META), :], sem.at[2 * CHUNKS + 2])
    last.start()
    for goes in (*leave, last):
        goes.wait()


def pack(values, cells, counts):
    owners, slots, chans = values.shape
    return pl.pallas_call(
        pack_kernel,
        out_shape=pltpu.HBM((owners, slots + META, chans), jnp.bfloat16),
        in_specs=[ANY] * 3,
        out_specs=ANY,
        scratch_shapes=[
            pltpu.VMEM((owners, slots, chans), jnp.bfloat16),
            pltpu.VMEM((slots, owners), jnp.int32),
            pltpu.VMEM((1, owners), jnp.int32),
            pltpu.VMEM((owners * META, chans), jnp.float32),
            pltpu.VMEM((owners, META, chans), jnp.bfloat16),
            pltpu.SemaphoreType.DMA((2 * CHUNKS + 3,)),
        ],
        compiler_params=pltpu.CompilerParams(vmem_limit_bytes=12 << 20),
        name="pack",
    )(off_chip(values), off_chip(cells), off_chip(counts))


def spread_kernel(field_ref, parted_ref, wide_ref):
    def step(r, carry):
        wide_ref[...] = field_ref[r].astype(jnp.float32)
        parted_ref[r, pl.ds(0, 64), :] = wide_ref[pl.ds(1, 64, stride=2), :].astype(jnp.bfloat16)
        parted_ref[r, pl.ds(64, 64), :] = wide_ref[pl.ds(0, 64, stride=2), :].astype(jnp.bfloat16)
        return carry

    lax.fori_loop(0, field_ref.shape[0], step, 0)


def spread(field):
    return pl.pallas_call(
        spread_kernel,
        out_shape=pltpu.HBM(field.shape, field.dtype),
        in_specs=[VMEM],
        out_specs=VMEM,
        scratch_shapes=[pltpu.VMEM((128, 128), jnp.float32)],
        compiler_params=pltpu.CompilerParams(vmem_limit_bytes=12 << 20),
        name="spread",
    )(field)


def scatter_kernel(place_ref, got_ref, parted_ref, acc_ref, other_ref, right_ref, left_ref, near_ref, rows_ref, *rest):
    start_ref, wide_ref, meta_ref, index_ref, late_ref, cells0_ref, cells1_ref, list_ref, sem = rest
    del place_ref
    sources, slots = got_ref.shape[0], got_ref.shape[1] - META
    part = 128 // CHUNKS
    pieces = []
    for n in range(CHUNKS):
        here = pl.ds(n * part, part)
        pieces.append(pltpu.make_async_copy(parted_ref.at[here], start_ref.at[here], sem.at[3 + n]))
        pieces[-1].start()

    def unpack(s, carry):
        meta_ref[pl.ds(pl.multiple_of(s * META, META), META), :] = got_ref[s, pl.ds(slots, META), :].astype(jnp.float32)
        return carry

    lax.fori_loop(0, sources, unpack, 0, unroll=8)
    high = meta_ref[pl.ds(0, sources, stride=META), :]
    low = meta_ref[pl.ds(1, sources, stride=META), :]
    again = meta_ref[pl.ds(2, sources, stride=META), :]
    spot = high * PITCH + low
    index_ref[...] = jnp.where(again > 0, 0.0, spot).astype(jnp.int32)
    lane = lax.broadcasted_iota(jnp.int32, again.shape, 1)
    crowd = jnp.sum(again.reshape(sources // GROUP, GROUP, 128), axis=1, keepdims=True)
    crowd = jnp.broadcast_to(crowd, (sources // GROUP, GROUP, 128)).reshape(sources, 128)
    late = jnp.where(lane < slots, again * spot, jnp.where(lane == slots + 2, crowd, again))
    late_ref[...] = late.astype(jnp.int32)

    cells = (cells0_ref, cells1_ref)

    def fetch(group, half):
        return pltpu.make_async_copy(index_ref.at[pl.ds(group * GROUP, GROUP), :], cells[half], sem.at[half])

    fetch(0, 0).start()
    fetch(1, 1).start()
    listed = pltpu.make_async_copy(late_ref, list_ref, sem.at[2])
    listed.start()

    def clear(r, carry):
        base = pl.multiple_of((r + 2) * PITCH, 8)
        for at, size in ((0, 72), (EVEN, 72)):
            other_ref[pl.ds(base + at, size), :] = jnp.zeros((size, 128), jnp.float32)
        return carry

    lax.fori_loop(0, 128, clear, 0)

    def widen(r, carry):
        base = pl.multiple_of((r + 2) * PITCH, 8)
        for at in (0, EVEN - 8, EVEN + 64):
            acc_ref[pl.ds(base + at, 8), :] = jnp.zeros((8, 128), jnp.float32)
        acc_ref[pl.ds(base + ODD, 64), :] = start_ref[r, pl.ds(0, 64), :].astype(jnp.float32)
        acc_ref[pl.ds(base + EVEN, 64), :] = start_ref[r, pl.ds(64, 64), :].astype(jnp.float32)
        return carry

    for n, piece in enumerate(pieces):
        piece.wait()
        lax.fori_loop(n * part, (n + 1) * part, widen, 0)
    accs = (acc_ref, other_ref)

    def add(step, carry):
        for half in range(2):
            group = step * 2 + half
            fetch(group, half).wait()
            for t in range(GROUP):
                wide = wide_ref.at[t % 2]
                wide[...] = got_ref[group * GROUP + t, pl.ds(0, slots), :].astype(jnp.float32)
                for n, k in enumerate(range(0, slots, BATCH)):
                    acc = accs[n % 2]
                    where = [cells[half][t, k + m] for m in range(BATCH)]
                    sums = [acc[pl.ds(i, 1), :] + wide[pl.ds(k + m, 1), :] for m, i in enumerate(where)]
                    for i, total in zip(where, sums):
                        acc[pl.ds(i, 1), :] = total

            @pl.when(group + 2 < sources // GROUP)
            def _():
                fetch(group + 2, half).start()

        return carry

    lax.fori_loop(0, sources // (2 * GROUP), add, 0)
    listed.wait()

    def rest_of(s, carry):
        repeats = list_ref[s, slots]
        furthest = list_ref[s, slots + 1]

        @pl.when(repeats > 0)
        def _():
            wide_ref[0] = got_ref[s, pl.ds(0, slots), :].astype(jnp.float32)

            def one(k, carry):
                i = list_ref[s, k]

                @pl.when(i > 0)
                def _():
                    acc_ref[pl.ds(i, 1), :] = acc_ref[pl.ds(i, 1), :] + wide_ref[0, pl.ds(k, 1), :]

                return carry

            lax.fori_loop(jnp.where(repeats > 1, 0, furthest), furthest + 1, one, 0)

        return carry

    for group in range(sources // GROUP):

        @pl.when(list_ref[group * GROUP, slots + 2] > 0)
        def _():
            lax.fori_loop(group * GROUP, (group + 1) * GROUP, rest_of, 0)


    def total(start, size, stride=1):
        here = pl.ds(start, size) if stride == 1 else pl.ds(start, size, stride=stride)
        return acc_ref[here, :] + other_ref[here, :]

    bf16 = jnp.bfloat16
    ends = (0, 1, 126, 127)
    for n, at in enumerate((EVEN + 63, ODD + 63)):
        right_ref[pl.ds(n * 128, 128), :] = total(2 * PITCH + at, 128, PITCH).astype(bf16)
    left_ref[pl.ds(0, 128), :] = total(2 * PITCH + EVEN, 128, PITCH).astype(bf16)
    near_ref[...] = total(2 * PITCH + ODD, 128, PITCH).astype(bf16)
    east = [total((r + 2) * PITCH + at, 1) for r in ends for at in (EVEN + 63, ODD + 63)]
    west = [total((r + 2) * PITCH + EVEN, 1) for r in ends]
    right_ref[pl.ds(256, 8), :] = jnp.concatenate(east, axis=0).astype(bf16)
    left_ref[pl.ds(128, 8), :] = jnp.concatenate(west + west, axis=0).astype(bf16)
    for n, r in enumerate(ends):
        base = (r + 2) * PITCH
        rows_ref[n, pl.ds(0, 64), :] = total(base + ODD, 64).astype(bf16)
        rows_ref[n, pl.ds(64, 64), :] = total(base + EVEN, 64).astype(bf16)


def scatter(place, got, start):
    return pl.pallas_call(
        scatter_kernel,
        out_shape=[
            pltpu.VMEM((SLABS * PITCH, 128), jnp.float32),
            pltpu.VMEM((SLABS * PITCH, 128), jnp.float32),
            jax.ShapeDtypeStruct((264, 128), jnp.bfloat16),
            jax.ShapeDtypeStruct((136, 128), jnp.bfloat16),
            jax.ShapeDtypeStruct((128, 128), jnp.bfloat16),
            jax.ShapeDtypeStruct((4, 128, 128), jnp.bfloat16),
        ],
        in_specs=[SMEM, VMEM, ANY],
        out_specs=[VMEM] * 6,
        scratch_shapes=[
            pltpu.VMEM((128, 128, 128), jnp.bfloat16),
            pltpu.VMEM((2, 96, 128), jnp.float32),
            pltpu.VMEM((128 * META, 128), jnp.float32),
            pltpu.VMEM((128, 128), jnp.int32),
            pltpu.VMEM((128, 128), jnp.int32),
            pltpu.SMEM((GROUP, 128), jnp.int32),
            pltpu.SMEM((GROUP, 128), jnp.int32),
            pltpu.SMEM((128, 128), jnp.int32),
            pltpu.SemaphoreType.DMA((3 + CHUNKS,)),
        ],
        compiler_params=pltpu.CompilerParams(vmem_limit_bytes=16 << 20),
        name="scatter",
    )(place, on_chip(got), off_chip(start))


def frame_kernel(place_ref, after_ref, rows_ref, west_ref, east_ref, round_ref, back_ref, own_ref):
    del after_ref
    f32, bf16 = jnp.float32, jnp.bfloat16
    west = west_ref[pl.ds(256, 8), :].astype(f32)
    east = east_ref[pl.ds(128, 8), :].astype(f32)
    for n in range(4):
        tail = jnp.concatenate([west[2 * n : 2 * n + 2], east[n : n + 1], jnp.zeros((5, 128), f32)], axis=0)
        own_ref[n, pl.ds(0, 128), :] = rows_ref[n]
        own_ref[n, pl.ds(128, 8), :] = tail.astype(bf16)
    descends = place_ref[1] < place_ref[2]
    for n in range(2):
        top, bottom = own_ref[n].astype(f32), own_ref[n + 2].astype(f32)
        round_ref[n] = jnp.where(descends, bottom, top).astype(bf16)
        back_ref[n] = jnp.where(descends, top, bottom).astype(bf16)


def frame(place, after, rows, west, east):
    return pl.pallas_call(
        frame_kernel,
        out_shape=[
            jax.ShapeDtypeStruct((2, 136, 128), jnp.bfloat16),
            jax.ShapeDtypeStruct((2, 136, 128), jnp.bfloat16),
            jax.ShapeDtypeStruct((4, 136, 128), jnp.bfloat16),
        ],
        in_specs=[SMEM, ANY] + [VMEM] * 3,
        out_specs=[VMEM] * 3,
        compiler_params=pltpu.CompilerParams(vmem_limit_bytes=4 << 20),
        name="frame",
    )(place, after, rows, west, east)


def inner_kernel(low, field_ref, other_ref, w1_ref, b1_ref, even_ref, odd_ref, edge_ref, lhs_ref, shift_ref, tail_ref):
    f32, bf16 = jnp.float32, jnp.bfloat16
    bias = jnp.concatenate([b1_ref[...], b1_ref[...]], axis=-1)
    weight = w1_ref[...].reshape(1536, 256)

    def fill(b):
        for n in range(ROWS + 2):
            base = (low + 1 + b * ROWS + n) * PITCH
            spans = [pl.ds(base + at, 64) for at in (ODD - 1, EVEN, ODD, EVEN + 1)]
            parts = [(field_ref[span, :] + other_ref[span, :]).astype(bf16) for span in spans]
            lhs_ref[b % 2, n] = jnp.concatenate(parts, axis=-1)

    steps = 64 // ROWS
    fill(0)
    for b in range(steps):
        held = lhs_ref.at[b % 2]
        window = jnp.concatenate([held[pl.ds(di, ROWS)].reshape(ROWS * 64, 512) for di in range(3)], axis=-1)
        pre = jnp.dot(window, weight, preferred_element_type=f32)
        if b + 1 < steps:
            fill(b + 1)
        hid = gelu(pre + bias).reshape(ROWS, 64, 256)
        shift_ref[:, pl.ds(8, 64), :] = hid[:, :, 128:]
        tail_ref[...] = hid[:, 56:, :128]
        for n in range(ROWS):
            line = pl.ds(b * ROWS + n, 1)
            edge_ref[0, line, :] = shift_ref[n, pl.ds(8, 1), :]
            edge_ref[1, line, :] = shift_ref[n, pl.ds(70, 1), :]
            edge_ref[2, line, :] = tail_ref[n, pl.ds(7, 1), :]
        wide = jnp.concatenate([shift_ref[:, pl.ds(7, 64), :], hid[:, :, :128], hid[:, :, 128:]], axis=-1)
        wide = wide.astype(bf16).reshape(ROWS // 2, 2, 64, 384)
        even_ref[pl.ds(b * (ROWS // 2), ROWS // 2)] = wide[:, 0]
        odd_ref[pl.ds(b * (ROWS // 2) + 1, ROWS // 2)] = wide[:, 1]


def inner(low, field, other, w1, b1):
    return pl.pallas_call(
        functools.partial(inner_kernel, low),
        out_shape=[
            pltpu.VMEM((32, 64, 384), jnp.bfloat16),
            pltpu.VMEM((33, 64, 384), jnp.bfloat16),
            jax.ShapeDtypeStruct((3, 64, 128), jnp.float32),
        ],
        in_specs=[VMEM] * 4,
        out_specs=[VMEM] * 3,
        scratch_shapes=[pltpu.VMEM((2, ROWS + 2, 64, 512), jnp.bfloat16), pltpu.VMEM((ROWS, 72, 128), jnp.float32), pltpu.VMEM((ROWS, 8, 128), jnp.float32)],
        compiler_params=pltpu.CompilerParams(vmem_limit_bytes=24 << 20),
        name="inner",
    )(on_chip(field), on_chip(other), w1, b1)


def rim_kernel(
    place_ref,
    even0_in,
    odd0_in,
    even1_in,
    odd1_in,
    edge0_ref,
    edge1_ref,
    right_ref,
    left_ref,
    near_ref,
    west_ref,
    east_ref,
    own_ref,
    round_ref,
    back_ref,
    w1_ref,
    w1s_ref,
    b1_ref,
    w2_ref,
    b2_ref,
    even0_ref,
    odd0_ref,
    even1_ref,
    odd1_ref,
    out_ref,
    cols_ref,
    strip_ref,
    shift_ref,
    side_ref,
    ends_ref,
    total_ref,
):
    del even0_in, odd0_in, even1_in, odd1_in
    f32, bf16 = jnp.float32, jnp.bfloat16
    north, south = place_ref[0] == 0, place_ref[0] == 3
    descends = place_ref[1] < place_ref[2]
    dot = functools.partial(jnp.dot, preferred_element_type=f32)
    bias = b1_ref[...]
    bias2 = jnp.concatenate([bias, bias], axis=-1)
    pairs = w1_ref[...].reshape(1536, 256)
    taps1 = w1s_ref[...].reshape(1152, 128)
    taps2 = w2_ref[...].reshape(1152, 128)

    def second_layer(b):
        even_ref, odd_ref = ((even0_ref, odd0_ref), (even1_ref, odd1_ref))[b // 4]
        p = b % 4 * 8
        window = [
            odd_ref[pl.ds(p, 8)].reshape(512, 384),
            even_ref[pl.ds(p, 8)].reshape(512, 384),
            odd_ref[pl.ds(p + 1, 8)].reshape(512, 384),
        ]
        total = dot(jnp.concatenate(window, axis=-1), taps2) + b2_ref[...]
        total_ref[pl.ds(b * 8, 8)] = total.reshape(8, 64, 128)

    odd1_ref[0] = odd0_ref[32]
    second_layer(1)

    body = (
        west_ref[pl.ds(0, 128), :],
        west_ref[pl.ds(128, 128), :],
        left_ref[pl.ds(0, 128), :],
        near_ref[...],
        right_ref[pl.ds(0, 128), :],
        right_ref[pl.ds(128, 128), :],
        east_ref[pl.ds(0, 128), :],
    )
    for n, col in enumerate(body):
        cols_ref[n, pl.ds(2, 128), :] = col.astype(f32)

    def wide(ref, n):
        return ref[n].astype(f32)

    above = [jnp.where(descends, wide(round_ref, n), wide(back_ref, n)) for n in range(2)]
    beneath = [jnp.where(descends, wide(back_ref, n), wide(round_ref, n)) for n in range(2)]
    second = jnp.where(north, above[1], above[0])
    first = jnp.where(north, above[0], above[1])
    own = [wide(own_ref, n) for n in range(4)]
    below = jnp.where(south, beneath[1], beneath[0])
    top = (jnp.where(north, own[0], second), first, jnp.where(north, second, own[0]))
    for slab, row in ((0, second), (1, first), (130, below)):
        for m, at in enumerate((128, 129, 64, 0, 127, 63, 130)):
            cols_ref[m, pl.ds(slab, 1), :] = row[at : at + 1]

    def lines(n, row):
        strip_ref[n, pl.ds(ODD, 64), :] = row[0:64]
        strip_ref[n, pl.ds(EVEN, 64), :] = row[64:128]
        strip_ref[n, pl.ds(ODD - 1, 1), :] = row[129:130]
        strip_ref[n, pl.ds(EVEN + 64, 1), :] = row[130:131]
        parts = [strip_ref[n, pl.ds(at, 64), :].astype(bf16) for at in (ODD - 1, EVEN, ODD, EVEN + 1)]
        return jnp.concatenate(parts, axis=-1)

    lhs = [lines(n, row) for n, row in enumerate((top[0], first, top[2], *own, below))]
    corner = []
    for row in top:
        corner.append(jnp.zeros((8, 128), f32))
        corner.extend(jnp.broadcast_to(row[at : at + 1], (8, 128)) for at in (128, 129, 64))
    corner = jnp.concatenate(corner, axis=-1).astype(bf16)
    stack = [jnp.concatenate([lhs[n] for n in picks], axis=-1) for picks in ((0, 1, 2), (1, 3, 4), (5, 6, 7))]
    second_layer(2)
    hid = gelu(dot(jnp.concatenate([*stack, corner, corner], axis=0), pairs) + bias2)

    windows = []
    for at in (0, 1, 4):
        parts = [cols_ref[at + m, pl.ds(di, 136), :] for di in range(3) for m in range(3)]
        windows.append(jnp.concatenate(parts, axis=-1))
    cols = gelu(dot(jnp.concatenate(windows, axis=0).astype(bf16), taps1) + bias)
    second_layer(3)
    for n, to in enumerate((0, 1, 5)):
        side_ref[to] = cols[n * 136 : (n + 1) * 136]
    for n in range(3):
        side_ref[n + 2, pl.ds(1, 64), :] = edge0_ref[n]
        side_ref[n + 2, pl.ds(65, 64), :] = edge1_ref[n]
    for n, r in enumerate((-1, 0, 127)):
        here = pl.ds(r + 1, 1)
        even, odd = hid[n * 64 : n * 64 + 64, :128], hid[n * 64 : n * 64 + 64, 128:]
        side_ref[1, here, :] = even[0:1]
        side_ref[2, here, :] = odd[0:1]
        side_ref[3, here, :] = odd[62:63]
        side_ref[4, here, :] = even[63:64]
        side_ref[5, here, :] = odd[63:64]
        shift_ref[pl.ds(8, 64), :] = odd
        line = jnp.concatenate([shift_ref[pl.ds(7, 64), :], even, odd], axis=-1).astype(bf16)
        if r == -1:
            odd0_ref[0] = line
        elif r == 0:
            even0_ref[0] = line
        else:
            odd1_ref[32] = line
    side_ref[0, pl.ds(0, 1), :] = hid[192:193, 128:]
    second_layer(4)

    windows = []
    for at in (0, 3):
        parts = [side_ref[at + m, pl.ds(a, 64, stride=2), :] for a in range(3) for m in range(3)]
        windows.append(jnp.concatenate(parts, axis=-1))
    ends_ref[...] = dot(jnp.concatenate(windows, axis=0).astype(bf16), taps2) + b2_ref[...]

    for b in (5, 6, 0, 7):
        second_layer(b)

    def finish(p, carry):
        total_ref[p, pl.ds(0, 1), :] = ends_ref[pl.ds(p, 1), :]
        total_ref[p, pl.ds(63, 1), :] = ends_ref[pl.ds(64 + p, 1), :]
        out_ref[p] = total_ref[p].astype(bf16)
        return carry

    lax.fori_loop(0, 64, finish, 0, unroll=8)


def rim(place, blocks, *rest):
    return pl.pallas_call(
        rim_kernel,
        out_shape=[pltpu.VMEM(b.shape, b.dtype) for b in blocks] + [jax.ShapeDtypeStruct((64, 64, 128), jnp.bfloat16)],
        in_specs=[SMEM] + [VMEM] * 19,
        out_specs=[VMEM] * 5,
        scratch_shapes=[
            pltpu.VMEM((7, 144, 128), jnp.float32),
            pltpu.VMEM((8, PITCH, 128), jnp.float32),
            pltpu.VMEM((72, 128), jnp.float32),
            pltpu.VMEM((6, 136, 128), jnp.float32),
            pltpu.VMEM((128, 128), jnp.float32),
            pltpu.VMEM((64, 64, 128), jnp.float32),
        ],
        input_output_aliases={1: 0, 2: 1, 3: 2, 4: 3},
        compiler_params=pltpu.CompilerParams(vmem_limit_bytes=20 << 20),
        name="rim",
    )(place, *map(on_chip, blocks), *rest)[4]


def shards(background, values, cells, counts, w1, b1, w2, b2):
    lat, lon = lax.axis_size("lat"), lax.axis_size("lon")
    half = lon // 2
    place = jnp.stack([lax.axis_index("lat"), lax.axis_index("lon"), jnp.int32(half)])
    east_pairs = [(i, (i + 1) % lon) for i in range(lon)]
    west_pairs = [(j, i) for i, j in east_pairs]
    round_pairs = []
    for i in range(half):
        circle = [b * lon + i for b in range(lat)] + [b * lon + i + half for b in reversed(range(lat))]
        round_pairs += zip(circle, circle[1:] + circle[:1])
    back_pairs = [(j, i) for i, j in round_pairs]

    sent = pack(values[0], cells[0].T, counts)
    got = lax.all_to_all(sent, ("lat", "lon"), split_axis=0, concat_axis=0, tiled=True)
    field, other, right, left, near, rows = scatter(place, got, spread(background))

    flat = w1.reshape(3, 384, 128)
    blank = jnp.zeros((3, 128, 128), jnp.bfloat16)
    paired = jnp.concatenate(
        [jnp.concatenate([flat, blank], axis=1), jnp.concatenate([blank, flat], axis=1)], axis=2
    )
    west = lax.ppermute(right, "lon", east_pairs)
    east = lax.ppermute(left, "lon", west_pairs)
    *upper, upper_edge = inner(0, field, other, paired, b1[None])
    ahead, behind, own = frame(place, upper_edge, rows, west, east)
    ahead = lax.ppermute(ahead, ("lat", "lon"), round_pairs)
    behind = lax.ppermute(behind, ("lat", "lon"), back_pairs)
    *lower, lower_edge = inner(64, field, other, paired, b1[None])
    return rim(
        place,
        (*upper, *lower),
        upper_edge,
        lower_edge,
        right,
        left,
        near,
        west,
        east,
        own,
        ahead,
        behind,
        paired,
        flat,
        b1[None],
        w2.reshape(3, 384, 128),
        b2[None],
    )


def solution(mesh):
    placed = (
        P("lat", "lon", None),
        P(("lat", "lon"), None, None, None),
        P(("lat", "lon"), None, None),
        P(("lat", "lon"), None),
        P(),
        P(),
        P(),
        P(),
    )
    return jax.shard_map(
        shards, mesh=mesh, in_specs=placed, out_specs=P("lat", "lon", None), check_vma=False
    )
```
